32 devices in a mesh: tile: 8 (over y, x, core), depth: 4 (over z).
Axes of the slice: x: 2, y: 2, z: 4, core: 2. Of those that a mesh axis runs over, the one named last changes fastest.
Arguments:
- initial_state: float32 [2, 32, 8192], P(None, 'depth', 'tile'), may hold values from -6 to 6
- observed: float32 [2, 32, 8192], P(None, 'depth', 'tile'), may hold values from -6 to 6
- edge_weight: float32 [8192], P('tile'), may hold values from 0.25 to 1
- land: int32 [8192], P('tile'), may hold values 0 or 1
- w_in: bfloat16 [64, 640], replicated, may hold values from -0.75 to 0.75
- b_in: float32 [640], replicated, may hold values from -3 to 3
- w_mid: bfloat16 [640, 640], replicated, may hold values from -0.25 to 0.25
- b_mid: float32 [640], replicated, may hold values from -3 to 3
- w_out: bfloat16 [640, 64], replicated, may hold values from -0.25 to 0.25
- b_out: float32 [64], replicated, may hold values from -3 to 3
Outputs:
- final_state: float32 [2, 32, 8192], P(None, 'depth', 'tile')
- sensitivity: float32 [2, 32, 8192], P(None, 'depth', 'tile')
- grad_w_in: float32 [64, 640], replicated
- grad_b_in: float32 [640], replicated
- grad_w_mid: float32 [640, 640], replicated
- grad_b_mid: float32 [640], replicated
- grad_w_out: float32 [640, 64], replicated
- grad_b_out: float32 [64], replicated
The draws below stay inside these ranges and needn't reach their ends.
All inputs are finite; a program needn't handle non-finite values. No bound on the sum of `land` on one device may be relied on, other than what follows from the above.
Results may differ from the reference program's by a relative error of at most 0.0017.
Values may be sent and summed in bfloat16 or wider, within the bound.
No kernel may reach another device: no remote copies, remote signals or barrier semaphores. Data moves between devices by JAX's collectives and lax.ppermute only.
A program may use at most 64 MiB of HBM per device.

```python
import math
import jax
import jax.numpy as jnp
from jax import lax

TILE_SIDE = 32
LEVELS = 32
MLP_WIDTH = 640
TIME_STEPS = 2
FEATURES = 64
TILE_CELLS = 1024
TILES = 8
COLUMNS = 8192


def plant(values, own_key, low, high):
    longest = values.shape.index(max(values.shape))
    spots = []
    for shift in (0, 1):
        where = [jax.random.randint(jax.random.fold_in(own_key, axis), (), 0, length) for axis, length in enumerate(values.shape)]
        where[longest] = (where[longest] + shift) % values.shape[longest]
        spots.append(tuple(where))
    return values.at[spots[0]].set(low).at[spots[1]].set(high)


def shard_levels(stream_key, extent, pieces, smallest, high):
    def one(dim, parts):
        draws = jax.random.uniform(jax.random.fold_in(jax.random.fold_in(stream_key, 6), dim), (parts,), jnp.float32, smallest / len(pieces), high / len(pieces))
        return jnp.repeat(jnp.exp(draws), extent[dim] // parts).reshape((-1,) + (1,) * (len(extent) - dim - 1))

    level = one(*pieces[0])
    for cut in pieces[1:]:
        level = level * one(*cut)
    return level


def gaussian(stream_key, extent, deviation, reach, shards=(), kind=jnp.bfloat16):
    entries = deviation * jax.random.normal(stream_key, extent, jnp.float32)
    if shards:
        entries = entries * shard_levels(stream_key, extent, shards, -0.22, 0.18)
    return jnp.clip(entries, -reach, reach).astype(kind)


def setup_inputs(seed: int = 0) -> dict:
    streams_of = jax.random.split(jax.random.key(seed), 11)
    initial_state = gaussian(streams_of[0], (2, LEVELS, COLUMNS), 1.0, 6.0, ((1, 4), (2, 8)), jnp.float32)
    observed = gaussian(streams_of[1], (2, LEVELS, COLUMNS), 1.0, 6.0, ((1, 4), (2, 8)), jnp.float32)
    edge_weight = jnp.clip(jnp.exp(math.log(1.0) - 1.3862944 * jax.random.uniform(streams_of[2], (COLUMNS,), jnp.float32) ** shard_levels(streams_of[2], (COLUMNS,), ((0, 8),), -0.2, 0.2)), 0.25, 1.0)
    land = plant((jax.random.randint(streams_of[3], (COLUMNS,), 0, 5) < 4).astype(jnp.int32), jax.random.fold_in(streams_of[3], 1), 0, 1)
    w_in = gaussian(streams_of[4], (FEATURES, MLP_WIDTH), FEATURES ** -0.5, 0.75)
    b_in = gaussian(streams_of[5], (MLP_WIDTH,), 0.5, 3.0, (), jnp.float32)
    w_mid = gaussian(streams_of[6], (MLP_WIDTH, MLP_WIDTH), MLP_WIDTH ** -0.5, 0.25)
    b_mid = gaussian(streams_of[7], (MLP_WIDTH,), 0.5, 3.0, (), jnp.float32)
    w_out = gaussian(streams_of[8], (MLP_WIDTH, FEATURES), MLP_WIDTH ** -0.5, 0.25)
    b_out = gaussian(streams_of[9], (FEATURES,), 0.5, 3.0, (), jnp.float32)
    return {"initial_state": initial_state, "observed": observed, "edge_weight": edge_weight, "land": land, "w_in": w_in, "b_in": b_in, "w_mid": w_mid, "b_mid": b_mid, "w_out": w_out, "b_out": b_out}


diffuse_coef = 0.2
step_size = 0.5


def neighbour_sum(flat_rows):
    row_count = flat_rows.shape[0]
    tile_grid = flat_rows.reshape(row_count, TILES, TILE_SIDE, TILE_SIDE)
    west_side = tile_grid[:, :, :, 0]
    east_side = tile_grid[:, :, :, -1]
    south_side = tile_grid[:, :, 0, :]
    north_side = tile_grid[:, :, -1, :]
    half_tiles = TILES // 2
    from_west = jnp.roll(east_side, 1, axis=1)
    from_east = jnp.roll(west_side, -1, axis=1)
    from_south = jnp.roll(south_side, half_tiles, axis=1)[..., ::-1]
    from_north = jnp.roll(north_side, half_tiles, axis=1)[..., ::-1]
    west_cells = jnp.concatenate([from_west[:, :, :, None], tile_grid[:, :, :, :-1]], axis=3)
    east_cells = jnp.concatenate([tile_grid[:, :, :, 1:], from_east[:, :, :, None]], axis=3)
    south_cells = jnp.concatenate([from_south[:, :, None, :], tile_grid[:, :, :-1, :]], axis=2)
    north_cells = jnp.concatenate([tile_grid[:, :, 1:, :], from_north[:, :, None, :]], axis=2)
    return (west_cells + east_cells + south_cells + north_cells).reshape(row_count, TILES * TILE_CELLS)


def silu_slope(pre_act):
    sigmoid_val = jax.nn.sigmoid(pre_act)
    return sigmoid_val * (1.0 + pre_act * (1.0 - sigmoid_val))


def closure_forward(inputs, params):
    w_in, b_in, w_mid, b_mid, w_out, b_out = params
    contract_rows = (((0,), (0,)), ((), ()))
    pre_one = lax.dot_general(w_in, inputs, contract_rows, preferred_element_type=jnp.float32) + b_in[:, None]
    hidden_one = jax.nn.silu(pre_one).astype(jnp.bfloat16)
    pre_two = lax.dot_general(w_mid, hidden_one, contract_rows, preferred_element_type=jnp.float32) + b_mid[:, None]
    hidden_two = jax.nn.silu(pre_two).astype(jnp.bfloat16)
    output = lax.dot_general(w_out, hidden_two, contract_rows, preferred_element_type=jnp.float32) + b_out[:, None]
    return output, (inputs, pre_one, hidden_one, pre_two, hidden_two)


def closure_backward(upstream, saved_cache, params):
    w_in, b_in, w_mid, b_mid, w_out, b_out = params
    inputs, pre_one, hidden_one, pre_two, hidden_two = saved_cache
    contract_cols = (((1,), (1,)), ((), ()))
    grad_w_out = lax.dot_general(hidden_two, upstream, contract_cols, preferred_element_type=jnp.float32)
    grad_b_out = jnp.sum(upstream.astype(jnp.float32), axis=1)
    slope_two = (jnp.dot(w_out, upstream, preferred_element_type=jnp.float32) * silu_slope(pre_two)).astype(jnp.bfloat16)
    grad_w_mid = lax.dot_general(hidden_one, slope_two, contract_cols, preferred_element_type=jnp.float32)
    grad_b_mid = jnp.sum(slope_two.astype(jnp.float32), axis=1)
    slope_one = (jnp.dot(w_mid, slope_two, preferred_element_type=jnp.float32) * silu_slope(pre_one)).astype(jnp.bfloat16)
    grad_w_in = lax.dot_general(inputs, slope_one, contract_cols, preferred_element_type=jnp.float32)
    grad_b_in = jnp.sum(slope_one.astype(jnp.float32), axis=1)
    back_grad = jnp.dot(w_in, slope_one, preferred_element_type=jnp.float32)
    return back_grad, (grad_w_in, grad_b_in, grad_w_mid, grad_b_mid, grad_w_out, grad_b_out)


def reference(initial_state, observed, edge_weight, land, w_in, b_in, w_mid, b_mid, w_out, b_out):
    params = (w_in, b_in, w_mid, b_mid, w_out, b_out)
    ocean_mask = land.astype(jnp.float32)
    weight = edge_weight * ocean_mask
    weight_sums = neighbour_sum(weight[None, :])[0]

    def diffuse(tracer_field):
        flat_rows = tracer_field.reshape(FEATURES, COLUMNS)
        scaled = flat_rows * weight[None, :]
        result_rows = weight[None, :] * (neighbour_sum(scaled) - flat_rows * weight_sums[None, :])
        return result_rows.reshape(tracer_field.shape)

    def blocks(matrix):
        return matrix.reshape(matrix.shape[0], TILES, TILE_CELLS).transpose(1, 0, 2)

    def unblock(stacked):
        return stacked.transpose(1, 0, 2).reshape(stacked.shape[1], COLUMNS)

    def forward_block(column_block):
        return closure_forward(column_block, params)[0]

    def accumulate(totals, block_pair):
        block_in, block_up = block_pair
        saved_cache = closure_forward(block_in, params)[1]
        back_grad, param_grads = closure_backward(block_up, saved_cache, params)
        return tuple(total + gradient for total, gradient in zip(totals, param_grads)), back_grad

    state_now = initial_state
    inputs_all = []
    for step_index in range(TIME_STEPS):
        inputs = state_now.astype(jnp.bfloat16).reshape(FEATURES, COLUMNS)
        inputs_all.append(inputs)
        tendency = unblock(lax.map(forward_block, blocks(inputs))).reshape(2, LEVELS, COLUMNS)
        state_now = state_now + diffuse_coef * diffuse(state_now) + step_size * ocean_mask[None, None, :] * tendency
    adjoint = ocean_mask[None, None, :] * (state_now - observed)
    totals = tuple(jnp.zeros(item_param.shape, jnp.float32) for item_param in params)
    for step_index in reversed(range(TIME_STEPS)):
        upstream = (step_size * ocean_mask[None, None, :] * adjoint).astype(jnp.bfloat16).reshape(FEATURES, COLUMNS)
        totals, backs = lax.scan(accumulate, totals, (blocks(inputs_all[step_index]), blocks(upstream)))
        adjoint = adjoint + diffuse_coef * diffuse(adjoint) + unblock(backs).reshape(2, LEVELS, COLUMNS)
    grad_scale = 1.0 / COLUMNS
    return (state_now, adjoint, totals[0] * grad_scale, totals[1] * grad_scale, totals[2] * grad_scale, totals[3] * grad_scale, totals[4] * grad_scale, totals[5] * grad_scale)
```

```python
import jax
import jax.numpy as jnp
from jax import lax
from jax.sharding import PartitionSpec as P

TILE_SIDE = 32
LEVELS = 32
TIME_STEPS = 2
FEATURES = 64
TILE_CELLS = 1024


diffuse_coef = 0.2
step_size = 0.5


def with_halo(cells, sides, width):
    for axis, dim in sides:
        count = lax.axis_size(axis)
        head = lax.slice_in_dim(cells, 0, width, axis=dim)
        tail = lax.slice_in_dim(cells, cells.shape[dim] - width, cells.shape[dim], axis=dim)
        cells = jnp.concatenate(
            [
                lax.ppermute(tail, axis, [(i, (i + 1) % count) for i in range(count)]),
                cells,
                lax.ppermute(head, axis, [((i + 1) % count, i) for i in range(count)]),
            ],
            axis=dim,
        )
    return cells


def passed_along(x, axis, by):
    length = lax.axis_size(axis)
    return lax.ppermute(x, axis, [(i, (i + by) % length) for i in range(length)])


def neighbour_sum(flat_rows):
    row_count = flat_rows.shape[0]
    tile_grid = flat_rows.reshape(row_count, TILE_SIDE, TILE_SIDE)
    zonal_pair = jnp.stack([tile_grid[:, :, -1], tile_grid[:, :, 0]], axis=1)
    padded = with_halo(zonal_pair[None], (("tile", 0),), 1)
    from_west = padded[0, :, 0, :]
    from_east = padded[2, :, 1, :]
    fold_pair = jnp.stack([tile_grid[:, 0, :], tile_grid[:, -1, :]], axis=1)
    across = passed_along(fold_pair, "tile", lax.axis_size("tile") // 2)[:, :, ::-1]
    west_cells = jnp.concatenate([from_west[:, :, None], tile_grid[:, :, :-1]], axis=2)
    east_cells = jnp.concatenate([tile_grid[:, :, 1:], from_east[:, :, None]], axis=2)
    south_cells = jnp.concatenate([across[:, 0, None, :], tile_grid[:, :-1, :]], axis=1)
    north_cells = jnp.concatenate([tile_grid[:, 1:, :], across[:, 1, None, :]], axis=1)
    return (west_cells + east_cells + south_cells + north_cells).reshape(row_count, TILE_CELLS)


def diffuse(tracer_field, weight, weight_sums):
    flat_rows = tracer_field.reshape(-1, TILE_CELLS)
    scaled = flat_rows * weight[None, :]
    result_rows = weight[None, :] * (neighbour_sum(scaled) - flat_rows * weight_sums[None, :])
    return result_rows.reshape(tracer_field.shape)


def silu_slope(pre_act):
    sigmoid_val = jax.nn.sigmoid(pre_act)
    return sigmoid_val * (1.0 + pre_act * (1.0 - sigmoid_val))


def closure_forward(inputs, params):
    w_in, b_in, w_mid, b_mid, w_out, b_out = params
    contract_rows = (((0,), (0,)), ((), ()))
    pre_one = (
        lax.dot_general(w_in, inputs, contract_rows, preferred_element_type=jnp.float32)
        + b_in[:, None]
    )
    hidden_one = jax.nn.silu(pre_one).astype(jnp.bfloat16)
    pre_two = (
        lax.dot_general(w_mid, hidden_one, contract_rows, preferred_element_type=jnp.float32)
        + b_mid[:, None]
    )
    hidden_two = jax.nn.silu(pre_two).astype(jnp.bfloat16)
    output = (
        lax.dot_general(w_out, hidden_two, contract_rows, preferred_element_type=jnp.float32)
        + b_out[:, None]
    )
    return (output, (inputs, pre_one, hidden_one, pre_two, hidden_two))


def closure_backward(upstream, saved_cache, params):
    w_in, b_in, w_mid, b_mid, w_out, b_out = params
    inputs, pre_one, hidden_one, pre_two, hidden_two = saved_cache
    contract_cols = (((1,), (1,)), ((), ()))
    grad_w_out = lax.dot_general(
        hidden_two, upstream, contract_cols, preferred_element_type=jnp.float32
    )
    grad_b_out = jnp.sum(upstream.astype(jnp.float32), axis=1)
    slope_two = (
        jnp.dot(w_out, upstream, preferred_element_type=jnp.float32) * silu_slope(pre_two)
    ).astype(jnp.bfloat16)
    grad_w_mid = lax.dot_general(
        hidden_one, slope_two, contract_cols, preferred_element_type=jnp.float32
    )
    grad_b_mid = jnp.sum(slope_two.astype(jnp.float32), axis=1)
    slope_one = (
        jnp.dot(w_mid, slope_two, preferred_element_type=jnp.float32) * silu_slope(pre_one)
    ).astype(jnp.bfloat16)
    grad_w_in = lax.dot_general(
        inputs, slope_one, contract_cols, preferred_element_type=jnp.float32
    )
    grad_b_in = jnp.sum(slope_one.astype(jnp.float32), axis=1)
    back_grad = jnp.dot(w_in, slope_one, preferred_element_type=jnp.float32)
    return (back_grad, (grad_w_in, grad_b_in, grad_w_mid, grad_b_mid, grad_w_out, grad_b_out))


def is_power_of_two(count):
    return count & (count - 1) == 0


def swapped(x, axis, even_bit, odd_bit):
    length = lax.axis_size(axis)
    return lax.ppermute(x, axis, [(i, i ^ (odd_bit if i & 1 else even_bit)) for i in range(length)])


def tile_rounds(length):
    bits = [1 << k for k in range(length.bit_length() - 1)]
    rounds = [(bits[0], bits[0])] if bits else []
    rest = bits[1:]
    for k in range(len(rest)):
        rounds.append((rest[k], rest[(k + 1) % len(rest)]))
    return rounds


def all_summed(block):
    tiles = lax.axis_size("tile")
    depths = lax.axis_size("depth")
    if not (is_power_of_two(tiles) and is_power_of_two(depths)):
        return lax.psum(block, ("tile", "depth"))
    width = block.shape[-1]
    tile = lax.axis_index("tile")
    rounds = tile_rounds(tiles)
    sides = []
    for even_bit, odd_bit in rounds:
        bit = jnp.where(tile & 1 == 1, odd_bit, even_bit)
        sides.append(((tile & bit) != 0).astype(jnp.int32))
    for (even_bit, odd_bit), side in zip(rounds, sides):
        halves = block.reshape(2, -1, width)
        sent = lax.dynamic_index_in_dim(halves, 1 - side, 0, False)
        kept = lax.dynamic_index_in_dim(halves, side, 0, False)
        block = kept + swapped(sent, "tile", even_bit, odd_bit)
    bit = 1
    while bit < depths:
        block = block + swapped(block, "depth", bit, bit)
        bit *= 2
    for (even_bit, odd_bit), side in zip(reversed(rounds), reversed(sides)):
        other = swapped(block, "tile", even_bit, odd_bit)
        block = jnp.where(side == 0, jnp.stack([block, other]), jnp.stack([other, block])).reshape(-1, width)
    return block


def reduced_gradients(totals):
    grad_w_in, grad_b_in, grad_w_mid, grad_b_mid, grad_w_out, grad_b_out = totals
    width = grad_w_mid.shape[1]
    features = grad_w_in.shape[0]
    bias_rows = jnp.zeros((8, width), jnp.float32)
    bias_rows = bias_rows.at[0].set(grad_b_in).at[1].set(grad_b_mid).at[2, :features].set(grad_b_out)
    parts = [grad_w_mid, grad_w_in, grad_w_out.T, bias_rows]
    rows = sum(part.shape[0] for part in parts)
    step = 8 * lax.axis_size("tile")
    pad = -rows % step
    block = jnp.concatenate(parts + [jnp.zeros((pad, width), jnp.float32)], axis=0)
    block = all_summed(block)
    top = width
    out_in = block[top : top + features]
    out_out = block[top + features : top + 2 * features].T
    biases = block[top + 2 * features : top + 2 * features + 8]
    return (out_in, biases[0], block[:width], biases[1], out_out, biases[2, :features])


def body(initial_state, observed, edge_weight, land, w_in, b_in, w_mid, b_mid, w_out, b_out):
    params = (w_in, b_in, w_mid, b_mid, w_out, b_out)
    ocean_mask = land.astype(jnp.float32)
    weight = edge_weight * ocean_mask
    weight_sums = neighbour_sum(weight[None, :])[0]

    def to_columns(segment):
        full_cols = lax.all_to_all(segment, "depth", split_axis=2, concat_axis=1, tiled=True)
        return full_cols.reshape(FEATURES, full_cols.shape[2])

    def to_segments(values):
        shaped = values.reshape(2, LEVELS, values.shape[1])
        segment_part = lax.all_to_all(shaped, "depth", split_axis=1, concat_axis=2, tiled=True)
        return segment_part

    state_now = initial_state
    caches = []
    for step_index in range(TIME_STEPS):
        inputs = to_columns(state_now.astype(jnp.bfloat16))
        tendency, saved_cache = closure_forward(inputs, params)
        caches.append(saved_cache)
        change = diffuse(state_now, weight, weight_sums)
        state_now = (
            state_now
            + diffuse_coef * change
            + step_size * ocean_mask[None, None, :] * to_segments(tendency)
        )
    adjoint = ocean_mask[None, None, :] * (state_now - observed)
    grad_list = []
    for step_index in reversed(range(TIME_STEPS)):
        upstream = to_columns(
            (step_size * ocean_mask[None, None, :] * adjoint).astype(jnp.bfloat16)
        )
        back_grad, param_grads = closure_backward(upstream, caches[step_index], params)
        grad_list.append(param_grads)
        spread = diffuse(adjoint, weight, weight_sums)
        adjoint = adjoint + diffuse_coef * spread + to_segments(back_grad)
    totals = grad_list[0]
    for param_grads in grad_list[1:]:
        totals = tuple((total + gradient for total, gradient in zip(totals, param_grads)))
    summed = reduced_gradients(totals)
    grad_scale = 1.0 / (lax.axis_size("tile") * TILE_CELLS)
    return (
        state_now,
        adjoint,
        summed[0] * grad_scale,
        summed[1] * grad_scale,
        summed[2] * grad_scale,
        summed[3] * grad_scale,
        summed[4] * grad_scale,
        summed[5] * grad_scale,
    )


def solution(mesh):
    return jax.shard_map(
        body,
        mesh=mesh,
        in_specs=(
            P(None, "depth", "tile"),
            P(None, "depth", "tile"),
            P("tile"),
            P("tile"),
            P(),
            P(),
            P(),
            P(),
            P(),
            P(),
        ),
        out_specs=(
            P(None, "depth", "tile"),
            P(None, "depth", "tile"),
            P(),
            P(),
            P(),
            P(),
            P(),
            P(),
        ),
        check_vma=False,
    )
```

```python
import functools

import jax
import jax.numpy as jnp
from jax import lax
from jax.experimental import pallas as pl
from jax.experimental.pallas import tpu as pltpu
from jax.sharding import PartitionSpec as P

TILE_SIDE = 32
LEVELS = 32
FEATURES = 64
TILE_CELLS = 1024
TRACERS = 2
LANES = 128

diffuse_coef = 0.2
step_size = 0.5


def pairings(tiles, depths):
    def at(t, d):
        return (t % tiles) * depths + d

    folds, rows, insides, outsides = [], [], [], []
    for t in range(tiles):
        for d in range(depths):
            me = at(t, d)
            ends = d in (0, depths - 1)
            folds.append((me, at(t + tiles // 2, d) if ends else at(t, d + 1 if d % 2 else d - 1)))
            rows.append((me, at(t, d - 1 if d % 2 else d + 1)))
            insides.append((me, at(t - 1 if t % 2 else t + 1, d)))
            outsides.append((me, at(t + 1 if t % 2 else t - 1, d)))
    return folds, rows, insides, outsides


def lane_of(shape):
    return lax.broadcasted_iota(jnp.int32, shape, 1)


def place_of(info):
    depth, last, tile = info[0], info[1], info[2]
    even_depth = depth % 2 == 0
    at_end = (depth == 0) | (depth == last)
    even_tile = tile % 2 == 0
    return even_depth, at_end, even_tile


def edges_of(scaled, info):
    even_depth, at_end, even_tile = place_of(info)
    half = scaled.shape[1] // 2
    lane = lane_of((scaled.shape[0], half))
    bottom = scaled[:, :half]
    top = pltpu.roll(scaled[:, half:], TILE_SIDE, 1)
    first = jnp.where(even_depth, bottom, top)
    second = jnp.where(even_depth, top, bottom)
    mirrored = first
    bit = 1
    while bit < TILE_SIDE:
        up = pltpu.roll(mirrored, bit, 1)
        down = pltpu.roll(mirrored, half - bit, 1)
        mirrored = jnp.where((lane & bit) != 0, up, down)
        bit *= 2
    first = jnp.where(at_end, mirrored, first)
    whole = scaled.shape[1]
    east = pltpu.roll(scaled, whole - (TILE_SIDE - 1), 1)

    def squeezed(cells):
        return jnp.where(lane % TILE_SIDE == 0, cells[:, :half], pltpu.roll(cells[:, half:], 1, 1))

    inside = squeezed(jnp.where(even_tile, east, scaled))
    outside = squeezed(jnp.where(even_tile, scaled, east))
    return first, second, inside, outside


def neighbour_sum(scaled, received, info):
    even_depth, _, even_tile = place_of(info)
    first, second, inside, outside = received
    whole = scaled.shape[1]
    half = whole // 2
    lane = lane_of(scaled.shape)
    place = lane % TILE_SIDE
    south = jnp.where(even_depth, first, second)
    north = pltpu.roll(jnp.where(even_depth, second, first), half - TILE_SIDE, 1)
    west = jnp.where(even_tile, outside, inside)
    east = jnp.where(even_tile, inside, outside)
    west = jnp.concatenate([west, pltpu.roll(west, half - 1, 1)], axis=1)
    east = jnp.concatenate([east, pltpu.roll(east, half - 1, 1)], axis=1)
    east = pltpu.roll(east, TILE_SIDE - 1, 1)
    south = jnp.concatenate([south, south], axis=1)
    north = jnp.concatenate([north, north], axis=1)
    west_cells = jnp.where(place == 0, west, pltpu.roll(scaled, 1, 1))
    east_cells = jnp.where(place == TILE_SIDE - 1, east, pltpu.roll(scaled, whole - 1, 1))
    south_cells = jnp.where(lane < TILE_SIDE, south, pltpu.roll(scaled, TILE_SIDE, 1))
    north_cells = jnp.where(lane >= whole - TILE_SIDE, north, pltpu.roll(scaled, whole - TILE_SIDE, 1))
    return west_cells + east_cells + south_cells + north_cells


def diffused(field, weight, weight_sums, received, info):
    sums = neighbour_sum(field * weight, received, info)
    return weight * (sums - field * weight_sums)


def mask_of(weight):
    return jnp.where(weight > 0.0, 1.0, 0.0)


def split_kernel(info, state_ref, observed_ref, *message_refs):
    depth = info[0]
    rows = state_ref.shape[0]
    width = message_refs[0].shape[1]
    for k, message_ref in enumerate(message_refs):
        start = pl.multiple_of((depth ^ k) * width, width)
        message_ref[:rows, :] = state_ref[:, pl.ds(start, width)]
        message_ref[rows:, :] = observed_ref[:, pl.ds(start, width)]


def gather_kernel(depths, info, edge_ref, land_ref, *refs):
    message_refs = refs[:depths]
    state_ref, observed_ref, weight_ref = refs[depths : depths + 3]
    edge_refs = refs[depths + 3 : depths + 7]
    held = refs[depths + 7]
    depth = info[0]
    width = state_ref.shape[1]
    levels = LEVELS // depths
    for k in range(depths):
        held[depth ^ k] = message_refs[k][...]
    for tracer in range(TRACERS):
        for d in range(depths):
            to = tracer * LEVELS + d * levels
            at = tracer * levels
            state_ref[to : to + levels, :] = held[d, at : at + levels, :]
            at = (TRACERS + tracer) * levels
            observed_ref[to : to + levels, :] = held[d, at : at + levels, :]
    start = pl.multiple_of(depth * width, width)
    land = land_ref[:, pl.ds(start, width)].astype(jnp.float32)
    weight = edge_ref[:, pl.ds(start, width)] * land
    weight_rows = jnp.broadcast_to(weight, weight_ref.shape)
    weight_ref[...] = weight_rows
    scaled = jnp.concatenate([state_ref[...] * weight, weight_rows], axis=0)
    for edge_out, edge in zip(edge_refs, edges_of(scaled, info)):
        edge_out[...] = edge


def sigmoid(z):
    return 0.5 * jnp.tanh(0.5 * z) + 0.5


def contract(a, b, dims):
    return lax.dot_general(a, b, ((dims[:1], dims[1:]), ((), ())), preferred_element_type=jnp.float32)


def forward_kernel(state_ref, w_in, b_in, w_mid, b_mid, w_out_t, b_out, q_ref, one_ref, slope_one_ref, two_ref, slope_two_ref):
    inputs = state_ref[...].astype(jnp.bfloat16)
    pre_one = contract(inputs, w_in[...], (0, 0)) + b_in[...]
    gate = sigmoid(pre_one)
    hidden = pre_one * gate
    slope_one_ref[...] = gate + hidden * (1.0 - gate)
    hidden_one = hidden.astype(jnp.bfloat16)
    one_ref[...] = hidden_one
    pre_two = contract(hidden_one, w_mid[...], (1, 0)) + b_mid[...]
    gate = sigmoid(pre_two)
    hidden = pre_two * gate
    slope_two_ref[...] = gate + hidden * (1.0 - gate)
    hidden_two = hidden.astype(jnp.bfloat16)
    two_ref[...] = hidden_two
    bias = b_out[...]
    bias = jnp.concatenate([bias, bias], axis=1)
    q_ref[...] = contract(w_out_t[...], hidden_two, (1, 1)) + bias


def first_step_kernel(info, state_ref, weight_ref, q_ref, e0, e1, e2, e3, next_ref, sums_ref, o0, o1, o2, o3):
    weight = weight_ref[0:1, :]
    state = state_ref[...]
    received = (e0[...], e1[...], e2[...], e3[...])
    scaled = jnp.concatenate([state * weight, weight_ref[...]], axis=0)
    sums = neighbour_sum(scaled, received, info)
    weight_sums = sums[FEATURES:, :]
    sums_ref[...] = weight_sums
    change = weight * (sums[:FEATURES, :] - state * weight_sums[0:1, :])
    state = state + diffuse_coef * change + step_size * mask_of(weight) * q_ref[...]
    next_ref[...] = state
    for edge_out, edge in zip((o0, o1, o2, o3), edges_of(state * weight, info)):
        edge_out[...] = edge


def last_step_kernel(
    info, state_ref, weight_ref, sums_ref, q_ref, observed_ref, e0, e1, e2, e3, next_ref, adjoint_ref, upstream_ref, o0, o1, o2, o3
):
    weight = weight_ref[0:1, :]
    mask = mask_of(weight)
    state = state_ref[...]
    received = (e0[...], e1[...], e2[...], e3[...])
    change = diffused(state, weight, sums_ref[0:1, :], received, info)
    state = state + diffuse_coef * change + step_size * mask * q_ref[...]
    next_ref[...] = state
    adjoint = mask * (state - observed_ref[...])
    adjoint_ref[...] = adjoint
    upstream_ref[...] = (step_size * mask * adjoint).astype(jnp.bfloat16)
    for edge_out, edge in zip((o0, o1, o2, o3), edges_of(adjoint * weight, info)):
        edge_out[...] = edge


def adjoint_kernel(info, adjoint_ref, weight_ref, sums_ref, back_ref, e0, e1, e2, e3, next_ref, upstream_ref, o0, o1, o2, o3):
    weight = weight_ref[0:1, :]
    adjoint = adjoint_ref[...]
    received = (e0[...], e1[...], e2[...], e3[...])
    adjoint = adjoint + diffuse_coef * diffused(adjoint, weight, sums_ref[0:1, :], received, info) + back_ref[...]
    next_ref[...] = adjoint
    upstream_ref[...] = (step_size * mask_of(weight) * adjoint).astype(jnp.bfloat16)
    for edge_out, edge in zip((o0, o1, o2, o3), edges_of(adjoint * weight, info)):
        edge_out[...] = edge


def end_kernel(depths, info, adjoint_ref, weight_ref, sums_ref, back_ref, final_ref, e0, e1, e2, e3, *refs):
    message_refs = refs[:depths]
    held = refs[depths]
    depth = info[0]
    weight = weight_ref[0:1, :]
    adjoint = adjoint_ref[...]
    received = (e0[...], e1[...], e2[...], e3[...])
    held[...] = adjoint + diffuse_coef * diffused(adjoint, weight, sums_ref[0:1, :], received, info) + back_ref[...]
    levels = LEVELS // depths
    for k in range(depths):
        for tracer in range(TRACERS):
            start = pl.multiple_of(tracer * LEVELS + (depth ^ k) * levels, levels)
            at = tracer * levels
            message_refs[k][at : at + levels, :] = final_ref[pl.ds(start, levels), :]
            at = (TRACERS + tracer) * levels
            message_refs[k][at : at + levels, :] = held[pl.ds(start, levels), :]


def join_kernel(depths, info, *refs):
    message_refs = refs[:depths]
    final_ref, sensitivity_ref = refs[depths:]
    depth = info[0]
    rows = final_ref.shape[0]
    width = message_refs[0].shape[1]
    for k, message_ref in enumerate(message_refs):
        start = pl.multiple_of((depth ^ k) * width, width)
        final_ref[:, pl.ds(start, width)] = message_ref[:rows, :]
        sensitivity_ref[:, pl.ds(start, width)] = message_ref[rows:, :]


CHUNKS = 8


def backward_kernel(with_sum, *refs):
    state_ref, upstream_ref, one_ref, slope_one_ref, two_ref, slope_two_ref, w_in, w_mid, w_out_t = refs[:9]
    if with_sum:
        earlier_ref, back_ref, total_ref = refs[9:]
    else:
        back_ref, total_ref = refs[9:]
    features = FEATURES
    width = w_mid.shape[0]
    mid_rows = width // CHUNKS
    side_rows = features // CHUNKS

    def store(first_row, rows, matrix):
        for c in range(CHUNKS):
            piece = matrix[c * rows : (c + 1) * rows, :]
            if with_sum:
                piece = piece + earlier_ref[c, first_row : first_row + rows, :]
            total_ref[c, first_row : first_row + rows, :] = piece

    upstream = upstream_ref[...]
    inputs = state_ref[...].astype(jnp.bfloat16)
    ones = jnp.ones((8, upstream.shape[1]), jnp.bfloat16)
    slope_two = (contract(upstream, w_out_t[...], (0, 0)) * slope_two_ref[...]).astype(jnp.bfloat16)
    slope_one = (contract(slope_two, w_mid[...], (1, 1)) * slope_one_ref[...]).astype(jnp.bfloat16)
    back_ref[...] = contract(w_in[...], slope_one, (1, 1))
    store(0, mid_rows, contract(one_ref[...], slope_two, (0, 0)))
    store(mid_rows, side_rows, contract(inputs, slope_one, (1, 0)))
    store(mid_rows + side_rows, side_rows, contract(upstream, two_ref[...], (1, 0)))
    bias_in = contract(ones, slope_one, (1, 0))
    bias_mid = contract(ones, slope_two, (1, 0))
    bias_out = contract(ones, upstream, (1, 1))
    bias_out = jnp.concatenate([bias_out, jnp.zeros((8, width - features), jnp.float32)], axis=1)
    first_row = mid_rows + 2 * side_rows
    for c in range(CHUNKS):
        rows = (bias_in, bias_mid, bias_out)[c] if c < 3 else jnp.zeros((8, width), jnp.float32)
        if with_sum:
            rows = rows + earlier_ref[c, first_row : first_row + 8, :]
        total_ref[c, first_row : first_row + 8, :] = rows


def spec_of(shape, dtype=jnp.float32):
    return jax.ShapeDtypeStruct(shape, dtype)


def called(kernel, outs, info, args, scratch=(), name=None):
    smem = pl.BlockSpec(memory_space=pltpu.SMEM)
    vmem = pl.BlockSpec(memory_space=pltpu.VMEM)
    in_specs = [smem] * len(info) + [vmem] * len(args)
    return pl.pallas_call(
        kernel,
        out_shape=tuple(outs),
        in_specs=in_specs,
        out_specs=tuple(vmem for _ in outs),
        scratch_shapes=list(scratch),
        compiler_params=pltpu.CompilerParams(vmem_limit_bytes=40 * 1024 * 1024),
        name=name,
    )(*info, *args)


def is_power_of_two(count):
    return count & (count - 1) == 0


def swapped(x, axis, even_bit, odd_bit):
    length = lax.axis_size(axis)
    return lax.ppermute(x, axis, [(i, i ^ (odd_bit if i & 1 else even_bit)) for i in range(length)])


def tile_rounds(length):
    bits = [1 << k for k in range(length.bit_length() - 1)]
    rounds = [(bits[0], bits[0])] if bits else []
    rest = bits[1:]
    for k in range(len(rest)):
        rounds.append((rest[k], rest[(k + 1) % len(rest)]))
    return rounds


def all_summed(block):
    tiles = lax.axis_size("tile")
    depths = lax.axis_size("depth")
    if not (is_power_of_two(tiles) and is_power_of_two(depths) and tiles <= CHUNKS):
        return lax.psum(block, ("tile", "depth"))
    tail = block.shape[1:]
    tile = lax.axis_index("tile")
    rounds = tile_rounds(tiles)
    sides = []
    for even_bit, odd_bit in rounds:
        bit = jnp.where(tile & 1 == 1, odd_bit, even_bit)
        sides.append(((tile & bit) != 0).astype(jnp.int32))
    for (even_bit, odd_bit), side in zip(rounds, sides):
        halves = block.reshape(2, block.shape[0] // 2, *tail)
        sent = lax.dynamic_index_in_dim(halves, 1 - side, 0, False)
        kept = lax.dynamic_index_in_dim(halves, side, 0, False)
        block = kept + swapped(sent, "tile", even_bit, odd_bit)
    bit = 1
    while bit < depths:
        block = block + swapped(block, "depth", bit, bit)
        bit *= 2
    for (even_bit, odd_bit), side in zip(reversed(rounds), reversed(sides)):
        other = swapped(block, "tile", even_bit, odd_bit)
        block = jnp.where(side == 0, jnp.stack([block, other]), jnp.stack([other, block]))
        block = block.reshape(block.shape[0] * block.shape[1], *tail)
    return block


def body(initial_state, observed, edge_weight, land, w_in, b_in, w_mid, b_mid, w_out, b_out):
    tiles = lax.axis_size("tile")
    depths = lax.axis_size("depth")
    tile = lax.axis_index("tile")
    depth = lax.axis_index("depth")
    info = (jnp.stack([depth, jnp.int32(depths - 1), tile]).astype(jnp.int32),)
    width = w_mid.shape[0]
    cells = TILE_CELLS // depths
    levels = LEVELS // depths
    rows = TRACERS * levels
    ways = pairings(tiles, depths)

    def exchanged(edges):
        return tuple(lax.ppermute(edge, ("tile", "depth"), way) for edge, way in zip(edges, ways))

    def across_depth(messages):
        out = [messages[0]]
        for k in range(1, depths):
            out.append(swapped(messages[k], "depth", k, k))
        return tuple(out)

    bias_in = b_in.reshape(1, width)
    bias_mid = b_mid.reshape(1, width)
    bias_out = jnp.broadcast_to(b_out[:, None], (FEATURES, LANES))
    w_out_t = w_out.T
    weights = (w_in, bias_in, w_mid, bias_mid, w_out_t, bias_out)
    field = spec_of((FEATURES, cells))
    half_field = spec_of((FEATURES, cells), jnp.bfloat16)
    edge = spec_of((FEATURES, LANES))
    cached = (
        field,
        spec_of((cells, width), jnp.bfloat16),
        spec_of((cells, width)),
        spec_of((cells, width), jnp.bfloat16),
        spec_of((cells, width)),
    )

    def closure(state):
        return called(forward_kernel, cached, (), (state, *weights), name="closure")

    message = spec_of((2 * rows, cells))
    messages = called(
        split_kernel,
        [message] * depths,
        info,
        (initial_state.reshape(rows, TILE_CELLS), observed.reshape(rows, TILE_CELLS)),
        name="split",
    )
    messages = across_depth(messages)
    first_edge = spec_of((FEATURES + 8, LANES))
    state_0, target, weight, *edges = called(
        functools.partial(gather_kernel, depths),
        (field, field, spec_of((8, cells)), first_edge, first_edge, first_edge, first_edge),
        info,
        (edge_weight.reshape(1, TILE_CELLS), land.reshape(1, TILE_CELLS), *messages),
        scratch=[pltpu.VMEM((depths, 2 * rows, cells), jnp.float32)],
        name="gather",
    )
    edges = exchanged(edges)
    q, *cache_0 = closure(state_0)
    state_1, weight_sums, *edges = called(
        first_step_kernel,
        (field, spec_of((8, cells)), edge, edge, edge, edge),
        info,
        (state_0, weight, q, *edges),
        name="step",
    )
    edges = exchanged(edges)
    q, *cache_1 = closure(state_1)
    state_2, adjoint, upstream, *edges = called(
        last_step_kernel,
        (field, field, half_field, edge, edge, edge, edge),
        info,
        (state_1, weight, weight_sums, q, target, *edges),
        name="last_step",
    )
    edges = exchanged(edges)
    total = spec_of((CHUNKS, width // CHUNKS + 2 * (FEATURES // CHUNKS) + 8, width))
    back, grads = called(
        functools.partial(backward_kernel, False),
        (field, total),
        (),
        (state_1, upstream, *cache_1, w_in, w_mid, w_out_t),
        name="backward",
    )
    adjoint, upstream, *edges = called(
        adjoint_kernel,
        (field, half_field, edge, edge, edge, edge),
        info,
        (adjoint, weight, weight_sums, back, *edges),
        name="adjoint",
    )
    edges = exchanged(edges)
    back, grads = called(
        functools.partial(backward_kernel, True),
        (field, total),
        (),
        (state_0, upstream, *cache_0, w_in, w_mid, w_out_t, grads),
        name="backward_sum",
    )
    messages = called(
        functools.partial(end_kernel, depths),
        [message] * depths,
        info,
        (adjoint, weight, weight_sums, back, state_2, *edges),
        scratch=[pltpu.VMEM((FEATURES, cells), jnp.float32)],
        name="end",
    )
    messages = across_depth(messages)
    whole = spec_of((rows, TILE_CELLS))
    final_state, sensitivity = called(functools.partial(join_kernel, depths), (whole, whole), info, messages, name="join")
    grads = all_summed(grads) * (1.0 / (tiles * TILE_CELLS))
    mid_rows = width // CHUNKS
    side_rows = FEATURES // CHUNKS
    first_row = mid_rows + 2 * side_rows
    grad_w_mid = grads[:, :mid_rows, :].reshape(width, width)
    grad_w_in = grads[:, mid_rows : mid_rows + side_rows, :].reshape(FEATURES, width)
    grad_w_out = grads[:, mid_rows + side_rows : first_row, :].reshape(FEATURES, width).T
    shape = (TRACERS, levels, TILE_CELLS)
    return (
        final_state.reshape(shape),
        sensitivity.reshape(shape),
        grad_w_in,
        grads[0, first_row],
        grad_w_mid,
        grads[1, first_row],
        grad_w_out,
        grads[2, first_row, :FEATURES],
    )


def solution(mesh):
    return jax.shard_map(
        body,
        mesh=mesh,
        in_specs=(
            P(None, "depth", "tile"),
            P(None, "depth", "tile"),
            P("tile"),
            P("tile"),
            P(),
            P(),
            P(),
            P(),
            P(),
            P(),
        ),
        out_specs=(
            P(None, "depth", "tile"),
            P(None, "depth", "tile"),
            P(),
            P(),
            P(),
            P(),
            P(),
            P(),
        ),
        check_vma=False,
    )
```

```python
import functools

import jax
import jax.numpy as jnp
from jax import lax
from jax.experimental import pallas as pl
from jax.experimental.pallas import tpu as pltpu
from jax.sharding import PartitionSpec as P

TILE_SIDE = 32
LEVELS = 32
FEATURES = 64
TILE_CELLS = 1024
TRACERS = 2
LANES = 128

diffuse_coef = 0.2
step_size = 0.5


def pairings(tiles, depths):
    def at(t, d):
        return (t % tiles) * depths + d

    folds, rows, insides, outsides = [], [], [], []
    for t in range(tiles):
        for d in range(depths):
            me = at(t, d)
            ends = d in (0, depths - 1)
            folds.append((me, at(t + tiles // 2, d) if ends else at(t, d + 1 if d % 2 else d - 1)))
            rows.append((me, at(t, d - 1 if d % 2 else d + 1)))
            insides.append((me, at(t - 1 if t % 2 else t + 1, d)))
            outsides.append((me, at(t + 1 if t % 2 else t - 1, d)))
    return folds, rows, insides, outsides


def lane_of(shape):
    return lax.broadcasted_iota(jnp.int32, shape, 1)


def place_of(info):
    depth, last, tile = info[0], info[1], info[2]
    even_depth = depth % 2 == 0
    at_end = (depth == 0) | (depth == last)
    even_tile = tile % 2 == 0
    return even_depth, at_end, even_tile


def edges_of(scaled, info):
    even_depth, at_end, even_tile = place_of(info)
    half = scaled.shape[1] // 2
    lane = lane_of((scaled.shape[0], half))
    bottom = scaled[:, :half]
    top = pltpu.roll(scaled[:, half:], TILE_SIDE, 1)
    first = jnp.where(even_depth, bottom, top)
    second = jnp.where(even_depth, top, bottom)
    mirrored = first
    bit = 1
    while bit < TILE_SIDE:
        up = pltpu.roll(mirrored, bit, 1)
        down = pltpu.roll(mirrored, half - bit, 1)
        mirrored = jnp.where((lane & bit) != 0, up, down)
        bit *= 2
    first = jnp.where(at_end, mirrored, first)
    whole = scaled.shape[1]
    east = pltpu.roll(scaled, whole - (TILE_SIDE - 1), 1)

    def squeezed(cells):
        return jnp.where(lane % TILE_SIDE == 0, cells[:, :half], pltpu.roll(cells[:, half:], 1, 1))

    inside = squeezed(jnp.where(even_tile, east, scaled))
    outside = squeezed(jnp.where(even_tile, scaled, east))
    return first, second, inside, outside


def neighbour_sum(scaled, received, info):
    even_depth, _, even_tile = place_of(info)
    first, second, inside, outside = received
    whole = scaled.shape[1]
    half = whole // 2
    lane = lane_of(scaled.shape)
    place = lane % TILE_SIDE
    south = jnp.where(even_depth, first, second)
    north = pltpu.roll(jnp.where(even_depth, second, first), half - TILE_SIDE, 1)
    west = jnp.where(even_tile, outside, inside)
    east = jnp.where(even_tile, inside, outside)
    west = jnp.concatenate([west, pltpu.roll(west, half - 1, 1)], axis=1)
    east = jnp.concatenate([east, pltpu.roll(east, half - 1, 1)], axis=1)
    east = pltpu.roll(east, TILE_SIDE - 1, 1)
    south = jnp.concatenate([south, south], axis=1)
    north = jnp.concatenate([north, north], axis=1)
    west_cells = jnp.where(place == 0, west, pltpu.roll(scaled, 1, 1))
    east_cells = jnp.where(place == TILE_SIDE - 1, east, pltpu.roll(scaled, whole - 1, 1))
    south_cells = jnp.where(lane < TILE_SIDE, south, pltpu.roll(scaled, TILE_SIDE, 1))
    north_cells = jnp.where(lane >= whole - TILE_SIDE, north, pltpu.roll(scaled, whole - TILE_SIDE, 1))
    return west_cells + east_cells + south_cells + north_cells


def diffused(field, weight, weight_sums, received, info):
    sums = neighbour_sum(field * weight, received, info)
    return weight * (sums - field * weight_sums)


def mask_of(weight):
    return jnp.where(weight > 0.0, 1.0, 0.0)


def split_kernel(info, state_ref, observed_ref, *message_refs):
    depth = info[0]
    rows = state_ref.shape[0]
    width = message_refs[0].shape[1]
    for k, message_ref in enumerate(message_refs):
        start = pl.multiple_of((depth ^ k) * width, width)
        message_ref[:rows, :] = state_ref[:, pl.ds(start, width)]
        message_ref[rows:, :] = observed_ref[:, pl.ds(start, width)]


def gather_kernel(depths, info, edge_ref, land_ref, *refs):
    message_refs = refs[:depths]
    state_ref, observed_ref, weight_ref = refs[depths : depths + 3]
    edge_refs = refs[depths + 3 : depths + 7]
    held = refs[depths + 7]
    depth = info[0]
    width = state_ref.shape[1]
    levels = LEVELS // depths
    for k in range(depths):
        held[depth ^ k] = message_refs[k][...]
    for tracer in range(TRACERS):
        for d in range(depths):
            to = tracer * LEVELS + d * levels
            at = tracer * levels
            state_ref[to : to + levels, :] = held[d, at : at + levels, :]
            at = (TRACERS + tracer) * levels
            observed_ref[to : to + levels, :] = held[d, at : at + levels, :]
    start = pl.multiple_of(depth * width, width)
    land = land_ref[:, pl.ds(start, width)].astype(jnp.float32)
    weight = edge_ref[:, pl.ds(start, width)] * land
    weight_rows = jnp.broadcast_to(weight, weight_ref.shape)
    weight_ref[...] = weight_rows
    scaled = jnp.concatenate([state_ref[...] * weight, weight_rows], axis=0)
    for edge_out, edge in zip(edge_refs, edges_of(scaled, info)):
        edge_out[...] = edge


def sigmoid(z):
    return 0.5 * jnp.tanh(0.5 * z) + 0.5


def contract(a, b, dims):
    return lax.dot_general(a, b, ((dims[:1], dims[1:]), ((), ())), preferred_element_type=jnp.float32)


def forward_kernel(state_ref, w_in, b_in, w_mid, b_mid, w_out_t, b_out, q_ref, one_ref, slope_one_ref, two_ref, slope_two_ref):
    inputs = state_ref[...].astype(jnp.bfloat16)
    pre_one = contract(inputs, w_in[...], (0, 0)) + b_in[...]
    gate = sigmoid(pre_one)
    hidden = pre_one * gate
    slope_one_ref[...] = gate + hidden * (1.0 - gate)
    hidden_one = hidden.astype(jnp.bfloat16)
    one_ref[...] = hidden_one
    pre_two = contract(hidden_one, w_mid[...], (1, 0)) + b_mid[...]
    gate = sigmoid(pre_two)
    hidden = pre_two * gate
    slope_two_ref[...] = gate + hidden * (1.0 - gate)
    hidden_two = hidden.astype(jnp.bfloat16)
    two_ref[...] = hidden_two
    bias = b_out[...]
    bias = jnp.concatenate([bias, bias], axis=1)
    q_ref[...] = contract(w_out_t[...], hidden_two, (1, 1)) + bias


def first_step_kernel(info, state_ref, weight_ref, q_ref, e0, e1, e2, e3, next_ref, sums_ref, o0, o1, o2, o3):
    weight = weight_ref[0:1, :]
    state = state_ref[...]
    received = (e0[...], e1[...], e2[...], e3[...])
    scaled = jnp.concatenate([state * weight, weight_ref[...]], axis=0)
    sums = neighbour_sum(scaled, received, info)
    weight_sums = sums[FEATURES:, :]
    sums_ref[...] = weight_sums
    change = weight * (sums[:FEATURES, :] - state * weight_sums[0:1, :])
    state = state + diffuse_coef * change + step_size * mask_of(weight) * q_ref[...]
    next_ref[...] = state
    for edge_out, edge in zip((o0, o1, o2, o3), edges_of(state * weight, info)):
        edge_out[...] = edge


def last_step_kernel(
    info, state_ref, weight_ref, sums_ref, q_ref, observed_ref, e0, e1, e2, e3, next_ref, adjoint_ref, upstream_ref, o0, o1, o2, o3
):
    weight = weight_ref[0:1, :]
    mask = mask_of(weight)
    state = state_ref[...]
    received = (e0[...], e1[...], e2[...], e3[...])
    change = diffused(state, weight, sums_ref[0:1, :], received, info)
    state = state + diffuse_coef * change + step_size * mask * q_ref[...]
    next_ref[...] = state
    adjoint = mask * (state - observed_ref[...])
    adjoint_ref[...] = adjoint
    upstream_ref[...] = (step_size * mask * adjoint).astype(jnp.bfloat16)
    for edge_out, edge in zip((o0, o1, o2, o3), edges_of(adjoint * weight, info)):
        edge_out[...] = edge


def adjoint_kernel(info, adjoint_ref, weight_ref, sums_ref, back_ref, e0, e1, e2, e3, next_ref, upstream_ref, o0, o1, o2, o3):
    weight = weight_ref[0:1, :]
    adjoint = adjoint_ref[...]
    received = (e0[...], e1[...], e2[...], e3[...])
    adjoint = adjoint + diffuse_coef * diffused(adjoint, weight, sums_ref[0:1, :], received, info) + back_ref[...]
    next_ref[...] = adjoint
    upstream_ref[...] = (step_size * mask_of(weight) * adjoint).astype(jnp.bfloat16)
    for edge_out, edge in zip((o0, o1, o2, o3), edges_of(adjoint * weight, info)):
        edge_out[...] = edge


def end_kernel(depths, info, adjoint_ref, weight_ref, sums_ref, back_ref, final_ref, e0, e1, e2, e3, *refs):
    message_refs = refs[:depths]
    held = refs[depths]
    depth = info[0]
    weight = weight_ref[0:1, :]
    adjoint = adjoint_ref[...]
    received = (e0[...], e1[...], e2[...], e3[...])
    held[...] = adjoint + diffuse_coef * diffused(adjoint, weight, sums_ref[0:1, :], received, info) + back_ref[...]
    levels = LEVELS // depths
    for k in range(depths):
        for tracer in range(TRACERS):
            start = pl.multiple_of(tracer * LEVELS + (depth ^ k) * levels, levels)
            at = tracer * levels
            message_refs[k][at : at + levels, :] = final_ref[pl.ds(start, levels), :]
            at = (TRACERS + tracer) * levels
            message_refs[k][at : at + levels, :] = held[pl.ds(start, levels), :]


def join_kernel(depths, info, *refs):
    message_refs = refs[:depths]
    final_ref, sensitivity_ref = refs[depths:]
    depth = info[0]
    rows = final_ref.shape[0]
    width = message_refs[0].shape[1]
    for k, message_ref in enumerate(message_refs):
        start = pl.multiple_of((depth ^ k) * width, width)
        final_ref[:, pl.ds(start, width)] = message_ref[:rows, :]
        sensitivity_ref[:, pl.ds(start, width)] = message_ref[rows:, :]


CHUNKS = 8


def backward_kernel(with_sum, *refs):
    state_ref, upstream_ref, one_ref, slope_one_ref, two_ref, slope_two_ref, w_in, w_mid, w_out_t = refs[:9]
    if with_sum:
        earlier_ref, back_ref, total_ref = refs[9:]
    else:
        back_ref, total_ref = refs[9:]
    features = FEATURES
    width = w_mid.shape[0]
    mid_rows = width // CHUNKS
    side_rows = features // CHUNKS

    def store(first_row, rows, matrix):
        for c in range(CHUNKS):
            piece = matrix[c * rows : (c + 1) * rows, :]
            if with_sum:
                piece = piece + earlier_ref[c, first_row : first_row + rows, :]
            total_ref[c, first_row : first_row + rows, :] = piece

    upstream = upstream_ref[...]
    inputs = state_ref[...].astype(jnp.bfloat16)
    ones = jnp.ones((8, upstream.shape[1]), jnp.bfloat16)
    slope_two = (contract(upstream, w_out_t[...], (0, 0)) * slope_two_ref[...]).astype(jnp.bfloat16)
    slope_one = (contract(slope_two, w_mid[...], (1, 1)) * slope_one_ref[...]).astype(jnp.bfloat16)
    back_ref[...] = contract(w_in[...], slope_one, (1, 1))
    store(0, mid_rows, contract(one_ref[...], slope_two, (0, 0)))
    store(mid_rows, side_rows, contract(inputs, slope_one, (1, 0)))
    store(mid_rows + side_rows, side_rows, contract(upstream, two_ref[...], (1, 0)))
    bias_in = contract(ones, slope_one, (1, 0))
    bias_mid = contract(ones, slope_two, (1, 0))
    bias_out = contract(ones, upstream, (1, 1))
    bias_out = jnp.concatenate([bias_out, jnp.zeros((8, width - features), jnp.float32)], axis=1)
    first_row = mid_rows + 2 * side_rows
    for c in range(CHUNKS):
        rows = (bias_in, bias_mid, bias_out)[c] if c < 3 else jnp.zeros((8, width), jnp.float32)
        if with_sum:
            rows = rows + earlier_ref[c, first_row : first_row + 8, :]
        total_ref[c, first_row : first_row + 8, :] = rows


def spec_of(shape, dtype=jnp.float32):
    return jax.ShapeDtypeStruct(shape, dtype)


def called(kernel, outs, info, args, scratch=(), name=None):
    smem = pl.BlockSpec(memory_space=pltpu.SMEM)
    vmem = pl.BlockSpec(memory_space=pltpu.VMEM)
    in_specs = [smem] * len(info) + [vmem] * len(args)
    return pl.pallas_call(
        kernel,
        out_shape=tuple(outs),
        in_specs=in_specs,
        out_specs=tuple(vmem for _ in outs),
        scratch_shapes=list(scratch),
        compiler_params=pltpu.CompilerParams(vmem_limit_bytes=40 * 1024 * 1024),
        name=name,
    )(*info, *args)


def is_power_of_two(count):
    return count & (count - 1) == 0


def swapped(x, axis, even_bit, odd_bit):
    length = lax.axis_size(axis)
    return lax.ppermute(x, axis, [(i, i ^ (odd_bit if i & 1 else even_bit)) for i in range(length)])


def tile_rounds(length):
    bits = [1 << k for k in range(length.bit_length() - 1)]
    rounds = [(bits[0], bits[0])] if bits else []
    rest = bits[1:]
    for k in range(len(rest)):
        rounds.append((rest[k], rest[(k + 1) % len(rest)]))
    return rounds


def halving_applies():
    tiles = lax.axis_size("tile")
    return is_power_of_two(tiles) and is_power_of_two(lax.axis_size("depth")) and tiles == CHUNKS


def all_summed(block, side_work):
    tail = block.shape[1:]
    depths = lax.axis_size("depth")
    tile = lax.axis_index("tile")
    rounds = tile_rounds(lax.axis_size("tile"))
    sides = []
    for even_bit, odd_bit in rounds:
        bit = jnp.where(tile & 1 == 1, odd_bit, even_bit)
        sides.append(((tile & bit) != 0).astype(jnp.int32))
    for (even_bit, odd_bit), side in zip(rounds, sides):
        halves = block.reshape(2, block.shape[0] // 2, *tail)
        sent = lax.dynamic_index_in_dim(halves, 1 - side, 0, False)
        kept = lax.dynamic_index_in_dim(halves, side, 0, False)
        sent = swapped(sent, "tile", even_bit, odd_bit)
        sent = side_work.send(sent)
        block = kept + sent
    bit = 1
    while bit < depths:
        sent = swapped(block, "depth", bit, bit)
        sent = side_work.send(sent)
        block = block + sent
        bit *= 2
    for (even_bit, odd_bit), side in zip(reversed(rounds), reversed(sides)):
        other = swapped(block, "tile", even_bit, odd_bit)
        other = side_work.send(other)
        block = jnp.where(side == 0, jnp.stack([block, other]), jnp.stack([other, block]))
        block = block.reshape(block.shape[0] * block.shape[1], *tail)
    return block


def body(initial_state, observed, edge_weight, land, w_in, b_in, w_mid, b_mid, w_out, b_out):
    tiles = lax.axis_size("tile")
    depths = lax.axis_size("depth")
    tile = lax.axis_index("tile")
    depth = lax.axis_index("depth")
    info = (jnp.stack([depth, jnp.int32(depths - 1), tile]).astype(jnp.int32),)
    width = w_mid.shape[0]
    cells = TILE_CELLS // depths
    levels = LEVELS // depths
    rows = TRACERS * levels
    ways = pairings(tiles, depths)

    def exchanged(edges):
        return tuple(lax.ppermute(edge, ("tile", "depth"), way) for edge, way in zip(edges, ways))

    def across_depth(messages):
        out = [messages[0]]
        for k in range(1, depths):
            out.append(swapped(messages[k], "depth", k, k))
        return tuple(out)

    bias_in = b_in.reshape(1, width)
    bias_mid = b_mid.reshape(1, width)
    bias_out = jnp.broadcast_to(b_out[:, None], (FEATURES, LANES))
    w_out_t = w_out.T
    weights = (w_in, bias_in, w_mid, bias_mid, w_out_t, bias_out)
    field = spec_of((FEATURES, cells))
    half_field = spec_of((FEATURES, cells), jnp.bfloat16)
    edge = spec_of((FEATURES, LANES))
    cached = (
        field,
        spec_of((cells, width), jnp.bfloat16),
        spec_of((cells, width)),
        spec_of((cells, width), jnp.bfloat16),
        spec_of((cells, width)),
    )

    def closure(state):
        return called(forward_kernel, cached, (), (state, *weights), name="closure")

    message = spec_of((2 * rows, cells))
    messages = called(
        split_kernel,
        [message] * depths,
        info,
        (initial_state.reshape(rows, TILE_CELLS), observed.reshape(rows, TILE_CELLS)),
        name="split",
    )
    messages = across_depth(messages)
    first_edge = spec_of((FEATURES + 8, LANES))
    state_0, target, weight, *edges = called(
        functools.partial(gather_kernel, depths),
        (field, field, spec_of((8, cells)), first_edge, first_edge, first_edge, first_edge),
        info,
        (edge_weight.reshape(1, TILE_CELLS), land.reshape(1, TILE_CELLS), *messages),
        scratch=[pltpu.VMEM((depths, 2 * rows, cells), jnp.float32)],
        name="gather",
    )
    edges = exchanged(edges)
    q, *cache_0 = closure(state_0)
    state_1, weight_sums, *edges = called(
        first_step_kernel,
        (field, spec_of((8, cells)), edge, edge, edge, edge),
        info,
        (state_0, weight, q, *edges),
        name="step",
    )
    edges = exchanged(edges)
    q, *cache_1 = closure(state_1)
    state_2, adjoint, upstream, *edges = called(
        last_step_kernel,
        (field, field, half_field, edge, edge, edge, edge),
        info,
        (state_1, weight, weight_sums, q, target, *edges),
        name="last_step",
    )
    edges = exchanged(edges)
    total = spec_of((CHUNKS, width // CHUNKS + 2 * (FEATURES // CHUNKS) + 8, width))
    back, grads = called(
        functools.partial(backward_kernel, False),
        (field, total),
        (),
        (state_1, upstream, *cache_1, w_in, w_mid, w_out_t),
        name="backward",
    )
    adjoint, upstream, *edges = called(
        adjoint_kernel,
        (field, half_field, edge, edge, edge, edge),
        info,
        (adjoint, weight, weight_sums, back, *edges),
        name="adjoint",
    )
    back, grads = called(
        functools.partial(backward_kernel, True),
        (field, total),
        (),
        (state_0, upstream, *cache_0, w_in, w_mid, w_out_t, grads),
        name="backward_sum",
    )
    whole = spec_of((rows, TILE_CELLS))
    ended = []

    def one_exchange(k, edge):
        return lax.ppermute(edge, ("tile", "depth"), ways[k])

    def last_transfers():
        held = list(edges)
        arrived = yield None
        arrived, *held = lax.optimization_barrier((arrived, *held))
        arrived = yield arrived
        got = [one_exchange(0, held[0]), one_exchange(1, held[1])]
        arrived, *rest = lax.optimization_barrier((arrived, *got, *held[2:]))
        got, held = rest[:2], rest[2:]
        arrived = yield arrived
        got += [one_exchange(2, held[0]), one_exchange(3, held[1])]
        arrived, *got = lax.optimization_barrier((arrived, *got))
        arrived = yield arrived
        messages = called(
            functools.partial(end_kernel, depths),
            [message] * depths,
            info,
            (adjoint, weight, weight_sums, back, state_2, *got),
            scratch=[pltpu.VMEM((FEATURES, cells), jnp.float32)],
            name="end",
        )
        out = [messages[0], swapped(messages[1], "depth", 1, 1)]
        arrived, *rest = lax.optimization_barrier((arrived, *out, *messages[2:]))
        out, messages = rest[:2], rest[2:]
        arrived = yield arrived
        out += [swapped(m, "depth", k + 2, k + 2) for k, m in enumerate(messages)]
        arrived, *out = lax.optimization_barrier((arrived, *out))
        arrived = yield arrived
        both = called(functools.partial(join_kernel, depths), (whole, whole), info, out, name="join")
        arrived, *both = lax.optimization_barrier((arrived, *both))
        ended.extend(both)
        while True:
            arrived = yield arrived

    side_work = last_transfers()
    next(side_work)
    if halving_applies():
        grads = all_summed(grads, side_work)
    else:
        grads = lax.psum(grads, ("tile", "depth"))
        for _ in range(6):
            grads = side_work.send(grads)
    final_state, sensitivity = ended
    grads = grads * (1.0 / (tiles * TILE_CELLS))
    mid_rows = width // CHUNKS
    side_rows = FEATURES // CHUNKS
    first_row = mid_rows + 2 * side_rows
    grad_w_mid = grads[:, :mid_rows, :].reshape(width, width)
    grad_w_in = grads[:, mid_rows : mid_rows + side_rows, :].reshape(FEATURES, width)
    grad_w_out = grads[:, mid_rows + side_rows : first_row, :].reshape(FEATURES, width).T
    shape = (TRACERS, levels, TILE_CELLS)
    return (
        final_state.reshape(shape),
        sensitivity.reshape(shape),
        grad_w_in,
        grads[0, first_row],
        grad_w_mid,
        grads[1, first_row],
        grad_w_out,
        grads[2, first_row, :FEATURES],
    )


def solution(mesh):
    return jax.shard_map(
        body,
        mesh=mesh,
        in_specs=(
            P(None, "depth", "tile"),
            P(None, "depth", "tile"),
            P("tile"),
            P("tile"),
            P(),
            P(),
            P(),
            P(),
            P(),
            P(),
        ),
        out_specs=(
            P(None, "depth", "tile"),
            P(None, "depth", "tile"),
            P(),
            P(),
            P(),
            P(),
            P(),
            P(),
        ),
        check_vma=False,
    )
```

```python
import functools

import jax
import jax.numpy as jnp
from jax import lax
from jax.experimental import pallas as pl
from jax.experimental.pallas import tpu as pltpu
from jax.sharding import PartitionSpec as P

TILE_SIDE = 32
LEVELS = 32
FEATURES = 64
TILE_CELLS = 1024
TRACERS = 2
LANES = 128
VMEM_LIMIT = 24 * 1024 * 1024

diffuse_coef = 0.2
step_size = 0.5


def pairings(tiles):
    fold = [(t, (t + tiles // 2) % tiles) for t in range(tiles)]
    inside = [(t, t ^ 1) for t in range(tiles)]
    outside = [(t, (t + 1 if t % 2 else t - 1) % tiles) for t in range(tiles)]
    return fold, inside, outside


def lane_of(shape):
    return lax.broadcasted_iota(jnp.int32, shape, 1)


def edges_of(scaled, info):
    even_tile = info[1] % 2 == 0
    rows, whole = scaled.shape
    lane = lane_of((rows, LANES))
    across = jnp.where(lane < LANES // 2, scaled[:, :LANES], scaled[:, whole - LANES :])
    bit = 1
    while bit < TILE_SIDE:
        up = pltpu.roll(across, bit, 1)
        down = pltpu.roll(across, LANES - bit, 1)
        across = jnp.where((lane & bit) != 0, up, down)
        bit *= 2
    place = lane % TILE_SIDE

    def squeezed(last):
        shift = LANES - (TILE_SIDE - 1) if last else 0
        out = None
        for k in range(whole // LANES):
            piece = scaled[:, k * LANES : (k + 1) * LANES]
            turn = (shift + k) % LANES
            piece = pltpu.roll(piece, turn, 1) if turn else piece
            out = piece if out is None else jnp.where(place == k, piece, out)
        return out

    west, east = squeezed(False), squeezed(True)
    return across, jnp.where(even_tile, east, west), jnp.where(even_tile, west, east)


def neighbour_sum(scaled, received, info):
    even_tile = info[1] % 2 == 0
    across, inside, outside = received
    whole = scaled.shape[1]
    count = whole // LANES
    lane = lane_of(scaled.shape)
    place = lane % TILE_SIDE
    west = jnp.where(even_tile, outside, inside)
    east = jnp.where(even_tile, inside, outside)

    def spread(edge, shift):
        turns = [(shift - k) % LANES for k in range(count)]
        return jnp.concatenate([pltpu.roll(edge, turn, 1) if turn else edge for turn in turns], axis=1)

    everywhere = jnp.concatenate([across] * count, axis=1)
    west_cells = jnp.where(place == 0, spread(west, 0), pltpu.roll(scaled, 1, 1))
    east_cells = jnp.where(place == TILE_SIDE - 1, spread(east, TILE_SIDE - 1), pltpu.roll(scaled, whole - 1, 1))
    south_cells = jnp.where(lane < TILE_SIDE, everywhere, pltpu.roll(scaled, TILE_SIDE, 1))
    north_cells = jnp.where(lane >= whole - TILE_SIDE, everywhere, pltpu.roll(scaled, whole - TILE_SIDE, 1))
    return west_cells + east_cells + south_cells + north_cells


def diffused(field, weight, weight_sums, received, info):
    sums = neighbour_sum(field * weight, received, info)
    return weight * (sums - field * weight_sums)


def mask_of(weight):
    return jnp.where(weight > 0.0, 1.0, 0.0)


def in_order(depths, info, message_refs, held, out_ref):
    for k in range(depths):
        held[info[0] ^ k] = message_refs[k][...]
    levels = LEVELS // depths
    for tracer in range(TRACERS):
        for d in range(depths):
            to = tracer * LEVELS + d * levels
            out_ref[to : to + levels, :] = held[d, tracer * levels : (tracer + 1) * levels, :]


def own_levels(depths, info, from_ref, to_ref):
    levels = LEVELS // depths
    for tracer in range(TRACERS):
        start = pl.multiple_of(tracer * LEVELS + info[0] * levels, levels)
        to_ref[tracer * levels : (tracer + 1) * levels, :] = from_ref[pl.ds(start, levels), :]


def gather_kernel(depths, info, edge_ref, land_ref, *refs):
    message_refs = refs[:depths]
    state_ref, weight_ref = refs[depths : depths + 2]
    edge_refs = refs[depths + 2 : depths + 5]
    in_order(depths, info, message_refs, refs[depths + 5], state_ref)
    weight = edge_ref[...] * land_ref[...].astype(jnp.float32)
    weight_rows = jnp.broadcast_to(weight, weight_ref.shape)
    weight_ref[...] = weight_rows
    scaled = jnp.concatenate([state_ref[...] * weight, weight_rows], axis=0)
    for edge_out, edge in zip(edge_refs, edges_of(scaled, info)):
        edge_out[...] = edge


def sigmoid(z):
    return 0.5 * jnp.tanh(0.5 * z) + 0.5


def contract(a, b, dims):
    return lax.dot_general(a, b, ((dims[:1], dims[1:]), ((), ())), preferred_element_type=jnp.float32)


def forward_kernel(state_ref, w_in, b_in, w_mid, b_mid, w_out_t, b_out, q_ref, one_ref, slope_one_ref, two_ref, slope_two_ref):
    inputs = state_ref[...].astype(jnp.bfloat16)
    pre_one = contract(inputs, w_in[...], (0, 0)) + b_in[...]
    gate = sigmoid(pre_one)
    hidden = pre_one * gate
    slope_one_ref[...] = gate + hidden * (1.0 - gate)
    hidden_one = hidden.astype(jnp.bfloat16)
    one_ref[...] = hidden_one
    pre_two = contract(hidden_one, w_mid[...], (1, 0)) + b_mid[...]
    gate = sigmoid(pre_two)
    hidden = pre_two * gate
    slope_two_ref[...] = gate + hidden * (1.0 - gate)
    hidden_two = hidden.astype(jnp.bfloat16)
    two_ref[...] = hidden_two
    bias = b_out[...]
    bias = jnp.concatenate([bias] * (q_ref.shape[1] // LANES), axis=1)
    q_ref[...] = contract(w_out_t[...], hidden_two, (1, 1)) + bias


def first_step_kernel(info, state_ref, weight_ref, q_ref, e0, e1, e2, next_ref, sums_ref, o0, o1, o2):
    weight = weight_ref[0:1, :]
    state = state_ref[...]
    received = (e0[...], e1[...], e2[...])
    scaled = jnp.concatenate([state * weight, weight_ref[...]], axis=0)
    sums = neighbour_sum(scaled, received, info)
    weight_sums = sums[FEATURES:, :]
    sums_ref[...] = weight_sums
    change = weight * (sums[:FEATURES, :] - state * weight_sums[0:1, :])
    state = state + diffuse_coef * change + step_size * mask_of(weight) * q_ref[...]
    next_ref[...] = state
    for edge_out, edge in zip((o0, o1, o2), edges_of(state * weight, info)):
        edge_out[...] = edge


def last_step_kernel(depths, info, state_ref, weight_ref, sums_ref, q_ref, e0, e1, e2, *refs):
    message_refs = refs[:depths]
    final_ref, adjoint_ref, upstream_ref, o0, o1, o2, held, ordered = refs[depths:]
    weight = weight_ref[0:1, :]
    mask = mask_of(weight)
    state = state_ref[...]
    received = (e0[...], e1[...], e2[...])
    change = diffused(state, weight, sums_ref[0:1, :], received, info)
    state = state + diffuse_coef * change + step_size * mask * q_ref[...]
    adjoint_ref[...] = state
    own_levels(depths, info, adjoint_ref, final_ref)
    in_order(depths, info, message_refs, held, ordered)
    adjoint = mask * (state - ordered[...])
    adjoint_ref[...] = adjoint
    upstream_ref[...] = (step_size * mask * adjoint).astype(jnp.bfloat16)
    for edge_out, edge in zip((o0, o1, o2), edges_of(adjoint * weight, info)):
        edge_out[...] = edge


def adjoint_kernel(depths, info, adjoint_ref, weight_ref, sums_ref, back_ref, e0, e1, e2, own_ref, upstream_ref, o0, o1, o2, held):
    weight = weight_ref[0:1, :]
    adjoint = adjoint_ref[...]
    received = (e0[...], e1[...], e2[...])
    adjoint = adjoint + diffuse_coef * diffused(adjoint, weight, sums_ref[0:1, :], received, info) + back_ref[...]
    upstream_ref[...] = (step_size * mask_of(weight) * adjoint).astype(jnp.bfloat16)
    held[...] = adjoint
    own_levels(depths, info, held, own_ref)
    for edge_out, edge in zip((o0, o1, o2), edges_of(own_ref[...] * weight, info)):
        edge_out[...] = edge


def end_kernel(depths, info, adjoint_ref, weight_ref, sums_ref, back_ref, e0, e1, e2, sensitivity_ref, own):
    weight = weight_ref[0:1, :]
    adjoint = adjoint_ref[...]
    received = (e0[...], e1[...], e2[...])
    own_levels(depths, info, back_ref, own)
    sensitivity_ref[...] = adjoint + diffuse_coef * diffused(adjoint, weight, sums_ref[0:1, :], received, info) + own[...]


CHUNKS = 8


def backward_kernel(with_sum, *refs):
    state_ref, upstream_ref, one_ref, slope_one_ref, two_ref, slope_two_ref, w_in, w_mid, w_out_t = refs[:9]
    if with_sum:
        earlier_ref, back_ref, total_ref = refs[9:]
    else:
        back_ref, total_ref = refs[9:]
    features = FEATURES
    width = w_mid.shape[0]
    mid_rows = width // CHUNKS
    side_rows = features // CHUNKS

    def store(first_row, rows, matrix):
        for c in range(CHUNKS):
            piece = matrix[c * rows : (c + 1) * rows, :]
            if with_sum:
                piece = piece + earlier_ref[c, first_row : first_row + rows, :]
            total_ref[c, first_row : first_row + rows, :] = piece

    upstream = upstream_ref[...]
    inputs = state_ref[...].astype(jnp.bfloat16)
    ones = jnp.ones((8, upstream.shape[1]), jnp.bfloat16)
    slope_two = (contract(upstream, w_out_t[...], (0, 0)) * slope_two_ref[...]).astype(jnp.bfloat16)
    slope_one = (contract(slope_two, w_mid[...], (1, 1)) * slope_one_ref[...]).astype(jnp.bfloat16)
    back_ref[...] = contract(w_in[...], slope_one, (1, 1))
    store(0, mid_rows, contract(one_ref[...], slope_two, (0, 0)))
    store(mid_rows, side_rows, contract(inputs, slope_one, (1, 0)))
    store(mid_rows + side_rows, side_rows, contract(upstream, two_ref[...], (1, 0)))
    bias_in = contract(ones, slope_one, (1, 0))
    bias_mid = contract(ones, slope_two, (1, 0))
    bias_out = contract(ones, upstream, (1, 1))
    bias_out = jnp.concatenate([bias_out, jnp.zeros((8, width - features), jnp.float32)], axis=1)
    first_row = mid_rows + 2 * side_rows
    for c in range(CHUNKS):
        rows = (bias_in, bias_mid, bias_out)[c] if c < 3 else jnp.zeros((8, width), jnp.float32)
        if with_sum:
            rows = rows + earlier_ref[c, first_row : first_row + 8, :]
        total_ref[c, first_row : first_row + 8, :] = rows


def spec_of(shape, dtype=jnp.float32):
    return jax.ShapeDtypeStruct(shape, dtype)


def called(kernel, outs, info, args, scratch=(), name=None):
    smem = pl.BlockSpec(memory_space=pltpu.SMEM)
    vmem = pl.BlockSpec(memory_space=pltpu.VMEM)
    in_specs = [smem] * len(info) + [vmem] * len(args)
    return pl.pallas_call(
        kernel,
        out_shape=tuple(outs),
        in_specs=in_specs,
        out_specs=tuple(vmem for _ in outs),
        scratch_shapes=list(scratch),
        compiler_params=pltpu.CompilerParams(vmem_limit_bytes=VMEM_LIMIT),
        name=name,
    )(*info, *args)


def is_power_of_two(count):
    return count & (count - 1) == 0


def swapped(x, axis, even_bit, odd_bit):
    length = lax.axis_size(axis)
    return lax.ppermute(x, axis, [(i, i ^ (odd_bit if i & 1 else even_bit)) for i in range(length)])


def tile_rounds(length):
    bits = [1 << k for k in range(length.bit_length() - 1)]
    rounds = [(bits[0], bits[0])] if bits else []
    rest = bits[1:]
    for k in range(len(rest)):
        rounds.append((rest[k], rest[(k + 1) % len(rest)]))
    return rounds


def halving_applies():
    tiles = lax.axis_size("tile")
    return tiles == CHUNKS


def all_summed(block, side_work):
    tail = block.shape[1:]
    tile = lax.axis_index("tile")
    rounds = tile_rounds(lax.axis_size("tile"))
    sides = []
    for even_bit, odd_bit in rounds:
        bit = jnp.where(tile & 1 == 1, odd_bit, even_bit)
        sides.append(((tile & bit) != 0).astype(jnp.int32))
    for (even_bit, odd_bit), side in zip(rounds, sides):
        halves = block.reshape(2, block.shape[0] // 2, *tail)
        sent = lax.dynamic_index_in_dim(halves, 1 - side, 0, False)
        kept = lax.dynamic_index_in_dim(halves, side, 0, False)
        sent = swapped(sent, "tile", even_bit, odd_bit)
        sent = side_work.send(sent)
        block = kept + sent
    for (even_bit, odd_bit), side in zip(reversed(rounds), reversed(sides)):
        other = swapped(block, "tile", even_bit, odd_bit)
        other = side_work.send(other)
        block = jnp.where(side == 0, jnp.stack([block, other]), jnp.stack([other, block]))
        block = block.reshape(block.shape[0] * block.shape[1], *tail)
    return block


def body(initial_state, observed, edge_weight, land, w_in, b_in, w_mid, b_mid, w_out, b_out):
    tiles = lax.axis_size("tile")
    depths = lax.axis_size("depth")
    info = (jnp.stack([lax.axis_index("depth"), lax.axis_index("tile")]).astype(jnp.int32),)
    width = w_mid.shape[0]
    levels = LEVELS // depths
    rows = TRACERS * levels
    ways = pairings(tiles)

    def exchanged(edges):
        return tuple(lax.ppermute(edge, "tile", way) for edge, way in zip(edges, ways))

    def from_depths(own):
        return (own, *(swapped(own, "depth", k, k) for k in range(1, depths)))

    bias_in = b_in.reshape(1, width)
    bias_mid = b_mid.reshape(1, width)
    bias_out = jnp.broadcast_to(b_out[:, None], (FEATURES, LANES))
    w_out_t = w_out.T
    weights = (w_in, bias_in, w_mid, bias_mid, w_out_t, bias_out)
    field = spec_of((FEATURES, TILE_CELLS))
    half_field = spec_of((FEATURES, TILE_CELLS), jnp.bfloat16)
    own_field = spec_of((rows, TILE_CELLS))
    weight_rows = spec_of((8, TILE_CELLS))
    edge = spec_of((FEATURES, LANES))
    first_edge = spec_of((FEATURES + 8, LANES))
    own_edge = spec_of((rows, LANES))
    held = pltpu.VMEM((depths, rows, TILE_CELLS), jnp.float32)
    whole = pltpu.VMEM((FEATURES, TILE_CELLS), jnp.float32)
    cached = (
        field,
        spec_of((TILE_CELLS, width), jnp.bfloat16),
        spec_of((TILE_CELLS, width)),
        spec_of((TILE_CELLS, width), jnp.bfloat16),
        spec_of((TILE_CELLS, width)),
    )

    def closure(state):
        return called(forward_kernel, cached, (), (state, *weights), name="closure")

    messages = from_depths(initial_state.reshape(rows, TILE_CELLS))
    state_0, weight, *edges = called(
        functools.partial(gather_kernel, depths),
        (field, weight_rows, first_edge, first_edge, first_edge),
        info,
        (edge_weight.reshape(1, TILE_CELLS), land.reshape(1, TILE_CELLS), *messages),
        scratch=[held],
        name="gather",
    )
    edges = exchanged(edges)
    state_0, target = lax.optimization_barrier((state_0, observed.reshape(rows, TILE_CELLS)))
    targets = from_depths(target)
    q, *cache_0 = closure(state_0)
    state_1, weight_sums, *edges = called(
        first_step_kernel,
        (field, weight_rows, edge, edge, edge),
        info,
        (state_0, weight, q, *edges),
        name="step",
    )
    edges = exchanged(edges)
    q, *cache_1 = closure(state_1)
    final_state, adjoint, upstream, *edges = called(
        functools.partial(last_step_kernel, depths),
        (own_field, field, half_field, edge, edge, edge),
        info,
        (state_1, weight, weight_sums, q, *edges, *targets),
        scratch=[held, whole],
        name="last_step",
    )
    edges = exchanged(edges)
    total = spec_of((CHUNKS, width // CHUNKS + 2 * (FEATURES // CHUNKS) + 8, width))
    back, grads = called(
        functools.partial(backward_kernel, False),
        (field, total),
        (),
        (state_1, upstream, *cache_1, w_in, w_mid, w_out_t),
        name="backward",
    )
    adjoint, upstream, *edges = called(
        functools.partial(adjoint_kernel, depths),
        (own_field, half_field, own_edge, own_edge, own_edge),
        info,
        (adjoint, weight, weight_sums, back, *edges),
        scratch=[whole],
        name="adjoint",
    )
    back, grads = called(
        functools.partial(backward_kernel, True),
        (field, total),
        (),
        (state_0, upstream, *cache_0, w_in, w_mid, w_out_t, grads),
        name="backward_sum",
    )
    ended = []

    def last_transfers():
        arrived = yield None
        arrived, *held = lax.optimization_barrier((arrived, *edges))
        arrived = yield arrived
        got = exchanged(held)
        arrived, *got = lax.optimization_barrier((arrived, *got))
        arrived = yield arrived
        (sensitivity,) = called(
            functools.partial(end_kernel, depths),
            (own_field,),
            info,
            (adjoint, weight, weight_sums, back, *got),
            scratch=[pltpu.VMEM((rows, TILE_CELLS), jnp.float32)],
            name="end",
        )
        arrived, sensitivity = lax.optimization_barrier((arrived, sensitivity))
        ended.append(sensitivity)
        while True:
            arrived = yield arrived

    side_work = last_transfers()
    next(side_work)
    if halving_applies():
        grads = all_summed(grads, side_work)
    else:
        grads = lax.psum(grads, "tile")
        for _ in range(3):
            grads = side_work.send(grads)
    (sensitivity,) = ended
    grads = grads * (1.0 / (tiles * TILE_CELLS))
    mid_rows = width // CHUNKS
    side_rows = FEATURES // CHUNKS
    first_row = mid_rows + 2 * side_rows
    grad_w_mid = grads[:, :mid_rows, :].reshape(width, width)
    grad_w_in = grads[:, mid_rows : mid_rows + side_rows, :].reshape(FEATURES, width)
    grad_w_out = grads[:, mid_rows + side_rows : first_row, :].reshape(FEATURES, width).T
    shape = (TRACERS, levels, TILE_CELLS)
    return (
        final_state.reshape(shape),
        sensitivity.reshape(shape),
        grad_w_in,
        grads[0, first_row],
        grad_w_mid,
        grads[1, first_row],
        grad_w_out,
        grads[2, first_row, :FEATURES],
    )


def solution(mesh):
    return jax.shard_map(
        body,
        mesh=mesh,
        in_specs=(
            P(None, "depth", "tile"),
            P(None, "depth", "tile"),
            P("tile"),
            P("tile"),
            P(),
            P(),
            P(),
            P(),
            P(),
            P(),
        ),
        out_specs=(
            P(None, "depth", "tile"),
            P(None, "depth", "tile"),
            P(),
            P(),
            P(),
            P(),
            P(),
            P(),
        ),
        check_vma=False,
    )
```

```python
import functools

import jax
import jax.numpy as jnp
from jax import lax
from jax.experimental import pallas as pl
from jax.experimental.pallas import tpu as pltpu
from jax.sharding import PartitionSpec as P

TILE_SIDE = 32
LEVELS = 32
FEATURES = 64
TILE_CELLS = 1024
TRACERS = 2
LANES = 128
VMEM_LIMIT = 24 * 1024 * 1024

diffuse_coef = 0.2
step_size = 0.5


def pairings(tiles):
    fold = [(t, (t + tiles // 2) % tiles) for t in range(tiles)]
    inside = [(t, t ^ 1) for t in range(tiles)]
    outside = [(t, (t + 1 if t % 2 else t - 1) % tiles) for t in range(tiles)]
    return fold, inside, outside


def lane_of(shape):
    return lax.broadcasted_iota(jnp.int32, shape, 1)


def edges_of(scaled, info):
    even_tile = info[1] % 2 == 0
    rows, whole = scaled.shape
    lane = lane_of((rows, LANES))
    across = jnp.where(lane < LANES // 2, scaled[:, :LANES], scaled[:, whole - LANES :])
    bit = 1
    while bit < TILE_SIDE:
        up = pltpu.roll(across, bit, 1)
        down = pltpu.roll(across, LANES - bit, 1)
        across = jnp.where((lane & bit) != 0, up, down)
        bit *= 2
    place = lane % TILE_SIDE

    def squeezed(last):
        shift = LANES - (TILE_SIDE - 1) if last else 0
        out = None
        for k in range(whole // LANES):
            piece = scaled[:, k * LANES : (k + 1) * LANES]
            turn = (shift + k) % LANES
            piece = pltpu.roll(piece, turn, 1) if turn else piece
            out = piece if out is None else jnp.where(place == k, piece, out)
        return out

    west, east = squeezed(False), squeezed(True)
    return across, jnp.where(even_tile, east, west), jnp.where(even_tile, west, east)


def neighbour_sum(scaled, received, info):
    even_tile = info[1] % 2 == 0
    across, inside, outside = received
    whole = scaled.shape[1]
    count = whole // LANES
    lane = lane_of(scaled.shape)
    place = lane % TILE_SIDE
    west = jnp.where(even_tile, outside, inside)
    east = jnp.where(even_tile, inside, outside)

    def spread(edge, shift):
        turns = [(shift - k) % LANES for k in range(count)]
        return jnp.concatenate([pltpu.roll(edge, turn, 1) if turn else edge for turn in turns], axis=1)

    everywhere = jnp.concatenate([across] * count, axis=1)
    west_cells = jnp.where(place == 0, spread(west, 0), pltpu.roll(scaled, 1, 1))
    east_cells = jnp.where(place == TILE_SIDE - 1, spread(east, TILE_SIDE - 1), pltpu.roll(scaled, whole - 1, 1))
    south_cells = jnp.where(lane < TILE_SIDE, everywhere, pltpu.roll(scaled, TILE_SIDE, 1))
    north_cells = jnp.where(lane >= whole - TILE_SIDE, everywhere, pltpu.roll(scaled, whole - TILE_SIDE, 1))
    return west_cells + east_cells + south_cells + north_cells


def diffused(field, weight, weight_sums, received, info):
    sums = neighbour_sum(field * weight, received, info)
    return weight * (sums - field * weight_sums)


def mask_of(weight):
    return jnp.where(weight > 0.0, 1.0, 0.0)


def in_order(depths, info, message_refs, held, out_ref):
    for k in range(depths):
        held[info[0] ^ k] = message_refs[k][...]
    levels = LEVELS // depths
    for tracer in range(TRACERS):
        for d in range(depths):
            to = tracer * LEVELS + d * levels
            out_ref[to : to + levels, :] = held[d, tracer * levels : (tracer + 1) * levels, :]


def own_levels(depths, info, from_ref, to_ref):
    levels = LEVELS // depths
    for tracer in range(TRACERS):
        start = pl.multiple_of(tracer * LEVELS + info[0] * levels, levels)
        to_ref[tracer * levels : (tracer + 1) * levels, :] = from_ref[pl.ds(start, levels), :]


def prepare_kernel(edge_ref, land_ref, state_ref, b_in, b_mid, b_out, weight_ref, own_ref, in_ref, mid_ref, out_ref):
    weight = edge_ref[...] * land_ref[...].astype(jnp.float32)
    weight_ref[...] = jnp.broadcast_to(weight, weight_ref.shape)
    own_ref[...] = state_ref[...]
    in_ref[...] = b_in[...].reshape(in_ref.shape)
    mid_ref[...] = b_mid[...].reshape(mid_ref.shape)
    rest = b_out[...].reshape(1, FEATURES)
    terms = []
    for _ in range(3):
        term = rest.astype(jnp.bfloat16)
        terms.append(term)
        rest = rest - term.astype(jnp.float32)
    terms.append(jnp.zeros((5, FEATURES), jnp.bfloat16))
    out_ref[...] = contract(jnp.concatenate(terms, axis=0), jnp.ones((8, LANES), jnp.bfloat16), (0, 0))


def gather_kernel(depths, info, weight_ref, *refs):
    message_refs = refs[:depths]
    state_ref = refs[depths]
    edge_refs = refs[depths + 1 : depths + 4]
    in_order(depths, info, message_refs, refs[depths + 4], state_ref)
    scaled = jnp.concatenate([state_ref[...] * weight_ref[0:1, :], weight_ref[...]], axis=0)
    for edge_out, edge in zip(edge_refs, edges_of(scaled, info)):
        edge_out[...] = edge


def sigmoid(z):
    return 0.5 * jnp.tanh(0.5 * z) + 0.5


def contract(a, b, dims):
    return lax.dot_general(a, b, ((dims[:1], dims[1:]), ((), ())), preferred_element_type=jnp.float32)


def layer(pre):
    gate = sigmoid(pre)
    hidden = pre * gate
    return hidden.astype(jnp.bfloat16), gate + hidden * (1.0 - gate)


def hidden_layers(state, w_in, b_in, w_mid, b_mid):
    inputs = state.astype(jnp.bfloat16)
    hidden_one, slope_one = layer(contract(inputs, w_in[...], (0, 0)) + b_in[...])
    hidden_two, slope_two = layer(contract(hidden_one, w_mid[...], (1, 0)) + b_mid[...])
    return hidden_one, slope_one, hidden_two, slope_two


def forward_kernel(state_ref, w_in, b_in, w_mid, b_mid, w_out_t, b_out, q_ref, *cache_refs):
    layers = hidden_layers(state_ref[...], w_in, b_in, w_mid, b_mid)
    bias = b_out[...]
    bias = jnp.concatenate([bias] * (q_ref.shape[1] // LANES), axis=1)
    q_ref[...] = contract(w_out_t[...], layers[2], (1, 1)) + bias
    for cache_ref, value in zip(cache_refs, layers):
        cache_ref[...] = value


def first_step_kernel(info, state_ref, weight_ref, q_ref, e0, e1, e2, next_ref, sums_ref, o0, o1, o2):
    weight = weight_ref[0:1, :]
    state = state_ref[...]
    received = (e0[...], e1[...], e2[...])
    scaled = jnp.concatenate([state * weight, weight_ref[...]], axis=0)
    sums = neighbour_sum(scaled, received, info)
    weight_sums = sums[FEATURES:, :]
    sums_ref[...] = weight_sums
    change = weight * (sums[:FEATURES, :] - state * weight_sums[0:1, :])
    state = state + diffuse_coef * change + step_size * mask_of(weight) * q_ref[...]
    next_ref[...] = state
    for edge_out, edge in zip((o0, o1, o2), edges_of(state * weight, info)):
        edge_out[...] = edge


def last_step_kernel(depths, info, state_ref, weight_ref, sums_ref, q_ref, e0, e1, e2, *refs):
    message_refs = refs[:depths]
    final_ref, adjoint_ref, upstream_ref, o0, o1, o2, held, ordered = refs[depths:]
    weight = weight_ref[0:1, :]
    mask = mask_of(weight)
    state = state_ref[...]
    received = (e0[...], e1[...], e2[...])
    change = diffused(state, weight, sums_ref[0:1, :], received, info)
    state = state + diffuse_coef * change + step_size * mask * q_ref[...]
    adjoint_ref[...] = state
    own_levels(depths, info, adjoint_ref, final_ref)
    in_order(depths, info, message_refs, held, ordered)
    adjoint = mask * (state - ordered[...])
    adjoint_ref[...] = adjoint
    upstream_ref[...] = (step_size * mask * adjoint).astype(jnp.bfloat16)
    for edge_out, edge in zip((o0, o1, o2), edges_of(adjoint * weight, info)):
        edge_out[...] = edge


def adjoint_kernel(depths, info, adjoint_ref, weight_ref, sums_ref, back_ref, e0, e1, e2, own_ref, upstream_ref, o0, o1, o2, held):
    weight = weight_ref[0:1, :]
    adjoint = adjoint_ref[...]
    received = (e0[...], e1[...], e2[...])
    adjoint = adjoint + diffuse_coef * diffused(adjoint, weight, sums_ref[0:1, :], received, info) + back_ref[...]
    upstream_ref[...] = (step_size * mask_of(weight) * adjoint).astype(jnp.bfloat16)
    held[...] = adjoint
    own_levels(depths, info, held, own_ref)
    for edge_out, edge in zip((o0, o1, o2), edges_of(own_ref[...] * weight, info)):
        edge_out[...] = edge


def end_kernel(depths, info, adjoint_ref, weight_ref, sums_ref, back_ref, e0, e1, e2, sensitivity_ref, own):
    weight = weight_ref[0:1, :]
    adjoint = adjoint_ref[...]
    received = (e0[...], e1[...], e2[...])
    own_levels(depths, info, back_ref, own)
    sensitivity_ref[...] = adjoint + diffuse_coef * diffused(adjoint, weight, sums_ref[0:1, :], received, info) + own[...]


HALVES = 2
EXPONENT_ROW = 4
TOP_EXPONENT = 14.0


def exponent_of(part):
    largest = jnp.max(jnp.max(jnp.abs(part), axis=0, keepdims=True), axis=1, keepdims=True)
    exponent = jnp.ceil(jnp.log2(jnp.maximum(largest, 1e-37))) - TOP_EXPONENT
    return jnp.clip(exponent, -110.0, 110.0)


def gradient_parts(inputs, upstream, layers, w_in, w_mid, w_out_t):
    hidden_one, slope_one, hidden_two, slope_two = layers
    width = w_mid.shape[0]
    ones = jnp.ones((8, upstream.shape[1]), jnp.bfloat16)
    slope_two = (contract(upstream, w_out_t[...], (0, 0)) * slope_two).astype(jnp.bfloat16)
    slope_one = (contract(slope_two, w_mid[...], (1, 1)) * slope_one).astype(jnp.bfloat16)
    back = contract(w_in[...], slope_one, (1, 1))
    bias_out = contract(ones, upstream, (1, 1))
    return back, (
        contract(hidden_one, slope_two, (0, 0)),
        contract(inputs, slope_one, (1, 0)),
        contract(upstream, hidden_two, (1, 0)),
        contract(ones, slope_one, (1, 0)),
        contract(ones, slope_two, (1, 0)),
        jnp.concatenate([bias_out, jnp.zeros((8, width - FEATURES), jnp.float32)], axis=1),
    )


def first_backward_kernel(state_ref, upstream_ref, w_in, b_in, w_mid, b_mid, w_out_t, back_ref, *part_refs):
    state = state_ref[...]
    layers = hidden_layers(state, w_in, b_in, w_mid, b_mid)
    back, parts = gradient_parts(state.astype(jnp.bfloat16), upstream_ref[...], layers, w_in, w_mid, w_out_t)
    back_ref[...] = back
    for part_ref, part in zip(part_refs, parts):
        part_ref[...] = part


def last_backward_kernel(info, state_ref, upstream_ref, one_ref, slope_one_ref, two_ref, slope_two_ref, w_in, w_mid, w_out_t, *refs):
    earlier_refs = refs[:6]
    back_ref, kept_ref, sent_ref = refs[6:]
    layers = (one_ref[...], slope_one_ref[...], two_ref[...], slope_two_ref[...])
    inputs = state_ref[...].astype(jnp.bfloat16)
    back, parts = gradient_parts(inputs, upstream_ref[...], layers, w_in, w_mid, w_out_t)
    back_ref[...] = back
    mid, side_in, side_out, bias_in, bias_mid, bias_out = [part + ref[...] for part, ref in zip(parts, earlier_refs)]
    row = lax.broadcasted_iota(jnp.int32, bias_in.shape, 0)
    own = info[1] % HALVES
    for half in range(HALVES):
        pieces = []
        for matrix in (mid, side_in, side_out):
            count = matrix.shape[0] // HALVES
            pieces.append(matrix[half * count : (half + 1) * count, :])
        tail = jnp.where(row == 0, bias_mid if half else bias_in, 0.0)
        if half == 0:
            tail = jnp.where(row == 1, bias_out, tail)
        pieces.append(tail)
        for k, exponent in enumerate([exponent_of(piece) for piece in pieces]):
            tail = jnp.where(row == EXPONENT_ROW + k, exponent, tail)
        pieces[-1] = tail

        def store(to_ref, pieces=pieces):
            at = 0
            for piece in pieces:
                to_ref[at : at + piece.shape[0], :] = piece
                at += piece.shape[0]

        pl.when(own == half)(functools.partial(store, kept_ref))
        pl.when(own != half)(functools.partial(store, sent_ref))


def spec_of(shape, dtype=jnp.float32):
    return jax.ShapeDtypeStruct(shape, dtype)


def called(kernel, outs, info, args, scratch=(), name=None):
    smem = pl.BlockSpec(memory_space=pltpu.SMEM)
    vmem = pl.BlockSpec(memory_space=pltpu.VMEM)
    in_specs = [smem] * len(info) + [vmem] * len(args)
    return pl.pallas_call(
        kernel,
        out_shape=tuple(outs),
        in_specs=in_specs,
        out_specs=tuple(vmem for _ in outs),
        scratch_shapes=list(scratch),
        compiler_params=pltpu.CompilerParams(vmem_limit_bytes=VMEM_LIMIT),
        name=name,
    )(*info, *args)


def swapped(x, axis, even_bit, odd_bit):
    length = lax.axis_size(axis)
    return lax.ppermute(x, axis, [(i, i ^ (odd_bit if i & 1 else even_bit)) for i in range(length)])


def by_part(rows, exponents):
    width = exponents.shape[1]
    starts = part_starts(rows)
    row = lax.broadcasted_iota(jnp.int32, (rows, width), 0)
    out = exponents[3:4]
    for k in (2, 1, 0):
        out = jnp.where(row < starts[k + 1], exponents[k : k + 1], out)
    return out


def part_starts(rows):
    side = FEATURES // HALVES
    return (0, rows - 8 - 2 * side, rows - 8 - side, rows - 8)


def exponents_of(half):
    return half[half.shape[0] - 8 + EXPONENT_ROW :, :].astype(jnp.float32)


def with_exponents(half, exponents):
    rows, width = half.shape
    row = lax.broadcasted_iota(jnp.int32, (rows, width), 0)
    out = half
    for k in range(4):
        out = jnp.where(row == rows - 8 + EXPONENT_ROW + k, exponents[k : k + 1], out)
    return out.astype(jnp.float16)


def exact_power(exponent):
    count = jnp.clip(-exponent, 0.0, 31.0).astype(jnp.int32)
    out = jnp.ones(exponent.shape, jnp.float32)
    for bit in range(5):
        out = out * jnp.where((count >> bit) & 1 == 1, 2.0 ** -(1 << bit), 1.0)
    return out


def summed_by_tile(kept, sent, side_work):
    rows = kept.shape[0]
    received = side_work.send(swapped(sent, "tile", 1, 1))
    exponents = jnp.maximum(exponents_of(kept), exponents_of(received)) + 1.0
    factors = lax.optimization_barrier(jnp.exp2(-exponents))
    half = with_exponents((kept + received) * by_part(rows, factors), exponents)
    for even_bit, odd_bit in ((2, 4), (4, 2)):
        received = side_work.send(swapped(half, "tile", even_bit, odd_bit))
        mine, other = exponents_of(half), exponents_of(received)
        exponents = jnp.maximum(mine, other) + 1.0
        factors = lax.optimization_barrier((exact_power(mine - exponents), exact_power(other - exponents)))
        total = half.astype(jnp.float32) * by_part(rows, factors[0])
        total = total + received.astype(jnp.float32) * by_part(rows, factors[1])
        half = with_exponents(total, exponents)
    other = swapped(half, "tile", 1, 1)
    first = lax.axis_index("tile") % HALVES == 0
    return jnp.where(first, jnp.stack([half, other]), jnp.stack([other, half]))


def body(initial_state, observed, edge_weight, land, w_in, b_in, w_mid, b_mid, w_out, b_out):
    tiles = lax.axis_size("tile")
    depths = lax.axis_size("depth")
    info = (jnp.stack([lax.axis_index("depth"), lax.axis_index("tile")]).astype(jnp.int32),)
    width = w_mid.shape[0]
    levels = LEVELS // depths
    rows = TRACERS * levels
    ways = pairings(tiles)

    def exchanged(edges):
        return tuple(lax.ppermute(edge, "tile", way) for edge, way in zip(edges, ways))

    def from_depths(own):
        return (own, *(swapped(own, "depth", k, k) for k in range(1, depths)))

    w_out_t = w_out.T
    field = spec_of((FEATURES, TILE_CELLS))
    half_field = spec_of((FEATURES, TILE_CELLS), jnp.bfloat16)
    own_field = spec_of((rows, TILE_CELLS))
    weight_rows = spec_of((8, TILE_CELLS))
    edge = spec_of((FEATURES, LANES))
    first_edge = spec_of((FEATURES + 8, LANES))
    own_edge = spec_of((rows, LANES))
    held = pltpu.VMEM((depths, rows, TILE_CELLS), jnp.float32)
    whole = pltpu.VMEM((FEATURES, TILE_CELLS), jnp.float32)
    cached = (
        spec_of((TILE_CELLS, width), jnp.bfloat16),
        spec_of((TILE_CELLS, width)),
        spec_of((TILE_CELLS, width), jnp.bfloat16),
        spec_of((TILE_CELLS, width)),
    )
    own_state = initial_state.reshape(rows, TILE_CELLS)
    others = from_depths(own_state)[1:]
    weight, own_state, bias_in, bias_mid, bias_out = called(
        prepare_kernel,
        (weight_rows, own_field, spec_of((1, width)), spec_of((1, width)), edge),
        (),
        (edge_weight.reshape(1, TILE_CELLS), land.reshape(1, TILE_CELLS), own_state, b_in, b_mid, b_out),
        name="prepare",
    )
    others, weight, own_state, bias_in, bias_mid, bias_out = lax.optimization_barrier(
        (others, weight, own_state, bias_in, bias_mid, bias_out)
    )
    weights = (w_in, bias_in, w_mid, bias_mid, w_out_t, bias_out)

    def closure(state, outs):
        return called(forward_kernel, (field, *outs), (), (state, *weights), name="closure")

    state_0, *edges = called(
        functools.partial(gather_kernel, depths),
        (field, first_edge, first_edge, first_edge),
        info,
        (weight, own_state, *others),
        scratch=[held],
        name="gather",
    )
    edges = exchanged(edges)
    state_0, target = lax.optimization_barrier((state_0, observed.reshape(rows, TILE_CELLS)))
    targets = from_depths(target)
    q, *cache_0 = closure(state_0, cached)
    state_1, weight_sums, *edges = called(
        first_step_kernel,
        (field, weight_rows, edge, edge, edge),
        info,
        (state_0, weight, q, *edges),
        name="step",
    )
    edges = exchanged(edges)
    (q,) = closure(state_1, ())
    final_state, adjoint, upstream, *edges = called(
        functools.partial(last_step_kernel, depths),
        (own_field, field, half_field, edge, edge, edge),
        info,
        (state_1, weight, weight_sums, q, *edges, *targets),
        scratch=[held, whole],
        name="last_step",
    )
    edges = exchanged(edges)
    side = spec_of((FEATURES, width))
    row_sum = spec_of((8, width))
    back, *parts = called(
        first_backward_kernel,
        (field, spec_of((width, width)), side, side, row_sum, row_sum, row_sum),
        (),
        (state_1, upstream, *weights[:5]),
        name="first_backward",
    )
    adjoint, upstream, *edges = called(
        functools.partial(adjoint_kernel, depths),
        (own_field, half_field, own_edge, own_edge, own_edge),
        info,
        (adjoint, weight, weight_sums, back, *edges),
        scratch=[whole],
        name="adjoint",
    )
    half = spec_of((width // HALVES + 2 * (FEATURES // HALVES) + 8, width))
    back, kept, sent = called(
        last_backward_kernel,
        (field, half, half),
        info,
        (state_0, upstream, *cache_0, w_in, w_mid, w_out_t, *parts),
        name="last_backward",
    )
    ended = []

    def last_transfers():
        arrived = yield None
        arrived, *held = lax.optimization_barrier((arrived, *edges))
        arrived = yield arrived
        got = exchanged(held)
        arrived, *got = lax.optimization_barrier((arrived, *got))
        arrived = yield arrived
        (sensitivity,) = called(
            functools.partial(end_kernel, depths),
            (own_field,),
            info,
            (adjoint, weight, weight_sums, back, *got),
            scratch=[pltpu.VMEM((rows, TILE_CELLS), jnp.float32)],
            name="end",
        )
        arrived, sensitivity = lax.optimization_barrier((arrived, sensitivity))
        ended.append(sensitivity)
        while True:
            arrived = yield arrived

    side_work = last_transfers()
    next(side_work)
    if tiles == 8:
        grads = summed_by_tile(kept, sent, side_work)
    else:
        first = lax.axis_index("tile") % HALVES == 0
        grads = jnp.where(first, jnp.stack([kept, sent]), jnp.stack([sent, kept]))
        grads = lax.psum(grads, "tile")
        for _ in range(3):
            grads = side_work.send(grads)
    (sensitivity,) = ended
    scale = 1.0 / (tiles * TILE_CELLS)
    starts = part_starts(half.shape[0])

    def part(k, count):
        values = grads[:, starts[k] : starts[k] + count, :]
        if grads.dtype != jnp.float16:
            return values * scale
        at = starts[3] + EXPONENT_ROW + k
        exponent = grads[:, at : at + 1, :].astype(jnp.float32)
        return values.astype(jnp.float32) * (jnp.exp2(exponent) * scale)

    grad_w_mid = part(0, width // HALVES).reshape(width, width)
    grad_w_in = part(1, FEATURES // HALVES).reshape(FEATURES, width)
    grad_w_out = part(2, FEATURES // HALVES).reshape(FEATURES, width).T
    biases = part(3, 2)
    shape = (TRACERS, levels, TILE_CELLS)
    return (
        final_state.reshape(shape),
        sensitivity.reshape(shape),
        grad_w_in,
        biases[0, 0],
        grad_w_mid,
        biases[1, 0],
        grad_w_out,
        biases[0, 1, :FEATURES],
    )


def solution(mesh):
    return jax.shard_map(
        body,
        mesh=mesh,
        in_specs=(
            P(None, "depth", "tile"),
            P(None, "depth", "tile"),
            P("tile"),
            P("tile"),
            P(),
            P(),
            P(),
            P(),
            P(),
            P(),
        ),
        out_specs=(
            P(None, "depth", "tile"),
            P(None, "depth", "tile"),
            P(),
            P(),
            P(),
            P(),
            P(),
            P(),
        ),
        check_vma=False,
    )
```

```python
import functools

import jax
import jax.numpy as jnp
from jax import lax
from jax.experimental import pallas as pl
from jax.experimental.pallas import tpu as pltpu
from jax.sharding import PartitionSpec as P

TILE_SIDE = 32
LEVELS = 32
FEATURES = 64
TILE_CELLS = 1024
TRACERS = 2
LANES = 128
VMEM_LIMIT = 24 * 1024 * 1024

diffuse_coef = 0.2
step_size = 0.5


def pairings(tiles):
    fold = [(t, (t + tiles // 2) % tiles) for t in range(tiles)]
    inside = [(t, t ^ 1) for t in range(tiles)]
    outside = [(t, (t + 1 if t % 2 else t - 1) % tiles) for t in range(tiles)]
    return fold, inside, outside


def lane_of(shape):
    return lax.broadcasted_iota(jnp.int32, shape, 1)


def edges_of(scaled, info):
    even_tile = info[1] % 2 == 0
    rows, whole = scaled.shape
    lane = lane_of((rows, LANES))
    across = jnp.where(lane < LANES // 2, scaled[:, :LANES], scaled[:, whole - LANES :])
    bit = 1
    while bit < TILE_SIDE:
        up = pltpu.roll(across, bit, 1)
        down = pltpu.roll(across, LANES - bit, 1)
        across = jnp.where((lane & bit) != 0, up, down)
        bit *= 2
    place = lane % TILE_SIDE

    def squeezed(last):
        shift = LANES - (TILE_SIDE - 1) if last else 0
        out = None
        for k in range(whole // LANES):
            piece = scaled[:, k * LANES : (k + 1) * LANES]
            turn = (shift + k) % LANES
            piece = pltpu.roll(piece, turn, 1) if turn else piece
            out = piece if out is None else jnp.where(place == k, piece, out)
        return out

    west, east = squeezed(False), squeezed(True)
    return across, jnp.where(even_tile, east, west), jnp.where(even_tile, west, east)


def neighbour_sum(scaled, received, info):
    even_tile = info[1] % 2 == 0
    across, inside, outside = received
    whole = scaled.shape[1]
    count = whole // LANES
    lane = lane_of(scaled.shape)
    place = lane % TILE_SIDE
    west = jnp.where(even_tile, outside, inside)
    east = jnp.where(even_tile, inside, outside)

    def spread(edge, shift):
        turns = [(shift - k) % LANES for k in range(count)]
        return jnp.concatenate([pltpu.roll(edge, turn, 1) if turn else edge for turn in turns], axis=1)

    everywhere = jnp.concatenate([across] * count, axis=1)
    west_cells = jnp.where(place == 0, spread(west, 0), pltpu.roll(scaled, 1, 1))
    east_cells = jnp.where(place == TILE_SIDE - 1, spread(east, TILE_SIDE - 1), pltpu.roll(scaled, whole - 1, 1))
    south_cells = jnp.where(lane < TILE_SIDE, everywhere, pltpu.roll(scaled, TILE_SIDE, 1))
    north_cells = jnp.where(lane >= whole - TILE_SIDE, everywhere, pltpu.roll(scaled, whole - TILE_SIDE, 1))
    return west_cells + east_cells + south_cells + north_cells


def diffused(field, weight, weight_sums, received, info):
    sums = neighbour_sum(field * weight, received, info)
    return weight * (sums - field * weight_sums)


def mask_of(weight):
    return jnp.where(weight > 0.0, 1.0, 0.0)


def in_order(depths, info, message_refs, held, out_ref):
    for k in range(depths):
        held[info[0] ^ k] = message_refs[k][...]
    levels = LEVELS // depths
    for tracer in range(TRACERS):
        for d in range(depths):
            to = tracer * LEVELS + d * levels
            out_ref[to : to + levels, :] = held[d, tracer * levels : (tracer + 1) * levels, :]


def own_levels(depths, info, from_ref, to_ref):
    levels = LEVELS // depths
    for tracer in range(TRACERS):
        start = pl.multiple_of(tracer * LEVELS + info[0] * levels, levels)
        to_ref[tracer * levels : (tracer + 1) * levels, :] = from_ref[pl.ds(start, levels), :]


def prepare_kernel(*refs):
    edge_ref, land_ref, state_ref, b_in, b_mid, b_out, *weight_refs = refs[:9]
    weight_out, own_ref, in_ref, mid_ref, out_ref, *held_refs = refs[9:17]
    edge, land, bias_in, bias_mid, bias_out, sems = refs[17:]
    pairs = [
        (edge_ref, edge),
        (land_ref, land),
        (b_in, bias_in),
        (b_mid, bias_mid),
        (b_out, bias_out),
        (state_ref, own_ref),
        *zip(weight_refs, held_refs),
    ]
    copies = [pltpu.make_async_copy(source, to, sems.at[k]) for k, (source, to) in enumerate(pairs)]
    for copy in copies:
        copy.start()
    for copy in copies:
        copy.wait()
    weight = edge[...] * land[...].astype(jnp.float32)
    weight_out[...] = jnp.broadcast_to(weight, weight_out.shape)
    in_ref[...] = bias_in[...].reshape(in_ref.shape)
    mid_ref[...] = bias_mid[...].reshape(mid_ref.shape)
    rest = bias_out[...].reshape(1, FEATURES)
    terms = []
    for _ in range(3):
        term = rest.astype(jnp.bfloat16)
        terms.append(term)
        rest = rest - term.astype(jnp.float32)
    terms.append(jnp.zeros((5, FEATURES), jnp.bfloat16))
    out_ref[...] = contract(jnp.concatenate(terms, axis=0), jnp.ones((8, LANES), jnp.bfloat16), (0, 0))


def gather_kernel(depths, info, weight_ref, *refs):
    message_refs = refs[:depths]
    state_ref = refs[depths]
    edge_refs = refs[depths + 1 : depths + 4]
    in_order(depths, info, message_refs, refs[depths + 4], state_ref)
    scaled = jnp.concatenate([state_ref[...] * weight_ref[0:1, :], weight_ref[...]], axis=0)
    for edge_out, edge in zip(edge_refs, edges_of(scaled, info)):
        edge_out[...] = edge


def sigmoid(z):
    return 0.5 * jnp.tanh(0.5 * z) + 0.5


def contract(a, b, dims):
    return lax.dot_general(a, b, ((dims[:1], dims[1:]), ((), ())), preferred_element_type=jnp.float32)


def layer(pre):
    gate = sigmoid(pre)
    hidden = pre * gate
    return hidden.astype(jnp.bfloat16), gate + hidden * (1.0 - gate)


def hidden_layers(state, w_in, b_in, w_mid, b_mid):
    inputs = state.astype(jnp.bfloat16)
    hidden_one, slope_one = layer(contract(inputs, w_in[...], (0, 0)) + b_in[...])
    hidden_two, slope_two = layer(contract(hidden_one, w_mid[...], (1, 0)) + b_mid[...])
    return hidden_one, slope_one, hidden_two, slope_two


def forward_kernel(state_ref, w_in, b_in, w_mid, b_mid, w_out_t, b_out, q_ref, *cache_refs):
    layers = hidden_layers(state_ref[...], w_in, b_in, w_mid, b_mid)
    bias = b_out[...]
    bias = jnp.concatenate([bias] * (q_ref.shape[1] // LANES), axis=1)
    q_ref[...] = contract(w_out_t[...], layers[2], (1, 1)) + bias
    for cache_ref, value in zip(cache_refs, layers):
        cache_ref[...] = value


def first_step_kernel(info, state_ref, weight_ref, q_ref, e0, e1, e2, next_ref, sums_ref, o0, o1, o2):
    weight = weight_ref[0:1, :]
    state = state_ref[...]
    received = (e0[...], e1[...], e2[...])
    scaled = jnp.concatenate([state * weight, weight_ref[...]], axis=0)
    sums = neighbour_sum(scaled, received, info)
    weight_sums = sums[FEATURES:, :]
    sums_ref[...] = weight_sums
    change = weight * (sums[:FEATURES, :] - state * weight_sums[0:1, :])
    state = state + diffuse_coef * change + step_size * mask_of(weight) * q_ref[...]
    next_ref[...] = state
    for edge_out, edge in zip((o0, o1, o2), edges_of(state * weight, info)):
        edge_out[...] = edge


def last_step_kernel(
    depths, info, state_ref, weight_ref, sums_ref, q_ref, e0, e1, e2, target_ref, final_ref, adjoint_ref, upstream_ref, o0, o1, o2, held, ordered
):
    weight = weight_ref[0:1, :]
    mask = mask_of(weight)
    state = state_ref[...]
    received = (e0[...], e1[...], e2[...])
    change = diffused(state, weight, sums_ref[0:1, :], received, info)
    state = state + diffuse_coef * change + step_size * mask * q_ref[...]
    adjoint_ref[...] = state
    own_levels(depths, info, adjoint_ref, final_ref)
    in_order(depths, info, [target_ref.at[k] for k in range(depths)], held, ordered)
    adjoint = mask * (state - ordered[...])
    adjoint_ref[...] = adjoint
    upstream_ref[...] = (step_size * mask * adjoint).astype(jnp.bfloat16)
    for edge_out, edge in zip((o0, o1, o2), edges_of(adjoint * weight, info)):
        edge_out[...] = edge


def adjoint_kernel(depths, info, adjoint_ref, weight_ref, sums_ref, back_ref, e0, e1, e2, own_ref, upstream_ref, o0, o1, o2, held):
    weight = weight_ref[0:1, :]
    adjoint = adjoint_ref[...]
    received = (e0[...], e1[...], e2[...])
    adjoint = adjoint + diffuse_coef * diffused(adjoint, weight, sums_ref[0:1, :], received, info) + back_ref[...]
    upstream_ref[...] = (step_size * mask_of(weight) * adjoint).astype(jnp.bfloat16)
    held[...] = adjoint
    own_levels(depths, info, held, own_ref)
    for edge_out, edge in zip((o0, o1, o2), edges_of(own_ref[...] * weight, info)):
        edge_out[...] = edge


def end_kernel(depths, info, adjoint_ref, weight_ref, sums_ref, back_ref, e0, e1, e2, sensitivity_ref, own):
    weight = weight_ref[0:1, :]
    adjoint = adjoint_ref[...]
    received = (e0[...], e1[...], e2[...])
    own_levels(depths, info, back_ref, own)
    sensitivity_ref[...] = adjoint + diffuse_coef * diffused(adjoint, weight, sums_ref[0:1, :], received, info) + own[...]


HALVES = 2
EXPONENT_ROW = 4
TOP_EXPONENT = 14.0


def block_parts(width):
    side = FEATURES // HALVES
    second = (width // HALVES - 2 * side) // 2 // 16 * 16
    return (width // HALVES - second,), (second, side, side)


def exponent_of(part):
    largest = jnp.max(jnp.max(jnp.abs(part), axis=0, keepdims=True), axis=1, keepdims=True)
    exponent = jnp.ceil(jnp.log2(jnp.maximum(largest, 1e-37))) - TOP_EXPONENT
    return jnp.clip(exponent, -110.0, 110.0)


def gradient_parts(inputs, upstream, layers, w_in, w_mid, w_out_t):
    hidden_one, slope_one, hidden_two, slope_two = layers
    width = w_mid.shape[0]
    ones = jnp.ones((8, upstream.shape[1]), jnp.bfloat16)
    slope_two = (contract(upstream, w_out_t[...], (0, 0)) * slope_two).astype(jnp.bfloat16)
    slope_one = (contract(slope_two, w_mid[...], (1, 1)) * slope_one).astype(jnp.bfloat16)
    back = contract(w_in[...], slope_one, (1, 1))
    bias_out = contract(ones, upstream, (1, 1))
    return back, (
        contract(hidden_one, slope_two, (0, 0)),
        contract(inputs, slope_one, (1, 0)),
        contract(upstream, hidden_two, (1, 0)),
        contract(ones, slope_one, (1, 0)),
        contract(ones, slope_two, (1, 0)),
        jnp.concatenate([bias_out, jnp.zeros((8, width - FEATURES), jnp.float32)], axis=1),
    )


def first_backward_kernel(state_ref, upstream_ref, w_in, b_in, w_mid, b_mid, w_out_t, back_ref, *part_refs):
    state = state_ref[...]
    layers = hidden_layers(state, w_in, b_in, w_mid, b_mid)
    back, parts = gradient_parts(state.astype(jnp.bfloat16), upstream_ref[...], layers, w_in, w_mid, w_out_t)
    back_ref[...] = back
    for part_ref, part in zip(part_refs, parts):
        part_ref[...] = part


def last_backward_kernel(info, state_ref, upstream_ref, one_ref, slope_one_ref, two_ref, slope_two_ref, w_in, w_mid, w_out_t, *refs):
    earlier_refs = refs[:6]
    back_ref, *block_refs = refs[6:]
    layers = (one_ref[...], slope_one_ref[...], two_ref[...], slope_two_ref[...])
    inputs = state_ref[...].astype(jnp.bfloat16)
    back, parts = gradient_parts(inputs, upstream_ref[...], layers, w_in, w_mid, w_out_t)
    back_ref[...] = back
    mid, side_in, side_out, bias_in, bias_mid, bias_out = [part + ref[...] for part, ref in zip(parts, earlier_refs)]
    row = lax.broadcasted_iota(jnp.int32, bias_in.shape, 0)
    own = info[1] % HALVES
    (top,), (_, side, _) = block_parts(w_mid.shape[0])
    for half in range(HALVES):
        count = mid.shape[0] // HALVES
        rows = mid[half * count : (half + 1) * count, :]
        tail = jnp.where(row == 0, bias_mid if half else bias_in, 0.0)
        if half == 0:
            tail = jnp.where(row == 1, bias_out, tail)
        at = slice(half * side, (half + 1) * side)
        blocks = ([rows[:top, :], jnp.zeros_like(tail)], [rows[top:, :], side_in[at, :], side_out[at, :], tail])
        for k, pieces in enumerate(blocks):
            last = pieces[-1]
            for j, piece in enumerate(pieces if k else pieces[:1]):
                last = jnp.where(row == EXPONENT_ROW + j, exponent_of(piece), last)
            pieces[-1] = last

            def store(to_ref, pieces=pieces):
                at = 0
                for piece in pieces:
                    to_ref[at : at + piece.shape[0], :] = piece
                    at += piece.shape[0]

            pl.when(own == half)(functools.partial(store, block_refs[k]))
            pl.when(own != half)(functools.partial(store, block_refs[2 + k]))


def spec_of(shape, dtype=jnp.float32):
    return jax.ShapeDtypeStruct(shape, dtype)


def closure_cost(passes):
    width = 640
    macs = TILE_CELLS * width * (2 * FEATURES + width) * passes
    return pl.CostEstimate(flops=2 * macs, transcendentals=2 * TILE_CELLS * width, bytes_accessed=8 * TILE_CELLS * width * passes)


def called(kernel, outs, info, args, scratch=(), name=None, fetches=False, passes=0):
    smem = pl.BlockSpec(memory_space=pltpu.SMEM)
    vmem = pl.BlockSpec(memory_space=pltpu.VMEM)
    in_specs = [smem] * len(info) + [pl.BlockSpec(memory_space=pltpu.HBM) if fetches else vmem] * len(args)
    return pl.pallas_call(
        kernel,
        out_shape=tuple(outs),
        in_specs=in_specs,
        out_specs=tuple(vmem for _ in outs),
        scratch_shapes=list(scratch),
        compiler_params=pltpu.CompilerParams(vmem_limit_bytes=VMEM_LIMIT),
        cost_estimate=closure_cost(passes) if passes else None,
        name=name,
    )(*info, *[pltpu.with_memory_space_constraint(arg, pltpu.HBM) if fetches else arg for arg in args])


def swapped(x, axis, even_bit, odd_bit):
    length = lax.axis_size(axis)
    return lax.ppermute(x, axis, [(i, i ^ (odd_bit if i & 1 else even_bit)) for i in range(length)])


def by_part(parts, exponents):
    if len(parts) == 1:
        return exponents[0:1]
    rows = sum(parts) + 8
    row = lax.broadcasted_iota(jnp.int32, (rows, exponents.shape[1]), 0)
    out = exponents[3:4]
    for k in (2, 1, 0):
        out = jnp.where(row < sum(parts[: k + 1]), exponents[k : k + 1], out)
    return out


def exponents_of(half):
    return half[half.shape[0] - 8 + EXPONENT_ROW :, :].astype(jnp.float32)


def with_exponents(half, exponents):
    rows, width = half.shape
    row = lax.broadcasted_iota(jnp.int32, (rows, width), 0)
    out = half
    for k in range(4):
        out = jnp.where(row == rows - 8 + EXPONENT_ROW + k, exponents[k : k + 1], out)
    return out.astype(jnp.float16)


def exact_power(exponent):
    count = jnp.clip(-exponent, 0.0, 31.0).astype(jnp.int32)
    out = jnp.ones(exponent.shape, jnp.float32)
    for bit in range(5):
        out = out * jnp.where((count >> bit) & 1 == 1, 2.0 ** -(1 << bit), 1.0)
    return out


def summed_by_tile(kept, sent, all_parts, side_work):
    received = [swapped(block, "tile", 1, 1) for block in sent]
    received[1] = side_work.send(received[1])
    blocks = []
    for block, other, parts in zip(kept, received, all_parts):
        exponents = jnp.maximum(exponents_of(block), exponents_of(other)) + 1.0
        factors = lax.optimization_barrier(jnp.exp2(-exponents))
        blocks.append(with_exponents((block + other) * by_part(parts, factors), exponents))
    for even_bit, odd_bit in ((2, 4), (4, 2)):
        received = [swapped(block, "tile", even_bit, odd_bit) for block in blocks]
        received[1] = side_work.send(received[1])
        added = []
        for block, other, parts in zip(blocks, received, all_parts):
            mine, others = exponents_of(block), exponents_of(other)
            exponents = jnp.maximum(mine, others) + 1.0
            factors = lax.optimization_barrier((exact_power(mine - exponents), exact_power(others - exponents)))
            total = block.astype(jnp.float32) * by_part(parts, factors[0])
            total = total + other.astype(jnp.float32) * by_part(parts, factors[1])
            added.append(with_exponents(total, exponents))
        blocks = added
    others = [swapped(block, "tile", 1, 1) for block in blocks]
    return by_half(blocks, others)


def by_half(own, others):
    first = lax.axis_index("tile") % HALVES == 0
    return [jnp.where(first, jnp.stack([a, b]), jnp.stack([b, a])) for a, b in zip(own, others)]


def body(initial_state, observed, edge_weight, land, w_in, b_in, w_mid, b_mid, w_out, b_out):
    tiles = lax.axis_size("tile")
    depths = lax.axis_size("depth")
    info = (jnp.stack([lax.axis_index("depth"), lax.axis_index("tile")]).astype(jnp.int32),)
    width = w_mid.shape[0]
    levels = LEVELS // depths
    rows = TRACERS * levels
    ways = pairings(tiles)

    def exchanged(edges):
        return tuple(lax.ppermute(edge, "tile", way) for edge, way in zip(edges, ways))

    def with_partner(blocks, bit):
        return jnp.concatenate([blocks, swapped(blocks, "depth", bit, bit)], axis=0)

    def from_depths(own):
        return (own, *(swapped(own, "depth", k, k) for k in range(1, depths)))

    w_out_t = w_out.T
    field = spec_of((FEATURES, TILE_CELLS))
    half_field = spec_of((FEATURES, TILE_CELLS), jnp.bfloat16)
    own_field = spec_of((rows, TILE_CELLS))
    weight_rows = spec_of((8, TILE_CELLS))
    edge = spec_of((FEATURES, LANES))
    first_edge = spec_of((FEATURES + 8, LANES))
    own_edge = spec_of((rows, LANES))
    held = pltpu.VMEM((depths, rows, TILE_CELLS), jnp.float32)
    whole = pltpu.VMEM((FEATURES, TILE_CELLS), jnp.float32)
    cached = (
        spec_of((TILE_CELLS, width), jnp.bfloat16),
        spec_of((TILE_CELLS, width)),
        spec_of((TILE_CELLS, width), jnp.bfloat16),
        spec_of((TILE_CELLS, width)),
    )
    own_state = initial_state.reshape(rows, TILE_CELLS)
    target = observed.reshape(rows, TILE_CELLS)
    others = from_depths(own_state)[1:]
    prepared = called(
        prepare_kernel,
        (
            weight_rows,
            own_field,
            spec_of((1, width)),
            spec_of((1, width)),
            edge,
            spec_of(w_in.shape, w_in.dtype),
            spec_of(w_mid.shape, w_mid.dtype),
            spec_of(w_out_t.shape, w_out_t.dtype),
        ),
        (),
        (edge_weight.reshape(1, TILE_CELLS), land.reshape(1, TILE_CELLS), own_state, b_in, b_mid, b_out, w_in, w_mid, w_out_t),
        scratch=[
            pltpu.VMEM((1, TILE_CELLS), jnp.float32),
            pltpu.VMEM((1, TILE_CELLS), jnp.int32),
            pltpu.VMEM((width,), jnp.float32),
            pltpu.VMEM((width,), jnp.float32),
            pltpu.VMEM((FEATURES,), jnp.float32),
            pltpu.SemaphoreType.DMA((9,)),
        ],
        name="prepare",
        fetches=True,
    )
    prepared, target = lax.optimization_barrier((prepared, target))
    targets = with_partner(target[None], 1)
    others, prepared = lax.optimization_barrier((others, prepared))
    weight, own_state, bias_in, bias_mid, bias_out, w_in, w_mid, w_out_t = prepared
    weights = (w_in, bias_in, w_mid, bias_mid, w_out_t, bias_out)

    def closure(state, outs):
        return called(forward_kernel, (field, *outs), (), (state, *weights), name="closure", passes=1)

    state_0, *edges = called(
        functools.partial(gather_kernel, depths),
        (field, first_edge, first_edge, first_edge),
        info,
        (weight, own_state, *others),
        scratch=[held],
        name="gather",
    )
    edges = exchanged(edges)
    state_0, targets = lax.optimization_barrier((state_0, targets))
    bit = 2
    while bit < depths:
        targets = with_partner(targets, bit)
        bit *= 2
    q, *cache_0 = closure(state_0, cached)
    state_1, weight_sums, *edges = called(
        first_step_kernel,
        (field, weight_rows, edge, edge, edge),
        info,
        (state_0, weight, q, *edges),
        name="step",
    )
    edges = exchanged(edges)
    (q,) = closure(state_1, ())
    final_state, adjoint, upstream, *edges = called(
        functools.partial(last_step_kernel, depths),
        (own_field, field, half_field, edge, edge, edge),
        info,
        (state_1, weight, weight_sums, q, *edges, targets),
        scratch=[held, whole],
        name="last_step",
    )
    edges = exchanged(edges)
    side = spec_of((FEATURES, width))
    row_sum = spec_of((8, width))
    back, *parts = called(
        first_backward_kernel,
        (field, spec_of((width, width)), side, side, row_sum, row_sum, row_sum),
        (),
        (state_1, upstream, *weights[:5]),
        name="first_backward",
        passes=3,
    )
    adjoint, upstream, *edges = called(
        functools.partial(adjoint_kernel, depths),
        (own_field, half_field, own_edge, own_edge, own_edge),
        info,
        (adjoint, weight, weight_sums, back, *edges),
        scratch=[whole],
        name="adjoint",
    )
    all_parts = block_parts(width)
    blocks = [spec_of((sum(parts) + 8, width)) for parts in all_parts]
    back, *blocks = called(
        last_backward_kernel,
        (field, *blocks, *blocks),
        info,
        (state_0, upstream, *cache_0, w_in, w_mid, w_out_t, *parts),
        name="last_backward",
        passes=2,
    )
    kept, sent = blocks[:2], blocks[2:]
    ended = []

    def last_transfers():
        arrived = yield None
        arrived, *held = lax.optimization_barrier((arrived, *edges))
        arrived = yield arrived
        got = exchanged(held)
        arrived, *got = lax.optimization_barrier((arrived, *got))
        arrived = yield arrived
        (sensitivity,) = called(
            functools.partial(end_kernel, depths),
            (own_field,),
            info,
            (adjoint, weight, weight_sums, back, *got),
            scratch=[pltpu.VMEM((rows, TILE_CELLS), jnp.float32)],
            name="end",
        )
        arrived, sensitivity = lax.optimization_barrier((arrived, sensitivity))
        ended.append(sensitivity)
        while True:
            arrived = yield arrived

    side_work = last_transfers()
    next(side_work)
    if tiles == 8:
        grads = summed_by_tile(kept, sent, all_parts, side_work)
    else:
        grads = lax.psum(by_half(kept, sent), "tile")
        for _ in range(3):
            grads[0] = side_work.send(grads[0])
    (sensitivity,) = ended
    scale = 1.0 / (tiles * TILE_CELLS)

    def part(b, k, count=None):
        start = sum(all_parts[b][:k])
        count = all_parts[b][k] if count is None else count
        values = grads[b][:, start : start + count, :]
        if values.dtype != jnp.float16:
            return values * scale
        at = sum(all_parts[b]) + EXPONENT_ROW + k
        exponent = grads[b][:, at : at + 1, :].astype(jnp.float32)
        return values.astype(jnp.float32) * (jnp.exp2(exponent) * scale)

    grad_w_mid = jnp.concatenate([part(0, 0), part(1, 0)], axis=1).reshape(width, width)
    grad_w_in = part(1, 1).reshape(FEATURES, width)
    grad_w_out = part(1, 2).reshape(FEATURES, width).T
    biases = part(1, 3, 2)
    shape = (TRACERS, levels, TILE_CELLS)
    return (
        final_state.reshape(shape),
        sensitivity.reshape(shape),
        grad_w_in,
        biases[0, 0],
        grad_w_mid,
        biases[1, 0],
        grad_w_out,
        biases[0, 1, :FEATURES],
    )


def solution(mesh):
    return jax.shard_map(
        body,
        mesh=mesh,
        in_specs=(
            P(None, "depth", "tile"),
            P(None, "depth", "tile"),
            P("tile"),
            P("tile"),
            P(),
            P(),
            P(),
            P(),
            P(),
            P(),
        ),
        out_specs=(
            P(None, "depth", "tile"),
            P(None, "depth", "tile"),
            P(),
            P(),
            P(),
            P(),
            P(),
            P(),
        ),
        check_vma=False,
    )
```

```python
import functools

import jax
import jax.numpy as jnp
from jax import lax
from jax.experimental import pallas as pl
from jax.experimental.pallas import tpu as pltpu
from jax.sharding import PartitionSpec as P

TILE_SIDE = 32
LEVELS = 32
FEATURES = 64
TILE_CELLS = 1024
TRACERS = 2
LANES = 128
VMEM_LIMIT = 24 * 1024 * 1024

diffuse_coef = 0.2
step_size = 0.5


def pairings(tiles):
    fold = [(t, (t + tiles // 2) % tiles) for t in range(tiles)]
    inside = [(t, t ^ 1) for t in range(tiles)]
    outside = [(t, (t + 1 if t % 2 else t - 1) % tiles) for t in range(tiles)]
    return fold, inside, outside


def lane_of(shape):
    return lax.broadcasted_iota(jnp.int32, shape, 1)


def edges_of(scaled, info):
    even_tile = info[1] % 2 == 0
    rows, whole = scaled.shape
    lane = lane_of((rows, LANES))
    across = jnp.where(lane < LANES // 2, scaled[:, :LANES], scaled[:, whole - LANES :])
    bit = 1
    while bit < TILE_SIDE:
        up = pltpu.roll(across, bit, 1)
        down = pltpu.roll(across, LANES - bit, 1)
        across = jnp.where((lane & bit) != 0, up, down)
        bit *= 2
    place = lane % TILE_SIDE

    def squeezed(last):
        shift = LANES - (TILE_SIDE - 1) if last else 0
        out = None
        for k in range(whole // LANES):
            piece = scaled[:, k * LANES : (k + 1) * LANES]
            turn = (shift + k) % LANES
            piece = pltpu.roll(piece, turn, 1) if turn else piece
            out = piece if out is None else jnp.where(place == k, piece, out)
        return out

    west, east = squeezed(False), squeezed(True)
    return across, jnp.where(even_tile, east, west), jnp.where(even_tile, west, east)


def neighbour_sum(scaled, received, info):
    even_tile = info[1] % 2 == 0
    across, inside, outside = received
    whole = scaled.shape[1]
    count = whole // LANES
    lane = lane_of(scaled.shape)
    place = lane % TILE_SIDE
    west = jnp.where(even_tile, outside, inside)
    east = jnp.where(even_tile, inside, outside)

    def spread(edge, shift):
        turns = [(shift - k) % LANES for k in range(count)]
        return jnp.concatenate([pltpu.roll(edge, turn, 1) if turn else edge for turn in turns], axis=1)

    everywhere = jnp.concatenate([across] * count, axis=1)
    west_cells = jnp.where(place == 0, spread(west, 0), pltpu.roll(scaled, 1, 1))
    east_cells = jnp.where(place == TILE_SIDE - 1, spread(east, TILE_SIDE - 1), pltpu.roll(scaled, whole - 1, 1))
    south_cells = jnp.where(lane < TILE_SIDE, everywhere, pltpu.roll(scaled, TILE_SIDE, 1))
    north_cells = jnp.where(lane >= whole - TILE_SIDE, everywhere, pltpu.roll(scaled, whole - TILE_SIDE, 1))
    return west_cells + east_cells + south_cells + north_cells


def diffused(field, weight, weight_sums, received, info):
    sums = neighbour_sum(field * weight, received, info)
    return weight * (sums - field * weight_sums)


def mask_of(weight):
    return jnp.where(weight > 0.0, 1.0, 0.0)


def in_order(depths, info, message_refs, held, out_ref):
    for k in range(depths):
        held[info[0] ^ k] = message_refs[k][...]
    levels = LEVELS // depths
    for tracer in range(TRACERS):
        for d in range(depths):
            to = tracer * LEVELS + d * levels
            out_ref[to : to + levels, :] = held[d, tracer * levels : (tracer + 1) * levels, :]


def own_levels(depths, info, from_ref, to_ref):
    levels = LEVELS // depths
    for tracer in range(TRACERS):
        start = pl.multiple_of(tracer * LEVELS + info[0] * levels, levels)
        to_ref[tracer * levels : (tracer + 1) * levels, :] = from_ref[pl.ds(start, levels), :]


def prepare_kernel(*refs):
    edge_ref, land_ref, state_ref, b_in, b_mid, b_out, *weight_refs = refs[:9]
    weight_out, own_ref, in_ref, mid_ref, out_ref, *held_refs = refs[9:17]
    edge, land, bias_in, bias_mid, bias_out, sems = refs[17:]
    pairs = [
        (edge_ref, edge),
        (land_ref, land),
        (b_in, bias_in),
        (b_mid, bias_mid),
        (b_out, bias_out),
        (state_ref, own_ref),
        *zip(weight_refs, held_refs),
    ]
    copies = [pltpu.make_async_copy(source, to, sems.at[k]) for k, (source, to) in enumerate(pairs)]
    for copy in copies:
        copy.start()
    for copy in copies:
        copy.wait()
    weight = edge[...] * land[...].astype(jnp.float32)
    weight_out[...] = jnp.broadcast_to(weight, weight_out.shape)
    in_ref[...] = 0.5 * bias_in[...].reshape(in_ref.shape)
    mid_ref[...] = 0.5 * bias_mid[...].reshape(mid_ref.shape)
    for held_ref in held_refs[:2]:
        held_ref[...] = (0.5 * held_ref[...].astype(jnp.float32)).astype(jnp.bfloat16)
    rest = bias_out[...].reshape(1, FEATURES)
    terms = []
    for _ in range(3):
        term = rest.astype(jnp.bfloat16)
        terms.append(term)
        rest = rest - term.astype(jnp.float32)
    terms.append(jnp.zeros((5, FEATURES), jnp.bfloat16))
    out_ref[...] = contract(jnp.concatenate(terms, axis=0), jnp.ones((8, LANES), jnp.bfloat16), (0, 0))


def gather_kernel(depths, info, weight_ref, *refs):
    message_refs = refs[:depths]
    state_ref = refs[depths]
    edge_refs = refs[depths + 1 : depths + 4]
    in_order(depths, info, message_refs, refs[depths + 4], state_ref)
    scaled = jnp.concatenate([state_ref[...] * weight_ref[0:1, :], weight_ref[...]], axis=0)
    for edge_out, edge in zip(edge_refs, edges_of(scaled, info)):
        edge_out[...] = edge


def contract(a, b, dims):
    return lax.dot_general(a, b, ((dims[:1], dims[1:]), ((), ())), preferred_element_type=jnp.float32)


def layer(y):
    a = 1.0 + jnp.tanh(y)
    hidden = y * a
    return hidden.astype(jnp.bfloat16), a * ((1.0 + (y + y)) - hidden)


def hidden_layers(state, w_in, b_in, w_mid, b_mid):
    inputs = state.astype(jnp.bfloat16)
    hidden_one, slope_one = layer(contract(inputs, w_in[...], (0, 0)) + b_in[...])
    hidden_two, slope_two = layer(contract(hidden_one, w_mid[...], (1, 0)) + b_mid[...])
    return hidden_one, slope_one, hidden_two, slope_two


def forward_kernel(state_ref, w_in, b_in, w_mid, b_mid, w_out_t, b_out, q_ref, *cache_refs):
    layers = hidden_layers(state_ref[...], w_in, b_in, w_mid, b_mid)
    bias = b_out[...]
    bias = jnp.concatenate([bias] * (q_ref.shape[1] // LANES), axis=1)
    q_ref[...] = contract(w_out_t[...], layers[2], (1, 1)) + bias
    for cache_ref, value in zip(cache_refs, layers):
        cache_ref[...] = value


def first_step_kernel(info, state_ref, weight_ref, q_ref, e0, e1, e2, next_ref, sums_ref, o0, o1, o2):
    weight = weight_ref[0:1, :]
    state = state_ref[...]
    received = (e0[...], e1[...], e2[...])
    scaled = jnp.concatenate([state * weight, weight_ref[...]], axis=0)
    sums = neighbour_sum(scaled, received, info)
    weight_sums = sums[FEATURES:, :]
    sums_ref[...] = weight_sums
    change = weight * (sums[:FEATURES, :] - state * weight_sums[0:1, :])
    state = state + diffuse_coef * change + step_size * mask_of(weight) * q_ref[...]
    next_ref[...] = state
    for edge_out, edge in zip((o0, o1, o2), edges_of(state * weight, info)):
        edge_out[...] = edge


def last_step_kernel(depths, info, state_ref, weight_ref, sums_ref, q_ref, e0, e1, e2, *refs):
    target_refs = refs[:depths]
    final_ref, adjoint_ref, upstream_ref, o0, o1, o2, held, ordered = refs[depths:]
    weight = weight_ref[0:1, :]
    mask = mask_of(weight)
    state = state_ref[...]
    received = (e0[...], e1[...], e2[...])
    change = diffused(state, weight, sums_ref[0:1, :], received, info)
    state = state + diffuse_coef * change + step_size * mask * q_ref[...]
    adjoint_ref[...] = state
    own_levels(depths, info, adjoint_ref, final_ref)
    in_order(depths, info, target_refs, held, ordered)
    adjoint = mask * (state - ordered[...])
    adjoint_ref[...] = adjoint
    upstream_ref[...] = (step_size * mask * adjoint).astype(jnp.bfloat16)
    for edge_out, edge in zip((o0, o1, o2), edges_of(adjoint * weight, info)):
        edge_out[...] = edge


def adjoint_kernel(depths, info, adjoint_ref, weight_ref, sums_ref, back_ref, e0, e1, e2, own_ref, upstream_ref, o0, o1, o2, held):
    weight = weight_ref[0:1, :]
    adjoint = adjoint_ref[...]
    received = (e0[...], e1[...], e2[...])
    adjoint = adjoint + diffuse_coef * diffused(adjoint, weight, sums_ref[0:1, :], received, info) + back_ref[...]
    upstream_ref[...] = (step_size * mask_of(weight) * adjoint).astype(jnp.bfloat16)
    held[...] = adjoint
    own_levels(depths, info, held, own_ref)
    for edge_out, edge in zip((o0, o1, o2), edges_of(own_ref[...] * weight, info)):
        edge_out[...] = edge


def end_kernel(depths, info, adjoint_ref, weight_ref, sums_ref, back_ref, e0, e1, e2, sensitivity_ref, own):
    weight = weight_ref[0:1, :]
    adjoint = adjoint_ref[...]
    received = (e0[...], e1[...], e2[...])
    own_levels(depths, info, back_ref, own)
    sensitivity_ref[...] = adjoint + diffuse_coef * diffused(adjoint, weight, sums_ref[0:1, :], received, info) + own[...]


HALVES = 2
EXPONENT_ROW = 4
TOP_EXPONENT = 14.0


def block_parts(width):
    side = FEATURES // HALVES
    second = (width // HALVES - 2 * side) // 2 // 16 * 16
    return (second, side, side), (width // HALVES - second,)


def exponent_of(part):
    largest = jnp.max(jnp.max(jnp.abs(part), axis=0, keepdims=True), axis=1, keepdims=True)
    exponent = jnp.ceil(jnp.log2(jnp.maximum(largest, 1e-37))) - TOP_EXPONENT
    return jnp.clip(exponent, -110.0, 110.0)


def gradient_parts(inputs, upstream, layers, w_in, w_mid, w_out_t):
    hidden_one, slope_one, hidden_two, slope_two = layers
    width = w_mid.shape[0]
    ones = jnp.ones((8, upstream.shape[1]), jnp.bfloat16)
    half = (0.5 * upstream.astype(jnp.float32)).astype(jnp.bfloat16)
    slope_two = (contract(half, w_out_t[...], (0, 0)) * slope_two).astype(jnp.bfloat16)
    slope_one = (contract(slope_two, w_mid[...], (1, 1)) * slope_one).astype(jnp.bfloat16)
    back = 2.0 * contract(w_in[...], slope_one, (1, 1))
    bias_out = contract(ones, upstream, (1, 1))
    return back, (
        contract(hidden_one, slope_two, (0, 0)),
        contract(inputs, slope_one, (1, 0)),
        contract(upstream, hidden_two, (1, 0)),
        contract(ones, slope_one, (1, 0)),
        contract(ones, slope_two, (1, 0)),
        jnp.concatenate([bias_out, jnp.zeros((8, width - FEATURES), jnp.float32)], axis=1),
    )


def first_backward_kernel(
    state_ref, upstream_ref, one_ref, slope_one_ref, two_ref, slope_two_ref, w_in, w_mid, w_out_t, back_ref, *part_refs
):
    layers = (one_ref[...], slope_one_ref[...], two_ref[...], slope_two_ref[...])
    inputs = state_ref[...].astype(jnp.bfloat16)
    back, parts = gradient_parts(inputs, upstream_ref[...], layers, w_in, w_mid, w_out_t)
    back_ref[...] = back
    for part_ref, part in zip(part_refs, parts):
        part_ref[...] = part


def last_backward_kernel(info, state_ref, upstream_ref, one_ref, slope_one_ref, two_ref, slope_two_ref, w_in, w_mid, w_out_t, *refs):
    earlier_refs = refs[:6]
    back_ref, *block_refs = refs[6:]
    layers = (one_ref[...], slope_one_ref[...], two_ref[...], slope_two_ref[...])
    inputs = state_ref[...].astype(jnp.bfloat16)
    back, parts = gradient_parts(inputs, upstream_ref[...], layers, w_in, w_mid, w_out_t)
    back_ref[...] = back
    mid, side_in, side_out, bias_in, bias_mid, bias_out = [part + ref[...] for part, ref in zip(parts, earlier_refs)]
    row = lax.broadcasted_iota(jnp.int32, bias_in.shape, 0)
    is_first = info[1] % HALVES == 0
    (top, side, _), _ = block_parts(w_mid.shape[0])
    count = mid.shape[0] // HALVES
    tails = (
        jnp.where(row == 0, bias_in, jnp.where(row == 1, bias_out, 0.0)),
        jnp.where(row == 0, bias_mid, 0.0),
    )
    for other in (False, True):

        def one(halves):
            return jnp.where(is_first, halves[other], halves[not other])

        first = [
            one((mid[:top, :], mid[count : count + top, :])),
            one((side_in[:side, :], side_in[side:, :])),
            one((side_out[:side, :], side_out[side:, :])),
            one(tails),
        ]
        second = [one((mid[top:count, :], mid[count + top :, :])), jnp.zeros_like(tails[0])]
        for pieces, to_ref, coded_parts in zip((first, second), block_refs[2 * other :], (4, 1)):
            for k in range(coded_parts):
                pieces[-1] = jnp.where(row == EXPONENT_ROW + k, exponent_of(pieces[k]), pieces[-1])
            at = 0
            for piece in pieces:
                to_ref[at : at + piece.shape[0], :] = piece
                at += piece.shape[0]


def spec_of(shape, dtype=jnp.float32):
    return jax.ShapeDtypeStruct(shape, dtype)


def closure_cost(passes):
    width = 640
    macs = TILE_CELLS * width * (2 * FEATURES + width) * passes
    return pl.CostEstimate(flops=2 * macs, transcendentals=2 * TILE_CELLS * width, bytes_accessed=8 * TILE_CELLS * width * passes)


def called(kernel, outs, info, args, scratch=(), name=None, fetches=False, passes=0):
    smem = pl.BlockSpec(memory_space=pltpu.SMEM)
    vmem = pl.BlockSpec(memory_space=pltpu.VMEM)
    in_specs = [smem] * len(info) + [pl.BlockSpec(memory_space=pltpu.HBM) if fetches else vmem] * len(args)
    return pl.pallas_call(
        kernel,
        out_shape=tuple(outs),
        in_specs=in_specs,
        out_specs=tuple(vmem for _ in outs),
        scratch_shapes=list(scratch),
        compiler_params=pltpu.CompilerParams(vmem_limit_bytes=VMEM_LIMIT),
        cost_estimate=closure_cost(passes) if passes else None,
        name=name,
    )(*info, *[pltpu.with_memory_space_constraint(arg, pltpu.HBM) if fetches else arg for arg in args])


def swapped(x, axis, even_bit, odd_bit):
    length = lax.axis_size(axis)
    return lax.ppermute(x, axis, [(i, i ^ (odd_bit if i & 1 else even_bit)) for i in range(length)])


def by_part(parts, exponents):
    if len(parts) == 1:
        return exponents[0:1]
    rows = sum(parts) + 8
    row = lax.broadcasted_iota(jnp.int32, (rows, exponents.shape[1]), 0)
    out = exponents[3:4]
    for k in (2, 1, 0):
        out = jnp.where(row < sum(parts[: k + 1]), exponents[k : k + 1], out)
    return out


def exponents_of(half):
    return half[half.shape[0] - 8 + EXPONENT_ROW :, :].astype(jnp.float32)


def with_exponents(half, exponents):
    rows, width = half.shape
    row = lax.broadcasted_iota(jnp.int32, (rows, width), 0)
    out = half
    for k in range(4):
        out = jnp.where(row == rows - 8 + EXPONENT_ROW + k, exponents[k : k + 1], out)
    return out.astype(jnp.float16)


def exact_power(exponent):
    count = jnp.clip(-exponent, 0.0, 31.0).astype(jnp.int32)
    out = jnp.ones(exponent.shape, jnp.float32)
    for bit in range(5):
        out = out * jnp.where((count >> bit) & 1 == 1, 2.0 ** -(1 << bit), 1.0)
    return out


def coded_sum(block, other, parts):
    exponents = jnp.maximum(exponents_of(block), exponents_of(other)) + 1.0
    factors = lax.optimization_barrier(jnp.exp2(-exponents))
    return with_exponents((block + other) * by_part(parts, factors), exponents)


def sum_of_coded(block, other, parts):
    mine, others = exponents_of(block), exponents_of(other)
    exponents = jnp.maximum(mine, others) + 1.0
    factors = lax.optimization_barrier((exact_power(mine - exponents), exact_power(others - exponents)))
    total = block.astype(jnp.float32) * by_part(parts, factors[0])
    total = total + other.astype(jnp.float32) * by_part(parts, factors[1])
    return with_exponents(total, exponents)


def summed_by_tile(kept, sent, all_parts, edges, exchanged, end, finish_first):
    tied = lax.optimization_barrier
    others = [swapped(block, "tile", 1, 1) for block in sent]
    first = coded_sum(kept[0], others[0], all_parts[0])
    second = coded_sum(kept[1], others[1], all_parts[1])
    later, edges = tied((second, edges))
    arrived = exchanged(edges)
    others = [swapped(block, "tile", 2, 4) for block in (first, second)]
    others[0], second = tied((others[0], later))
    first = sum_of_coded(first, others[0], all_parts[0])
    others[1], held, arrived = tied((others[1], first, arrived))
    second = sum_of_coded(second, others[1], all_parts[1])
    others = [swapped(block, "tile", 4, 2) for block in (first, second)]
    others[0], later, ended = tied((others[0], second, end(arrived)))
    first = sum_of_coded(held, others[0], all_parts[0])
    finished = finish_first(by_half(first, swapped(first, "tile", 1, 1)))
    second = sum_of_coded(later, others[1], all_parts[1])
    return ended, finished, by_half(second, swapped(second, "tile", 1, 1))


def by_half(own, other):
    first = lax.axis_index("tile") % HALVES == 0
    return jnp.where(first, jnp.stack([own, other]), jnp.stack([other, own]))


def body(initial_state, observed, edge_weight, land, w_in, b_in, w_mid, b_mid, w_out, b_out):
    tiles = lax.axis_size("tile")
    depths = lax.axis_size("depth")
    info = (jnp.stack([lax.axis_index("depth"), lax.axis_index("tile")]).astype(jnp.int32),)
    width = w_mid.shape[0]
    levels = LEVELS // depths
    rows = TRACERS * levels
    ways = pairings(tiles)

    def exchanged(edges):
        return tuple(lax.ppermute(edge, "tile", way) for edge, way in zip(edges, ways))

    def from_depths(own):
        return (own, *(swapped(own, "depth", k, k) for k in range(1, depths)))

    w_out_t = w_out.T
    field = spec_of((FEATURES, TILE_CELLS))
    half_field = spec_of((FEATURES, TILE_CELLS), jnp.bfloat16)
    own_field = spec_of((rows, TILE_CELLS))
    weight_rows = spec_of((8, TILE_CELLS))
    edge = spec_of((FEATURES, LANES))
    first_edge = spec_of((FEATURES + 8, LANES))
    own_edge = spec_of((rows, LANES))
    held = pltpu.VMEM((depths, rows, TILE_CELLS), jnp.float32)
    whole = pltpu.VMEM((FEATURES, TILE_CELLS), jnp.float32)
    cached = (
        spec_of((TILE_CELLS, width), jnp.bfloat16),
        spec_of((TILE_CELLS, width)),
        spec_of((TILE_CELLS, width), jnp.bfloat16),
        spec_of((TILE_CELLS, width)),
    )
    own_state = initial_state.reshape(rows, TILE_CELLS)
    target = observed.reshape(rows, TILE_CELLS)
    others = from_depths(own_state)[1:]
    prepared = called(
        prepare_kernel,
        (
            weight_rows,
            own_field,
            spec_of((1, width)),
            spec_of((1, width)),
            edge,
            spec_of(w_in.shape, w_in.dtype),
            spec_of(w_mid.shape, w_mid.dtype),
            spec_of(w_out_t.shape, w_out_t.dtype),
        ),
        (),
        (edge_weight.reshape(1, TILE_CELLS), land.reshape(1, TILE_CELLS), own_state, b_in, b_mid, b_out, w_in, w_mid, w_out_t),
        scratch=[
            pltpu.VMEM((1, TILE_CELLS), jnp.float32),
            pltpu.VMEM((1, TILE_CELLS), jnp.int32),
            pltpu.VMEM((width,), jnp.float32),
            pltpu.VMEM((width,), jnp.float32),
            pltpu.VMEM((FEATURES,), jnp.float32),
            pltpu.SemaphoreType.DMA((9,)),
        ],
        name="prepare",
        fetches=True,
    )
    prepared, target = lax.optimization_barrier((prepared, target))
    targets = from_depths(target)
    others, prepared = lax.optimization_barrier((others, prepared))
    weight, own_state, bias_in, bias_mid, bias_out, w_in, w_mid, w_out_t = prepared
    weights = (w_in, bias_in, w_mid, bias_mid, w_out_t, bias_out)

    def closure(state, outs):
        return called(forward_kernel, (field, *outs), (), (state, *weights), name="closure", passes=1)

    state_0, *edges = called(
        functools.partial(gather_kernel, depths),
        (field, first_edge, first_edge, first_edge),
        info,
        (weight, own_state, *others),
        scratch=[held],
        name="gather",
    )
    edges = exchanged(edges)
    q, *cache_0 = closure(state_0, cached)
    q, targets = lax.optimization_barrier((q, targets))
    state_1, weight_sums, *edges = called(
        first_step_kernel,
        (field, weight_rows, edge, edge, edge),
        info,
        (state_0, weight, q, *edges),
        name="step",
    )
    edges = exchanged(edges)
    q, *cache_1 = closure(state_1, cached)
    final_state, adjoint, upstream, *edges = called(
        functools.partial(last_step_kernel, depths),
        (own_field, field, half_field, edge, edge, edge),
        info,
        (state_1, weight, weight_sums, q, *edges, *targets),
        scratch=[held, whole],
        name="last_step",
    )
    edges = exchanged(edges)
    side = spec_of((FEATURES, width))
    row_sum = spec_of((8, width))
    back, *parts = called(
        first_backward_kernel,
        (field, spec_of((width, width)), side, side, row_sum, row_sum, row_sum),
        (),
        (state_1, upstream, *cache_1, w_in, w_mid, w_out_t),
        name="first_backward",
        passes=2,
    )
    adjoint, upstream, *edges = called(
        functools.partial(adjoint_kernel, depths),
        (own_field, half_field, own_edge, own_edge, own_edge),
        info,
        (adjoint, weight, weight_sums, back, *edges),
        scratch=[whole],
        name="adjoint",
    )
    all_parts = block_parts(width)
    blocks = [spec_of((sum(parts) + 8, width)) for parts in all_parts]
    back, *blocks = called(
        last_backward_kernel,
        (field, *blocks, *blocks),
        info,
        (state_0, upstream, *cache_0, w_in, w_mid, w_out_t, *parts),
        name="last_backward",
        passes=2,
    )
    kept, sent = blocks[:2], blocks[2:]
    scale = 1.0 / (tiles * TILE_CELLS)

    def end(arrived):
        (sensitivity,) = called(
            functools.partial(end_kernel, depths),
            (own_field,),
            info,
            (adjoint, weight, weight_sums, back, *arrived),
            scratch=[pltpu.VMEM((rows, TILE_CELLS), jnp.float32)],
            name="end",
        )
        return sensitivity

    def part(block, b, k, count=None):
        start = sum(all_parts[b][:k])
        count = all_parts[b][k] if count is None else count
        values = block[:, start : start + count, :]
        if values.dtype != jnp.float16:
            return values * scale
        at = sum(all_parts[b]) + EXPONENT_ROW + k
        exponent = block[:, at : at + 1, :].astype(jnp.float32)
        return values.astype(jnp.float32) * (jnp.exp2(exponent) * scale)

    def finish_first(block):
        grad_w_in = part(block, 0, 1).reshape(FEATURES, width)
        grad_w_out = part(block, 0, 2).reshape(FEATURES, width).T
        biases = part(block, 0, 3, 2)
        return grad_w_in, biases[0, 0], biases[1, 0], grad_w_out, biases[0, 1, :FEATURES], block

    if tiles == 8:
        sensitivity, finished, second = summed_by_tile(kept, sent, all_parts, tuple(edges), exchanged, end, finish_first)
    else:
        first, second = lax.psum([by_half(*args) for args in zip(kept, sent)], "tile")
        finished = finish_first(first)
        sensitivity = end(exchanged(edges))
    grad_w_in, grad_b_in, grad_b_mid, grad_w_out, grad_b_out, first = finished
    grad_w_mid = jnp.concatenate([part(first, 0, 0), part(second, 1, 0)], axis=1).reshape(width, width)
    shape = (TRACERS, levels, TILE_CELLS)
    return (
        final_state.reshape(shape),
        sensitivity.reshape(shape),
        grad_w_in,
        grad_b_in,
        grad_w_mid,
        grad_b_mid,
        grad_w_out,
        grad_b_out,
    )


def solution(mesh):
    return jax.shard_map(
        body,
        mesh=mesh,
        in_specs=(
            P(None, "depth", "tile"),
            P(None, "depth", "tile"),
            P("tile"),
            P("tile"),
            P(),
            P(),
            P(),
            P(),
            P(),
            P(),
        ),
        out_specs=(
            P(None, "depth", "tile"),
            P(None, "depth", "tile"),
            P(),
            P(),
            P(),
            P(),
            P(),
            P(),
        ),
        check_vma=False,
    )
```

```python
import functools

import jax
import jax.numpy as jnp
from jax import lax
from jax.experimental import pallas as pl
from jax.experimental.pallas import tpu as pltpu
from jax.sharding import PartitionSpec as P

TILE_SIDE = 32
LEVELS = 32
FEATURES = 64
TILE_CELLS = 1024
TRACERS = 2
LANES = 128
VMEM_LIMIT = 24 * 1024 * 1024

diffuse_coef = 0.2
step_size = 0.5


def pairings(tiles):
    fold = [(t, (t + tiles // 2) % tiles) for t in range(tiles)]
    inside = [(t, t ^ 1) for t in range(tiles)]
    outside = [(t, (t + 1 if t % 2 else t - 1) % tiles) for t in range(tiles)]
    return fold, inside, outside


def lane_of(shape):
    return lax.broadcasted_iota(jnp.int32, shape, 1)


def is_even_tile(info, shape):
    return (jnp.broadcast_to(info[1:2, : shape[1]], shape) & 1) == 0


def by_depth(depths, info, choices):
    shape = choices[0].shape
    depth = jnp.broadcast_to(info[0:1, : shape[1]], shape)
    out = choices[depths - 1]
    for d in range(depths - 1):
        out = jnp.where(depth == d, choices[d], out)
    return out


def edges_of(scaled, info):
    rows, whole = scaled.shape
    even_tile = is_even_tile(info, (rows, LANES))
    lane = lane_of((rows, LANES))
    across = jnp.where(lane < LANES // 2, scaled[:, :LANES], scaled[:, whole - LANES :])
    bit = 1
    while bit < TILE_SIDE:
        up = pltpu.roll(across, bit, 1)
        down = pltpu.roll(across, LANES - bit, 1)
        across = jnp.where((lane & bit) != 0, up, down)
        bit *= 2
    place = lane & (TILE_SIDE - 1)

    def squeezed(last):
        shift = LANES - (TILE_SIDE - 1) if last else 0
        out = None
        for k in range(whole // LANES):
            piece = scaled[:, k * LANES : (k + 1) * LANES]
            turn = (shift + k) % LANES
            piece = pltpu.roll(piece, turn, 1) if turn else piece
            out = piece if out is None else jnp.where(place == k, piece, out)
        return out

    west, east = squeezed(False), squeezed(True)
    return across, jnp.where(even_tile, east, west), jnp.where(even_tile, west, east)


def neighbour_sum(scaled, received, info):
    across, inside, outside = received
    even_tile = is_even_tile(info, inside.shape)
    whole = scaled.shape[1]
    count = whole // LANES
    lane = lane_of(scaled.shape)
    place = lane & (TILE_SIDE - 1)
    west = jnp.where(even_tile, outside, inside)
    east = jnp.where(even_tile, inside, outside)

    def spread(edge, shift):
        turns = [(shift - k) % LANES for k in range(count)]
        return jnp.concatenate([pltpu.roll(edge, turn, 1) if turn else edge for turn in turns], axis=1)

    everywhere = jnp.concatenate([across] * count, axis=1)
    west_cells = jnp.where(place == 0, spread(west, 0), pltpu.roll(scaled, 1, 1))
    east_cells = jnp.where(place == TILE_SIDE - 1, spread(east, TILE_SIDE - 1), pltpu.roll(scaled, whole - 1, 1))
    south_cells = jnp.where(lane < TILE_SIDE, everywhere, pltpu.roll(scaled, TILE_SIDE, 1))
    north_cells = jnp.where(lane >= whole - TILE_SIDE, everywhere, pltpu.roll(scaled, whole - TILE_SIDE, 1))
    return west_cells + east_cells + south_cells + north_cells


def diffused(field, weight, weight_sums, received, info):
    sums = neighbour_sum(field * weight, received, info)
    return weight * (sums - field * weight_sums)


def mask_of(weight):
    return jnp.where(weight > 0.0, 1.0, 0.0)


def in_order(depths, info, message_refs, out_ref):
    levels = LEVELS // depths
    for d in range(depths):
        values = by_depth(depths, info, [message_refs[own ^ d][...] for own in range(depths)])
        for tracer in range(TRACERS):
            to = tracer * LEVELS + d * levels
            out_ref[to : to + levels, :] = values[tracer * levels : (tracer + 1) * levels, :]


def own_levels(depths, info, from_ref, to_ref):
    levels = LEVELS // depths
    for tracer in range(TRACERS):
        starts = [tracer * LEVELS + d * levels for d in range(depths)]
        values = by_depth(depths, info, [from_ref[at : at + levels, :] for at in starts])
        to_ref[tracer * levels : (tracer + 1) * levels, :] = values


def prepare_kernel(*refs):
    edge_ref, land_ref, state_ref, b_in, b_mid, b_out, *weight_refs = refs[:9]
    weight_out, own_ref, in_ref, mid_ref, out_ref, *held_refs = refs[9:17]
    edge, land, bias_in, bias_mid, bias_out, sems = refs[17:]
    pairs = [
        (edge_ref, edge),
        (land_ref, land),
        (b_in, bias_in),
        (b_mid, bias_mid),
        (b_out, bias_out),
        (state_ref, own_ref),
        *zip(weight_refs, held_refs),
    ]
    copies = [pltpu.make_async_copy(source, to, sems.at[k]) for k, (source, to) in enumerate(pairs)]
    for copy in copies:
        copy.start()
    for copy in copies:
        copy.wait()
    weight = edge[...] * land[...].astype(jnp.float32)
    weight_out[...] = jnp.broadcast_to(weight, weight_out.shape)
    in_ref[...] = 0.5 * bias_in[...].reshape(in_ref.shape)
    mid_ref[...] = 0.5 * bias_mid[...].reshape(mid_ref.shape)
    for held_ref in held_refs[:2]:
        held_ref[...] = (0.5 * held_ref[...].astype(jnp.float32)).astype(jnp.bfloat16)
    rest = bias_out[...].reshape(1, FEATURES)
    terms = []
    for _ in range(3):
        term = rest.astype(jnp.bfloat16)
        terms.append(term)
        rest = rest - term.astype(jnp.float32)
    terms.append(jnp.zeros((5, FEATURES), jnp.bfloat16))
    out_ref[...] = contract(jnp.concatenate(terms, axis=0), jnp.ones((8, LANES), jnp.bfloat16), (0, 0))


def gather_kernel(depths, info, weight_ref, *refs):
    message_refs = refs[:depths]
    state_ref = refs[depths]
    edge_refs = refs[depths + 1 : depths + 4]
    in_order(depths, info, message_refs, state_ref)
    scaled = jnp.concatenate([state_ref[...] * weight_ref[0:1, :], weight_ref[...]], axis=0)
    for edge_out, edge in zip(edge_refs, edges_of(scaled, info)):
        edge_out[...] = edge


def contract(a, b, dims):
    return lax.dot_general(a, b, ((dims[:1], dims[1:]), ((), ())), preferred_element_type=jnp.float32)


def layer(y):
    a = 1.0 + jnp.tanh(y)
    hidden = y * a
    return hidden.astype(jnp.bfloat16), a * ((1.0 + (y + y)) - hidden)


def hidden_layers(state, w_in, b_in, w_mid, b_mid):
    inputs = state.astype(jnp.bfloat16)
    hidden_one, slope_one = layer(contract(inputs, w_in[...], (0, 0)) + b_in[...])
    hidden_two, slope_two = layer(contract(hidden_one, w_mid[...], (1, 0)) + b_mid[...])
    return hidden_one, slope_one, hidden_two, slope_two


def forward_kernel(state_ref, w_in, b_in, w_mid, b_mid, w_out_t, b_out, q_ref, *cache_refs):
    layers = hidden_layers(state_ref[...], w_in, b_in, w_mid, b_mid)
    bias = b_out[...]
    bias = jnp.concatenate([bias] * (q_ref.shape[1] // LANES), axis=1)
    q_ref[...] = contract(w_out_t[...], layers[2], (1, 1)) + bias
    for cache_ref, value in zip(cache_refs, layers):
        cache_ref[...] = value


def first_step_kernel(info, state_ref, weight_ref, q_ref, e0, e1, e2, next_ref, sums_ref, o0, o1, o2):
    weight = weight_ref[0:1, :]
    state = state_ref[...]
    received = (e0[...], e1[...], e2[...])
    scaled = jnp.concatenate([state * weight, weight_ref[...]], axis=0)
    sums = neighbour_sum(scaled, received, info)
    weight_sums = sums[FEATURES:, :]
    sums_ref[...] = weight_sums
    change = weight * (sums[:FEATURES, :] - state * weight_sums[0:1, :])
    state = state + diffuse_coef * change + step_size * mask_of(weight) * q_ref[...]
    next_ref[...] = state
    for edge_out, edge in zip((o0, o1, o2), edges_of(state * weight, info)):
        edge_out[...] = edge


def last_step_kernel(depths, info, state_ref, weight_ref, sums_ref, q_ref, e0, e1, e2, *refs):
    target_refs = refs[:depths]
    final_ref, adjoint_ref, upstream_ref, o0, o1, o2, ordered = refs[depths:]
    weight = weight_ref[0:1, :]
    mask = mask_of(weight)
    state = state_ref[...]
    received = (e0[...], e1[...], e2[...])
    change = diffused(state, weight, sums_ref[0:1, :], received, info)
    state = state + diffuse_coef * change + step_size * mask * q_ref[...]
    adjoint_ref[...] = state
    own_levels(depths, info, adjoint_ref, final_ref)
    in_order(depths, info, target_refs, ordered)
    adjoint = mask * (state - ordered[...])
    adjoint_ref[...] = adjoint
    upstream_ref[...] = (step_size * mask * adjoint).astype(jnp.bfloat16)
    for edge_out, edge in zip((o0, o1, o2), edges_of(adjoint * weight, info)):
        edge_out[...] = edge


def adjoint_kernel(depths, info, adjoint_ref, weight_ref, sums_ref, back_ref, e0, e1, e2, own_ref, upstream_ref, o0, o1, o2, held):
    weight = weight_ref[0:1, :]
    adjoint = adjoint_ref[...]
    received = (e0[...], e1[...], e2[...])
    adjoint = adjoint + diffuse_coef * diffused(adjoint, weight, sums_ref[0:1, :], received, info) + back_ref[...]
    upstream_ref[...] = (step_size * mask_of(weight) * adjoint).astype(jnp.bfloat16)
    held[...] = adjoint
    own_levels(depths, info, held, own_ref)
    for edge_out, edge in zip((o0, o1, o2), edges_of(own_ref[...] * weight, info)):
        edge_out[...] = edge


def end_kernel(depths, info, adjoint_ref, weight_ref, sums_ref, back_ref, e0, e1, e2, sensitivity_ref, own):
    weight = weight_ref[0:1, :]
    adjoint = adjoint_ref[...]
    received = (e0[...], e1[...], e2[...])
    own_levels(depths, info, back_ref, own)
    sensitivity_ref[...] = adjoint + diffuse_coef * diffused(adjoint, weight, sums_ref[0:1, :], received, info) + own[...]


HALVES = 2
EXPONENT_ROW = 4
TOP_EXPONENT = 14.0


def block_parts(width):
    side = FEATURES // HALVES
    second = (width // HALVES - 2 * side) // 2 // 16 * 16
    return (second, side, side), (width // HALVES - second,)


def exponent_of(part):
    largest = jnp.max(jnp.max(jnp.abs(part), axis=0, keepdims=True), axis=1, keepdims=True)
    exponent = jnp.ceil(jnp.log2(jnp.maximum(largest, 1e-37))) - TOP_EXPONENT
    return jnp.clip(exponent, -110.0, 110.0)


def gradient_parts(inputs, upstream, layers, w_in, w_mid, w_out_t):
    hidden_one, slope_one, hidden_two, slope_two = layers
    width = w_mid.shape[0]
    ones = jnp.ones((8, upstream.shape[1]), jnp.bfloat16)
    half = (0.5 * upstream.astype(jnp.float32)).astype(jnp.bfloat16)
    slope_two = (contract(half, w_out_t[...], (0, 0)) * slope_two).astype(jnp.bfloat16)
    slope_one = (contract(slope_two, w_mid[...], (1, 1)) * slope_one).astype(jnp.bfloat16)
    back = 2.0 * contract(w_in[...], slope_one, (1, 1))
    bias_out = contract(ones, upstream, (1, 1))
    return back, (
        contract(hidden_one, slope_two, (0, 0)),
        contract(inputs, slope_one, (1, 0)),
        contract(upstream, hidden_two, (1, 0)),
        contract(ones, slope_one, (1, 0)),
        contract(ones, slope_two, (1, 0)),
        jnp.concatenate([bias_out, jnp.zeros((8, width - FEATURES), jnp.float32)], axis=1),
    )


def first_backward_kernel(
    state_ref, upstream_ref, one_ref, slope_one_ref, two_ref, slope_two_ref, w_in, w_mid, w_out_t, back_ref, *part_refs
):
    layers = (one_ref[...], slope_one_ref[...], two_ref[...], slope_two_ref[...])
    inputs = state_ref[...].astype(jnp.bfloat16)
    back, parts = gradient_parts(inputs, upstream_ref[...], layers, w_in, w_mid, w_out_t)
    back_ref[...] = back
    for part_ref, part in zip(part_refs, parts):
        part_ref[...] = part


def last_backward_kernel(info, state_ref, upstream_ref, one_ref, slope_one_ref, two_ref, slope_two_ref, w_in, w_mid, w_out_t, *refs):
    earlier_refs = refs[:6]
    back_ref, *block_refs = refs[6:]
    layers = (one_ref[...], slope_one_ref[...], two_ref[...], slope_two_ref[...])
    inputs = state_ref[...].astype(jnp.bfloat16)
    back, parts = gradient_parts(inputs, upstream_ref[...], layers, w_in, w_mid, w_out_t)
    back_ref[...] = back
    mid, side_in, side_out, bias_in, bias_mid, bias_out = [part + ref[...] for part, ref in zip(parts, earlier_refs)]
    row = lax.broadcasted_iota(jnp.int32, bias_in.shape, 0)
    (top, side, _), _ = block_parts(w_mid.shape[0])
    count = mid.shape[0] // HALVES
    tails = (
        jnp.where(row == 0, bias_in, jnp.where(row == 1, bias_out, 0.0)),
        jnp.where(row == 0, bias_mid, 0.0),
    )
    for other in (False, True):

        def one(halves):
            return jnp.where(is_even_tile(info, halves[0].shape), halves[other], halves[not other])

        first = [
            one((mid[:top, :], mid[count : count + top, :])),
            one((side_in[:side, :], side_in[side:, :])),
            one((side_out[:side, :], side_out[side:, :])),
            one(tails),
        ]
        second = [one((mid[top:count, :], mid[count + top :, :])), jnp.zeros_like(tails[0])]
        for pieces, to_ref, coded_parts in zip((first, second), block_refs[2 * other :], (4, 1)):
            for k in range(coded_parts):
                pieces[-1] = jnp.where(row == EXPONENT_ROW + k, exponent_of(pieces[k]), pieces[-1])
            at = 0
            for piece in pieces:
                to_ref[at : at + piece.shape[0], :] = piece
                at += piece.shape[0]


def spec_of(shape, dtype=jnp.float32):
    return jax.ShapeDtypeStruct(shape, dtype)


def closure_cost(passes):
    width = 640
    macs = TILE_CELLS * width * (2 * FEATURES + width) * passes
    return pl.CostEstimate(flops=2 * macs, transcendentals=2 * TILE_CELLS * width, bytes_accessed=8 * TILE_CELLS * width * passes)


def called(kernel, outs, info, args, scratch=(), name=None, fetches=False, passes=0):
    vmem = pl.BlockSpec(memory_space=pltpu.VMEM)
    in_specs = [vmem] * len(info) + [pl.BlockSpec(memory_space=pltpu.HBM) if fetches else vmem] * len(args)
    return pl.pallas_call(
        kernel,
        out_shape=tuple(outs),
        in_specs=in_specs,
        out_specs=tuple(vmem for _ in outs),
        scratch_shapes=list(scratch),
        compiler_params=pltpu.CompilerParams(vmem_limit_bytes=VMEM_LIMIT),
        cost_estimate=closure_cost(passes) if passes else None,
        name=name,
    )(*info, *[pltpu.with_memory_space_constraint(arg, pltpu.HBM) if fetches else arg for arg in args])


def swapped(x, axis, even_bit, odd_bit):
    length = lax.axis_size(axis)
    return lax.ppermute(x, axis, [(i, i ^ (odd_bit if i & 1 else even_bit)) for i in range(length)])


def by_part(parts, exponents):
    if len(parts) == 1:
        return exponents[0:1]
    rows = sum(parts) + 8
    row = lax.broadcasted_iota(jnp.int32, (rows, exponents.shape[1]), 0)
    out = exponents[3:4]
    for k in (2, 1, 0):
        out = jnp.where(row < sum(parts[: k + 1]), exponents[k : k + 1], out)
    return out


def exponents_of(half):
    return half[half.shape[0] - 8 + EXPONENT_ROW :, :].astype(jnp.float32)


def with_exponents(half, exponents):
    rows, width = half.shape
    row = lax.broadcasted_iota(jnp.int32, (rows, width), 0)
    out = half
    for k in range(4):
        out = jnp.where(row == rows - 8 + EXPONENT_ROW + k, exponents[k : k + 1], out)
    return out.astype(jnp.float16)


def exact_power(exponent):
    count = jnp.clip(-exponent, 0.0, 31.0).astype(jnp.int32)
    out = jnp.ones(exponent.shape, jnp.float32)
    for bit in range(5):
        out = out * jnp.where((count >> bit) & 1 == 1, 2.0 ** -(1 << bit), 1.0)
    return out


def coded_sum(block, other, parts):
    exponents = jnp.maximum(exponents_of(block), exponents_of(other)) + 1.0
    factors = lax.optimization_barrier(jnp.exp2(-exponents))
    return with_exponents((block + other) * by_part(parts, factors), exponents)


def sum_of_coded(block, other, parts):
    mine, others = exponents_of(block), exponents_of(other)
    exponents = jnp.maximum(mine, others) + 1.0
    factors = lax.optimization_barrier((exact_power(mine - exponents), exact_power(others - exponents)))
    total = block.astype(jnp.float32) * by_part(parts, factors[0])
    total = total + other.astype(jnp.float32) * by_part(parts, factors[1])
    return with_exponents(total, exponents)


def summed_by_tile(kept, sent, all_parts, edges, exchanged, end, finish_first):
    tied = lax.optimization_barrier
    others = [swapped(block, "tile", 1, 1) for block in sent]
    first = coded_sum(kept[0], others[0], all_parts[0])
    others[1], held = tied((others[1], first))
    second = coded_sum(kept[1], others[1], all_parts[1])
    later, edges = tied((second, edges))
    arrived = exchanged(edges)
    others = [swapped(block, "tile", 2, 4) for block in (first, second)]
    others[0], second = tied((others[0], later))
    first = sum_of_coded(held, others[0], all_parts[0])
    others[1], held, arrived = tied((others[1], first, arrived))
    second = sum_of_coded(second, others[1], all_parts[1])
    others = [swapped(block, "tile", 4, 2) for block in (first, second)]
    others[0], later, ended = tied((others[0], second, end(arrived)))
    first = sum_of_coded(held, others[0], all_parts[0])
    finished = finish_first(by_half(first, swapped(first, "tile", 1, 1)))
    second = sum_of_coded(later, others[1], all_parts[1])
    return ended, finished, by_half(second, swapped(second, "tile", 1, 1))


def by_half(own, other):
    first = lax.axis_index("tile") % HALVES == 0
    return jnp.where(first, jnp.stack([own, other]), jnp.stack([other, own]))


def body(initial_state, observed, edge_weight, land, w_in, b_in, w_mid, b_mid, w_out, b_out):
    tiles = lax.axis_size("tile")
    depths = lax.axis_size("depth")
    row = lax.broadcasted_iota(jnp.int32, (8, TILE_CELLS), 0)
    info = (jnp.where(row == 0, lax.axis_index("depth"), lax.axis_index("tile")).astype(jnp.int32),)
    width = w_mid.shape[0]
    levels = LEVELS // depths
    rows = TRACERS * levels
    ways = pairings(tiles)

    def exchanged(edges):
        return tuple(lax.ppermute(edge, "tile", way) for edge, way in zip(edges, ways))

    def from_depths(own):
        return (own, *(swapped(own, "depth", k, k) for k in range(1, depths)))

    w_out_t = w_out.T
    field = spec_of((FEATURES, TILE_CELLS))
    half_field = spec_of((FEATURES, TILE_CELLS), jnp.bfloat16)
    own_field = spec_of((rows, TILE_CELLS))
    weight_rows = spec_of((8, TILE_CELLS))
    edge = spec_of((FEATURES, LANES))
    first_edge = spec_of((FEATURES + 8, LANES))
    own_edge = spec_of((rows, LANES))
    whole = pltpu.VMEM((FEATURES, TILE_CELLS), jnp.float32)
    cached = (
        spec_of((TILE_CELLS, width), jnp.bfloat16),
        spec_of((TILE_CELLS, width)),
        spec_of((TILE_CELLS, width), jnp.bfloat16),
        spec_of((TILE_CELLS, width)),
    )
    own_state = initial_state.reshape(rows, TILE_CELLS)
    target = observed.reshape(rows, TILE_CELLS)
    others = from_depths(own_state)[1:]
    prepared = called(
        prepare_kernel,
        (
            weight_rows,
            own_field,
            spec_of((1, width)),
            spec_of((1, width)),
            edge,
            spec_of(w_in.shape, w_in.dtype),
            spec_of(w_mid.shape, w_mid.dtype),
            spec_of(w_out_t.shape, w_out_t.dtype),
        ),
        (),
        (edge_weight.reshape(1, TILE_CELLS), land.reshape(1, TILE_CELLS), own_state, b_in, b_mid, b_out, w_in, w_mid, w_out_t),
        scratch=[
            pltpu.VMEM((1, TILE_CELLS), jnp.float32),
            pltpu.VMEM((1, TILE_CELLS), jnp.int32),
            pltpu.VMEM((width,), jnp.float32),
            pltpu.VMEM((width,), jnp.float32),
            pltpu.VMEM((FEATURES,), jnp.float32),
            pltpu.SemaphoreType.DMA((9,)),
        ],
        name="prepare",
        fetches=True,
    )
    prepared, target = lax.optimization_barrier((prepared, target))
    targets = from_depths(target)
    others, prepared = lax.optimization_barrier((others, prepared))
    weight, own_state, bias_in, bias_mid, bias_out, w_in, w_mid, w_out_t = prepared
    weights = (w_in, bias_in, w_mid, bias_mid, w_out_t, bias_out)

    def closure(state, outs):
        return called(forward_kernel, (field, *outs), (), (state, *weights), name="closure", passes=1)

    state_0, *edges = called(
        functools.partial(gather_kernel, depths),
        (field, first_edge, first_edge, first_edge),
        info,
        (weight, own_state, *others),
        name="gather",
    )
    edges = exchanged(edges)
    q, *cache_0 = closure(state_0, cached)
    q, targets = lax.optimization_barrier((q, targets))
    state_1, weight_sums, *edges = called(
        first_step_kernel,
        (field, weight_rows, edge, edge, edge),
        info,
        (state_0, weight, q, *edges),
        name="step",
    )
    edges = exchanged(edges)
    q, *cache_1 = closure(state_1, cached)
    final_state, adjoint, upstream, *edges = called(
        functools.partial(last_step_kernel, depths),
        (own_field, field, half_field, edge, edge, edge),
        info,
        (state_1, weight, weight_sums, q, *edges, *targets),
        scratch=[whole],
        name="last_step",
    )
    edges = exchanged(edges)
    side = spec_of((FEATURES, width))
    row_sum = spec_of((8, width))
    back, *parts = called(
        first_backward_kernel,
        (field, spec_of((width, width)), side, side, row_sum, row_sum, row_sum),
        (),
        (state_1, upstream, *cache_1, w_in, w_mid, w_out_t),
        name="first_backward",
        passes=2,
    )
    adjoint, upstream, *edges = called(
        functools.partial(adjoint_kernel, depths),
        (own_field, half_field, own_edge, own_edge, own_edge),
        info,
        (adjoint, weight, weight_sums, back, *edges),
        scratch=[whole],
        name="adjoint",
    )
    all_parts = block_parts(width)
    blocks = [spec_of((sum(parts) + 8, width)) for parts in all_parts]
    back, *blocks = called(
        last_backward_kernel,
        (field, *blocks, *blocks),
        info,
        (state_0, upstream, *cache_0, w_in, w_mid, w_out_t, *parts),
        name="last_backward",
        passes=2,
    )
    kept, sent = blocks[:2], blocks[2:]
    scale = 1.0 / (tiles * TILE_CELLS)

    def end(arrived):
        (sensitivity,) = called(
            functools.partial(end_kernel, depths),
            (own_field,),
            info,
            (adjoint, weight, weight_sums, back, *arrived),
            scratch=[pltpu.VMEM((rows, TILE_CELLS), jnp.float32)],
            name="end",
        )
        return sensitivity

    def part(block, b, k, count=None):
        start = sum(all_parts[b][:k])
        count = all_parts[b][k] if count is None else count
        values = block[:, start : start + count, :]
        if values.dtype != jnp.float16:
            return values * scale
        at = sum(all_parts[b]) + EXPONENT_ROW + k
        exponent = block[:, at : at + 1, :].astype(jnp.float32)
        return values.astype(jnp.float32) * (jnp.exp2(exponent) * scale)

    def finish_first(block):
        grad_w_in = part(block, 0, 1).reshape(FEATURES, width)
        grad_w_out = part(block, 0, 2).reshape(FEATURES, width).T
        biases = part(block, 0, 3, 2)
        return grad_w_in, biases[0, 0], biases[1, 0], grad_w_out, biases[0, 1, :FEATURES], block

    if tiles == 8:
        sensitivity, finished, second = summed_by_tile(kept, sent, all_parts, tuple(edges), exchanged, end, finish_first)
    else:
        first, second = lax.psum([by_half(*args) for args in zip(kept, sent)], "tile")
        finished = finish_first(first)
        sensitivity = end(exchanged(edges))
    grad_w_in, grad_b_in, grad_b_mid, grad_w_out, grad_b_out, first = finished
    grad_w_mid = jnp.concatenate([part(first, 0, 0), part(second, 1, 0)], axis=1).reshape(width, width)
    shape = (TRACERS, levels, TILE_CELLS)
    return (
        final_state.reshape(shape),
        sensitivity.reshape(shape),
        grad_w_in,
        grad_b_in,
        grad_w_mid,
        grad_b_mid,
        grad_w_out,
        grad_b_out,
    )


def solution(mesh):
    return jax.shard_map(
        body,
        mesh=mesh,
        in_specs=(
            P(None, "depth", "tile"),
            P(None, "depth", "tile"),
            P("tile"),
            P("tile"),
            P(),
            P(),
            P(),
            P(),
            P(),
            P(),
        ),
        out_specs=(
            P(None, "depth", "tile"),
            P(None, "depth", "tile"),
            P(),
            P(),
            P(),
            P(),
            P(),
            P(),
        ),
        check_vma=False,
    )
```

```python
import functools

import jax
import jax.numpy as jnp
from jax import lax
from jax.experimental import pallas as pl
from jax.experimental.pallas import tpu as pltpu
from jax.sharding import PartitionSpec as P

TILE_SIDE = 32
LEVELS = 32
FEATURES = 64
TILE_CELLS = 1024
TRACERS = 2
LANES = 128
VMEM_LIMIT = 24 * 1024 * 1024

diffuse_coef = 0.2
step_size = 0.5


def pairings(tiles):
    fold = [(t, (t + tiles // 2) % tiles) for t in range(tiles)]
    inside = [(t, t ^ 1) for t in range(tiles)]
    outside = [(t, (t + 1 if t % 2 else t - 1) % tiles) for t in range(tiles)]
    return fold, inside, outside


def lane_of(shape):
    return lax.broadcasted_iota(jnp.int32, shape, 1)


def is_even_tile(info, shape):
    return (jnp.broadcast_to(info[1:2, : shape[1]], shape) & 1) == 0


def by_depth(depths, info, choices):
    shape = choices[0].shape
    depth = jnp.broadcast_to(info[0:1, : shape[1]], shape)
    out = choices[depths - 1]
    for d in range(depths - 1):
        out = jnp.where(depth == d, choices[d], out)
    return out


def edges_of(scaled, info):
    rows, whole = scaled.shape
    even_tile = is_even_tile(info, (rows, LANES))
    lane = lane_of((rows, LANES))
    across = jnp.where(lane < LANES // 2, scaled[:, :LANES], scaled[:, whole - LANES :])
    bit = 1
    while bit < TILE_SIDE:
        up = pltpu.roll(across, bit, 1)
        down = pltpu.roll(across, LANES - bit, 1)
        across = jnp.where((lane & bit) != 0, up, down)
        bit *= 2
    place = lane & (TILE_SIDE - 1)

    def squeezed(last):
        shift = LANES - (TILE_SIDE - 1) if last else 0
        out = None
        for k in range(whole // LANES):
            piece = scaled[:, k * LANES : (k + 1) * LANES]
            turn = (shift + k) % LANES
            piece = pltpu.roll(piece, turn, 1) if turn else piece
            out = piece if out is None else jnp.where(place == k, piece, out)
        return out

    west, east = squeezed(False), squeezed(True)
    return across, jnp.where(even_tile, east, west), jnp.where(even_tile, west, east)


def neighbour_sum(scaled, received, info):
    across, inside, outside = received
    even_tile = is_even_tile(info, inside.shape)
    whole = scaled.shape[1]
    count = whole // LANES
    lane = lane_of(scaled.shape)
    place = lane & (TILE_SIDE - 1)
    west = jnp.where(even_tile, outside, inside)
    east = jnp.where(even_tile, inside, outside)

    def spread(edge, shift):
        turns = [(shift - k) % LANES for k in range(count)]
        return jnp.concatenate([pltpu.roll(edge, turn, 1) if turn else edge for turn in turns], axis=1)

    everywhere = jnp.concatenate([across] * count, axis=1)
    west_cells = jnp.where(place == 0, spread(west, 0), pltpu.roll(scaled, 1, 1))
    east_cells = jnp.where(place == TILE_SIDE - 1, spread(east, TILE_SIDE - 1), pltpu.roll(scaled, whole - 1, 1))
    south_cells = jnp.where(lane < TILE_SIDE, everywhere, pltpu.roll(scaled, TILE_SIDE, 1))
    north_cells = jnp.where(lane >= whole - TILE_SIDE, everywhere, pltpu.roll(scaled, whole - TILE_SIDE, 1))
    return west_cells + east_cells + south_cells + north_cells


def diffused(field, weight, weight_sums, received, info):
    sums = neighbour_sum(field * weight, received, info)
    return weight * (sums - field * weight_sums)


def mask_of(weight):
    return jnp.where(weight > 0.0, 1.0, 0.0)


def in_order(depths, info, message_refs, out_ref):
    levels = LEVELS // depths
    for d in range(depths):
        values = by_depth(depths, info, [message_refs[own ^ d][...] for own in range(depths)])
        for tracer in range(TRACERS):
            to = tracer * LEVELS + d * levels
            out_ref[to : to + levels, :] = values[tracer * levels : (tracer + 1) * levels, :]


def own_levels(depths, info, from_ref, to_ref):
    levels = LEVELS // depths
    for tracer in range(TRACERS):
        starts = [tracer * LEVELS + d * levels for d in range(depths)]
        values = by_depth(depths, info, [from_ref[at : at + levels, :] for at in starts])
        to_ref[tracer * levels : (tracer + 1) * levels, :] = values


def prepare_kernel(*refs):
    edge_ref, land_ref, state_ref, b_in, b_mid, b_out, *weight_refs = refs[:9]
    weight_out, own_ref, in_ref, mid_ref, out_ref, *held_refs = refs[9:17]
    edge, land, bias_in, bias_mid, bias_out, sems = refs[17:]
    pairs = [
        (edge_ref, edge),
        (land_ref, land),
        (b_in, bias_in),
        (b_mid, bias_mid),
        (b_out, bias_out),
        (state_ref, own_ref),
        *zip(weight_refs, held_refs),
    ]
    copies = [pltpu.make_async_copy(source, to, sems.at[k]) for k, (source, to) in enumerate(pairs)]
    for copy in copies:
        copy.start()
    for copy in copies:
        copy.wait()
    weight = edge[...] * land[...].astype(jnp.float32)
    weight_out[...] = jnp.broadcast_to(weight, weight_out.shape)
    in_ref[...] = 0.5 * bias_in[...].reshape(in_ref.shape)
    mid_ref[...] = 0.5 * bias_mid[...].reshape(mid_ref.shape)
    for held_ref in held_refs[:2]:
        held_ref[...] = (0.5 * held_ref[...].astype(jnp.float32)).astype(jnp.bfloat16)
    rest = bias_out[...].reshape(1, FEATURES)
    terms = []
    for _ in range(3):
        term = rest.astype(jnp.bfloat16)
        terms.append(term)
        rest = rest - term.astype(jnp.float32)
    terms.append(jnp.zeros((5, FEATURES), jnp.bfloat16))
    out_ref[...] = contract(jnp.concatenate(terms, axis=0), jnp.ones((8, LANES), jnp.bfloat16), (0, 0))


def gather_kernel(depths, info, weight_ref, *refs):
    message_refs = refs[:depths]
    state_ref = refs[depths]
    edge_refs = refs[depths + 1 : depths + 4]
    in_order(depths, info, message_refs, state_ref)
    scaled = jnp.concatenate([state_ref[...] * weight_ref[0:1, :], weight_ref[...]], axis=0)
    for edge_out, edge in zip(edge_refs, edges_of(scaled, info)):
        edge_out[...] = edge


def contract(a, b, dims):
    return lax.dot_general(a, b, ((dims[:1], dims[1:]), ((), ())), preferred_element_type=jnp.float32)


def layer(y):
    a = 1.0 + jnp.tanh(y)
    hidden = y * a
    return hidden.astype(jnp.bfloat16), a * ((1.0 + (y + y)) - hidden)


def hidden_layers(state, w_in, b_in, w_mid, b_mid):
    inputs = state.astype(jnp.bfloat16)
    hidden_one, slope_one = layer(contract(inputs, w_in[...], (0, 0)) + b_in[...])
    hidden_two, slope_two = layer(contract(hidden_one, w_mid[...], (1, 0)) + b_mid[...])
    return hidden_one, slope_one, hidden_two, slope_two


def forward_kernel(state_ref, w_in, b_in, w_mid, b_mid, w_out_t, b_out, q_ref, *cache_refs):
    layers = hidden_layers(state_ref[...], w_in, b_in, w_mid, b_mid)
    bias = b_out[...]
    bias = jnp.concatenate([bias] * (q_ref.shape[1] // LANES), axis=1)
    q_ref[...] = contract(w_out_t[...], layers[2], (1, 1)) + bias
    for cache_ref, value in zip(cache_refs, layers):
        cache_ref[...] = value


def first_step_kernel(info, state_ref, weight_ref, q_ref, e0, e1, e2, next_ref, sums_ref, o0, o1, o2):
    weight = weight_ref[0:1, :]
    state = state_ref[...]
    received = (e0[...], e1[...], e2[...])
    scaled = jnp.concatenate([state * weight, weight_ref[...]], axis=0)
    sums = neighbour_sum(scaled, received, info)
    weight_sums = sums[FEATURES:, :]
    sums_ref[...] = weight_sums
    change = weight * (sums[:FEATURES, :] - state * weight_sums[0:1, :])
    state = state + diffuse_coef * change + step_size * mask_of(weight) * q_ref[...]
    next_ref[...] = state
    for edge_out, edge in zip((o0, o1, o2), edges_of(state * weight, info)):
        edge_out[...] = edge


def last_step_kernel(depths, info, state_ref, weight_ref, sums_ref, q_ref, e0, e1, e2, *refs):
    target_refs = refs[:depths]
    final_ref, adjoint_ref, upstream_ref, o0, o1, o2, ordered = refs[depths:]
    weight = weight_ref[0:1, :]
    mask = mask_of(weight)
    state = state_ref[...]
    received = (e0[...], e1[...], e2[...])
    change = diffused(state, weight, sums_ref[0:1, :], received, info)
    state = state + diffuse_coef * change + step_size * mask * q_ref[...]
    adjoint_ref[...] = state
    own_levels(depths, info, adjoint_ref, final_ref)
    in_order(depths, info, target_refs, ordered)
    adjoint = mask * (state - ordered[...])
    adjoint_ref[...] = adjoint
    upstream_ref[...] = (step_size * mask * adjoint).astype(jnp.bfloat16)
    for edge_out, edge in zip((o0, o1, o2), edges_of(adjoint * weight, info)):
        edge_out[...] = edge


def adjoint_kernel(depths, info, adjoint_ref, weight_ref, sums_ref, back_ref, e0, e1, e2, own_ref, upstream_ref, o0, o1, o2, held):
    weight = weight_ref[0:1, :]
    adjoint = adjoint_ref[...]
    received = (e0[...], e1[...], e2[...])
    adjoint = adjoint + diffuse_coef * diffused(adjoint, weight, sums_ref[0:1, :], received, info) + back_ref[...]
    upstream_ref[...] = (step_size * mask_of(weight) * adjoint).astype(jnp.bfloat16)
    held[...] = adjoint
    own_levels(depths, info, held, own_ref)
    for edge_out, edge in zip((o0, o1, o2), edges_of(own_ref[...] * weight, info)):
        edge_out[...] = edge


def end_kernel(depths, info, adjoint_ref, weight_ref, sums_ref, back_ref, e0, e1, e2, sensitivity_ref, own):
    weight = weight_ref[0:1, :]
    adjoint = adjoint_ref[...]
    received = (e0[...], e1[...], e2[...])
    own_levels(depths, info, back_ref, own)
    sensitivity_ref[...] = adjoint + diffuse_coef * diffused(adjoint, weight, sums_ref[0:1, :], received, info) + own[...]


HALVES = 2
EXPONENT_ROW = 4
TOP_EXPONENT = 14.0


def block_parts(width):
    side = FEATURES // HALVES
    second = (width // HALVES - 2 * side) // 2 // 16 * 16
    return (second, side, side), (width // HALVES - second,)


def exponent_of(part):
    largest = jnp.max(jnp.max(jnp.abs(part), axis=0, keepdims=True), axis=1, keepdims=True)
    exponent = jnp.ceil(jnp.log2(jnp.maximum(largest, 1e-37))) - TOP_EXPONENT
    return jnp.clip(exponent, -110.0, 110.0)


def gradient_parts(inputs, upstream, layers, w_in, w_mid, w_out_t):
    hidden_one, slope_one, hidden_two, slope_two = layers
    width = w_mid.shape[0]
    ones = jnp.ones((8, upstream.shape[1]), jnp.bfloat16)
    half = (0.5 * upstream.astype(jnp.float32)).astype(jnp.bfloat16)
    slope_two = (contract(half, w_out_t[...], (0, 0)) * slope_two).astype(jnp.bfloat16)
    slope_one = (contract(slope_two, w_mid[...], (1, 1)) * slope_one).astype(jnp.bfloat16)
    back = 2.0 * contract(w_in[...], slope_one, (1, 1))
    bias_out = contract(ones, upstream, (1, 1))
    return back, (
        contract(hidden_one, slope_two, (0, 0)),
        contract(inputs, slope_one, (1, 0)),
        contract(upstream, hidden_two, (1, 0)),
        contract(ones, slope_one, (1, 0)),
        contract(ones, slope_two, (1, 0)),
        jnp.concatenate([bias_out, jnp.zeros((8, width - FEATURES), jnp.float32)], axis=1),
    )


def first_backward_kernel(
    state_ref, upstream_ref, one_ref, slope_one_ref, two_ref, slope_two_ref, w_in, w_mid, w_out_t, back_ref, *part_refs
):
    layers = (one_ref[...], slope_one_ref[...], two_ref[...], slope_two_ref[...])
    inputs = state_ref[...].astype(jnp.bfloat16)
    back, parts = gradient_parts(inputs, upstream_ref[...], layers, w_in, w_mid, w_out_t)
    back_ref[...] = back
    for part_ref, part in zip(part_refs, parts):
        part_ref[...] = part


def last_backward_kernel(info, state_ref, upstream_ref, one_ref, slope_one_ref, two_ref, slope_two_ref, w_in, w_mid, w_out_t, *refs):
    earlier_refs = refs[:6]
    back_ref, *block_refs = refs[6:]
    layers = (one_ref[...], slope_one_ref[...], two_ref[...], slope_two_ref[...])
    inputs = state_ref[...].astype(jnp.bfloat16)
    back, parts = gradient_parts(inputs, upstream_ref[...], layers, w_in, w_mid, w_out_t)
    back_ref[...] = back
    mid, side_in, side_out, bias_in, bias_mid, bias_out = [part + ref[...] for part, ref in zip(parts, earlier_refs)]
    row = lax.broadcasted_iota(jnp.int32, bias_in.shape, 0)
    (top, side, _), _ = block_parts(w_mid.shape[0])
    count = mid.shape[0] // HALVES
    tails = (
        jnp.where(row == 0, bias_in, jnp.where(row == 1, bias_out, 0.0)),
        jnp.where(row == 0, bias_mid, 0.0),
    )
    for other in (False, True):

        def one(halves):
            return jnp.where(is_even_tile(info, halves[0].shape), halves[other], halves[not other])

        first = [
            one((mid[:top, :], mid[count : count + top, :])),
            one((side_in[:side, :], side_in[side:, :])),
            one((side_out[:side, :], side_out[side:, :])),
            one(tails),
        ]
        second = [one((mid[top:count, :], mid[count + top :, :])), jnp.zeros_like(tails[0])]
        for pieces, to_ref, coded_parts in zip((first, second), block_refs[2 * other :], (4, 1)):
            for k in range(coded_parts):
                pieces[-1] = jnp.where(row == EXPONENT_ROW + k, exponent_of(pieces[k]), pieces[-1])
            at = 0
            for piece in pieces:
                to_ref[at : at + piece.shape[0], :] = piece
                at += piece.shape[0]


def decoded(scale, info, half, own, other, start, rows, exponent_row):
    def rows_of(at, number):
        pair = (own[at : at + number, :], other[at : at + number, :])
        return jnp.where(is_even_tile(info, pair[0].shape), pair[half], pair[1 - half])

    return rows_of(start, rows) * (jnp.exp2(rows_of(exponent_row, 1)) * scale)


def first_finish_kernel(scale, info, own, other, mid_ref, in_ref, out_ref, b_in, b_mid, b_out, held, sems):
    width = own.shape[1]
    (top, side, _), _ = block_parts(width)
    at = top + 2 * side + EXPONENT_ROW
    copies = []
    for half in range(HALVES):
        part = functools.partial(decoded, scale, info, half, own, other)
        held[half] = part(0, top, at)
        copies.append(pltpu.make_async_copy(held.at[half], mid_ref.at[pl.ds(half * (width // HALVES), top)], sems.at[half]))
        copies[half].start()
        in_ref[half * side : (half + 1) * side, :] = part(top, side, at + 1)
        out_ref[half * side : (half + 1) * side, :] = part(top + side, side, at + 2)
        tail = part(top + 2 * side, 8, at + 3)
        if half == 0:
            b_in[...] = tail[0:1, :].reshape(b_in.shape)
            b_out[...] = tail[1:2, : b_out.shape[0]].reshape(b_out.shape)
        else:
            b_mid[...] = tail[0:1, :].reshape(b_mid.shape)
    for copy in copies:
        copy.wait()


def second_finish_kernel(scale, info, own, other, begun_ref, mid_ref, held, sems):
    width = own.shape[1]
    (top, _, _), (rest,) = block_parts(width)
    copies = []
    for half in range(HALVES):
        held[half] = decoded(scale, info, half, own, other, 0, rest, rest + EXPONENT_ROW)
        to = mid_ref.at[pl.ds(half * (width // HALVES) + top, rest)]
        copies.append(pltpu.make_async_copy(held.at[half], to, sems.at[half]))
        copies[half].start()
    for copy in copies:
        copy.wait()


def spec_of(shape, dtype=jnp.float32):
    return jax.ShapeDtypeStruct(shape, dtype)


def closure_cost(passes):
    width = 640
    macs = TILE_CELLS * width * (2 * FEATURES + width) * passes
    return pl.CostEstimate(flops=2 * macs, transcendentals=2 * TILE_CELLS * width, bytes_accessed=8 * TILE_CELLS * width * passes)


def called(kernel, outs, info, args, scratch=(), name=None, fetches=False, passes=0):
    vmem = pl.BlockSpec(memory_space=pltpu.VMEM)
    in_specs = [vmem] * len(info) + [pl.BlockSpec(memory_space=pltpu.HBM) if fetches else vmem] * len(args)
    return pl.pallas_call(
        kernel,
        out_shape=tuple(outs),
        in_specs=in_specs,
        out_specs=tuple(vmem for _ in outs),
        scratch_shapes=list(scratch),
        compiler_params=pltpu.CompilerParams(vmem_limit_bytes=VMEM_LIMIT),
        cost_estimate=closure_cost(passes) if passes else None,
        name=name,
    )(*info, *[pltpu.with_memory_space_constraint(arg, pltpu.HBM) if fetches else arg for arg in args])


def swapped(x, axis, even_bit, odd_bit):
    length = lax.axis_size(axis)
    return lax.ppermute(x, axis, [(i, i ^ (odd_bit if i & 1 else even_bit)) for i in range(length)])


def by_part(parts, exponents):
    if len(parts) == 1:
        return exponents[0:1]
    rows = sum(parts) + 8
    row = lax.broadcasted_iota(jnp.int32, (rows, exponents.shape[1]), 0)
    out = exponents[3:4]
    for k in (2, 1, 0):
        out = jnp.where(row < sum(parts[: k + 1]), exponents[k : k + 1], out)
    return out


def exponents_of(half):
    return half[half.shape[0] - 8 + EXPONENT_ROW :, :].astype(jnp.float32)


def with_exponents(half, exponents):
    rows, width = half.shape
    row = lax.broadcasted_iota(jnp.int32, (rows, width), 0)
    out = half
    for k in range(4):
        out = jnp.where(row == rows - 8 + EXPONENT_ROW + k, exponents[k : k + 1], out)
    return out.astype(jnp.float16)


def exact_power(exponent):
    count = jnp.clip(-exponent, 0.0, 31.0).astype(jnp.int32)
    out = jnp.ones(exponent.shape, jnp.float32)
    for bit in range(5):
        out = out * jnp.where((count >> bit) & 1 == 1, 2.0 ** -(1 << bit), 1.0)
    return out


def coded_sum(block, other, parts):
    exponents = jnp.maximum(exponents_of(block), exponents_of(other)) + 1.0
    factors = lax.optimization_barrier(jnp.exp2(-exponents))
    return with_exponents((block + other) * by_part(parts, factors), exponents)


def sum_of_coded(block, other, parts):
    mine, others = exponents_of(block), exponents_of(other)
    exponents = jnp.maximum(mine, others) + 1.0
    factors = lax.optimization_barrier((exact_power(mine - exponents), exact_power(others - exponents)))
    total = block.astype(jnp.float32) * by_part(parts, factors[0])
    total = total + other.astype(jnp.float32) * by_part(parts, factors[1])
    return with_exponents(total, exponents)


def summed_by_tile(kept, sent, all_parts, edges, exchanged, end):
    tied = lax.optimization_barrier
    others = [swapped(block, "tile", 1, 1) for block in sent]
    first = coded_sum(kept[0], others[0], all_parts[0])
    others[1], held = tied((others[1], first))
    second = coded_sum(kept[1], others[1], all_parts[1])
    later, edges = tied((second, edges))
    arrived = exchanged(edges)
    others = [swapped(block, "tile", 2, 4) for block in (first, second)]
    others[0], second = tied((others[0], later))
    first = sum_of_coded(held, others[0], all_parts[0])
    others[1], held, arrived = tied((others[1], first, arrived))
    second = sum_of_coded(second, others[1], all_parts[1])
    others = [swapped(block, "tile", 4, 2) for block in (first, second)]
    others[0], later, ended = tied((others[0], second, end(arrived)))
    first = sum_of_coded(held, others[0], all_parts[0])
    others[1], held = tied((others[1], first))
    second = sum_of_coded(later, others[1], all_parts[1])
    blocks = [held, swapped(first, "tile", 1, 1), second, swapped(second, "tile", 1, 1)]
    return ended, [block.astype(jnp.float32) for block in blocks]


def by_half(own, other):
    first = lax.axis_index("tile") % HALVES == 0
    return jnp.where(first, jnp.stack([own, other]), jnp.stack([other, own]))


def body(initial_state, observed, edge_weight, land, w_in, b_in, w_mid, b_mid, w_out, b_out):
    tiles = lax.axis_size("tile")
    depths = lax.axis_size("depth")
    row = lax.broadcasted_iota(jnp.int32, (8, TILE_CELLS), 0)
    info = (jnp.where(row == 0, lax.axis_index("depth"), lax.axis_index("tile")).astype(jnp.int32),)
    width = w_mid.shape[0]
    levels = LEVELS // depths
    rows = TRACERS * levels
    ways = pairings(tiles)

    def exchanged(edges):
        return tuple(lax.ppermute(edge, "tile", way) for edge, way in zip(edges, ways))

    def from_depths(own):
        return (own, *(swapped(own, "depth", k, k) for k in range(1, depths)))

    w_out_t = w_out.T
    field = spec_of((FEATURES, TILE_CELLS))
    half_field = spec_of((FEATURES, TILE_CELLS), jnp.bfloat16)
    own_field = spec_of((rows, TILE_CELLS))
    weight_rows = spec_of((8, TILE_CELLS))
    edge = spec_of((FEATURES, LANES))
    first_edge = spec_of((FEATURES + 8, LANES))
    own_edge = spec_of((rows, LANES))
    whole = pltpu.VMEM((FEATURES, TILE_CELLS), jnp.float32)
    cached = (
        spec_of((TILE_CELLS, width), jnp.bfloat16),
        spec_of((TILE_CELLS, width)),
        spec_of((TILE_CELLS, width), jnp.bfloat16),
        spec_of((TILE_CELLS, width)),
    )
    own_state = initial_state.reshape(rows, TILE_CELLS)
    target = observed.reshape(rows, TILE_CELLS)
    others = from_depths(own_state)[1:]
    prepared = called(
        prepare_kernel,
        (
            weight_rows,
            own_field,
            spec_of((1, width)),
            spec_of((1, width)),
            edge,
            spec_of(w_in.shape, w_in.dtype),
            spec_of(w_mid.shape, w_mid.dtype),
            spec_of(w_out_t.shape, w_out_t.dtype),
        ),
        (),
        (edge_weight.reshape(1, TILE_CELLS), land.reshape(1, TILE_CELLS), own_state, b_in, b_mid, b_out, w_in, w_mid, w_out_t),
        scratch=[
            pltpu.VMEM((1, TILE_CELLS), jnp.float32),
            pltpu.VMEM((1, TILE_CELLS), jnp.int32),
            pltpu.VMEM((width,), jnp.float32),
            pltpu.VMEM((width,), jnp.float32),
            pltpu.VMEM((FEATURES,), jnp.float32),
            pltpu.SemaphoreType.DMA((9,)),
        ],
        name="prepare",
        fetches=True,
    )
    prepared, target = lax.optimization_barrier((prepared, target))
    targets = from_depths(target)
    others, prepared = lax.optimization_barrier((others, prepared))
    weight, own_state, bias_in, bias_mid, bias_out, w_in, w_mid, w_out_t = prepared
    weights = (w_in, bias_in, w_mid, bias_mid, w_out_t, bias_out)

    def closure(state, outs):
        return called(forward_kernel, (field, *outs), (), (state, *weights), name="closure", passes=1)

    state_0, *edges = called(
        functools.partial(gather_kernel, depths),
        (field, first_edge, first_edge, first_edge),
        info,
        (weight, own_state, *others),
        name="gather",
    )
    edges = exchanged(edges)
    q, *cache_0 = closure(state_0, cached)
    q, targets = lax.optimization_barrier((q, targets))
    state_1, weight_sums, *edges = called(
        first_step_kernel,
        (field, weight_rows, edge, edge, edge),
        info,
        (state_0, weight, q, *edges),
        name="step",
    )
    edges = exchanged(edges)
    q, *cache_1 = closure(state_1, cached)
    final_state, adjoint, upstream, *edges = called(
        functools.partial(last_step_kernel, depths),
        (own_field, field, half_field, edge, edge, edge),
        info,
        (state_1, weight, weight_sums, q, *edges, *targets),
        scratch=[whole],
        name="last_step",
    )
    edges = exchanged(edges)
    side = spec_of((FEATURES, width))
    row_sum = spec_of((8, width))
    back, *parts = called(
        first_backward_kernel,
        (field, spec_of((width, width)), side, side, row_sum, row_sum, row_sum),
        (),
        (state_1, upstream, *cache_1, w_in, w_mid, w_out_t),
        name="first_backward",
        passes=2,
    )
    adjoint, upstream, *edges = called(
        functools.partial(adjoint_kernel, depths),
        (own_field, half_field, own_edge, own_edge, own_edge),
        info,
        (adjoint, weight, weight_sums, back, *edges),
        scratch=[whole],
        name="adjoint",
    )
    all_parts = block_parts(width)
    blocks = [spec_of((sum(parts) + 8, width)) for parts in all_parts]
    back, *blocks = called(
        last_backward_kernel,
        (field, *blocks, *blocks),
        info,
        (state_0, upstream, *cache_0, w_in, w_mid, w_out_t, *parts),
        name="last_backward",
        passes=2,
    )
    kept, sent = blocks[:2], blocks[2:]
    scale = 1.0 / (tiles * TILE_CELLS)

    def end(arrived):
        (sensitivity,) = called(
            functools.partial(end_kernel, depths),
            (own_field,),
            info,
            (adjoint, weight, weight_sums, back, *arrived),
            scratch=[pltpu.VMEM((rows, TILE_CELLS), jnp.float32)],
            name="end",
        )
        return sensitivity

    def part(block, b, k, count=None):
        start = sum(all_parts[b][:k])
        count = all_parts[b][k] if count is None else count
        return block[:, start : start + count, :] * scale

    if tiles == 8:
        sensitivity, blocks = summed_by_tile(kept, sent, all_parts, tuple(edges), exchanged, end)
        whole_mid = spec_of((width, width))
        vmem, hbm = (pl.BlockSpec(memory_space=space) for space in (pltpu.VMEM, pltpu.HBM))
        limit = pltpu.CompilerParams(vmem_limit_bytes=VMEM_LIMIT)
        begun, grad_w_in, grad_w_out, grad_b_in, grad_b_mid, grad_b_out = pl.pallas_call(
            functools.partial(first_finish_kernel, scale),
            out_shape=(whole_mid, side, side, spec_of((width,)), spec_of((width,)), spec_of((FEATURES,))),
            in_specs=[vmem, vmem, vmem],
            out_specs=(hbm, vmem, vmem, vmem, vmem, vmem),
            scratch_shapes=[pltpu.VMEM((HALVES, all_parts[0][0], width), jnp.float32), pltpu.SemaphoreType.DMA((HALVES,))],
            compiler_params=limit,
            name="first_finish",
        )(*info, *blocks[:2])
        (grad_w_mid,) = pl.pallas_call(
            functools.partial(second_finish_kernel, scale),
            out_shape=(whole_mid,),
            in_specs=[vmem, vmem, vmem, hbm],
            out_specs=(hbm,),
            scratch_shapes=[pltpu.VMEM((HALVES, all_parts[1][0], width), jnp.float32), pltpu.SemaphoreType.DMA((HALVES,))],
            input_output_aliases={3: 0},
            compiler_params=limit,
            name="second_finish",
        )(*info, *blocks[2:], begun)
        grad_w_out = grad_w_out.T
    else:
        first, second = lax.psum([by_half(*args) for args in zip(kept, sent)], "tile")
        sensitivity = end(exchanged(edges))
        grad_w_mid = jnp.concatenate([part(first, 0, 0), part(second, 1, 0)], axis=1).reshape(width, width)
        grad_w_in = part(first, 0, 1).reshape(FEATURES, width)
        grad_w_out = part(first, 0, 2).reshape(FEATURES, width).T
        biases = part(first, 0, 3, 2)
        grad_b_in, grad_b_mid, grad_b_out = biases[0, 0], biases[1, 0], biases[0, 1, :FEATURES]
    shape = (TRACERS, levels, TILE_CELLS)
    return (
        final_state.reshape(shape),
        sensitivity.reshape(shape),
        grad_w_in,
        grad_b_in,
        grad_w_mid,
        grad_b_mid,
        grad_w_out,
        grad_b_out,
    )


def solution(mesh):
    return jax.shard_map(
        body,
        mesh=mesh,
        in_specs=(
            P(None, "depth", "tile"),
            P(None, "depth", "tile"),
            P("tile"),
            P("tile"),
            P(),
            P(),
            P(),
            P(),
            P(),
            P(),
        ),
        out_specs=(
            P(None, "depth", "tile"),
            P(None, "depth", "tile"),
            P(),
            P(),
            P(),
            P(),
            P(),
            P(),
        ),
        check_vma=False,
    )
```

```python
import functools

import jax
import jax.numpy as jnp
from jax import lax
from jax.experimental import pallas as pl
from jax.experimental.pallas import tpu as pltpu
from jax.sharding import PartitionSpec as P

TILE_SIDE = 32
LEVELS = 32
FEATURES = 64
TILE_CELLS = 1024
TRACERS = 2
LANES = 128
VMEM_LIMIT = 24 * 1024 * 1024

diffuse_coef = 0.2
step_size = 0.5


def pairings(tiles):
    fold = [(t, (t + tiles // 2) % tiles) for t in range(tiles)]
    inside = [(t, t ^ 1) for t in range(tiles)]
    outside = [(t, (t + 1 if t % 2 else t - 1) % tiles) for t in range(tiles)]
    return fold, inside, outside


def lane_of(shape):
    return lax.broadcasted_iota(jnp.int32, shape, 1)


def is_even_tile(info, shape):
    return (jnp.broadcast_to(info[1:2, : shape[1]], shape) & 1) == 0


def by_depth(depths, info, choices):
    shape = choices[0].shape
    depth = jnp.broadcast_to(info[0:1, : shape[1]], shape)
    out = choices[depths - 1]
    for d in range(depths - 1):
        out = jnp.where(depth == d, choices[d], out)
    return out


def edges_of(scaled, info):
    rows, whole = scaled.shape
    even_tile = is_even_tile(info, (rows, LANES))
    lane = lane_of((rows, LANES))
    across = jnp.where(lane < LANES // 2, scaled[:, :LANES], scaled[:, whole - LANES :])
    bit = 1
    while bit < TILE_SIDE:
        up = pltpu.roll(across, bit, 1)
        down = pltpu.roll(across, LANES - bit, 1)
        across = jnp.where((lane & bit) != 0, up, down)
        bit *= 2
    place = lane & (TILE_SIDE - 1)

    def squeezed(last):
        shift = LANES - (TILE_SIDE - 1) if last else 0
        out = None
        for k in range(whole // LANES):
            piece = scaled[:, k * LANES : (k + 1) * LANES]
            turn = (shift + k) % LANES
            piece = pltpu.roll(piece, turn, 1) if turn else piece
            out = piece if out is None else jnp.where(place == k, piece, out)
        return out

    west, east = squeezed(False), squeezed(True)
    return across, jnp.where(even_tile, east, west), jnp.where(even_tile, west, east)


def neighbour_sum(scaled, received, info):
    across, inside, outside = received
    even_tile = is_even_tile(info, inside.shape)
    whole = scaled.shape[1]
    count = whole // LANES
    lane = lane_of(scaled.shape)
    place = lane & (TILE_SIDE - 1)
    west = jnp.where(even_tile, outside, inside)
    east = jnp.where(even_tile, inside, outside)

    def spread(edge, shift):
        turns = [(shift - k) % LANES for k in range(count)]
        return jnp.concatenate([pltpu.roll(edge, turn, 1) if turn else edge for turn in turns], axis=1)

    everywhere = jnp.concatenate([across] * count, axis=1)
    west_cells = jnp.where(place == 0, spread(west, 0), pltpu.roll(scaled, 1, 1))
    east_cells = jnp.where(place == TILE_SIDE - 1, spread(east, TILE_SIDE - 1), pltpu.roll(scaled, whole - 1, 1))
    south_cells = jnp.where(lane < TILE_SIDE, everywhere, pltpu.roll(scaled, TILE_SIDE, 1))
    north_cells = jnp.where(lane >= whole - TILE_SIDE, everywhere, pltpu.roll(scaled, whole - TILE_SIDE, 1))
    return west_cells + east_cells + south_cells + north_cells


def diffused(field, weight, weight_sums, received, info):
    sums = neighbour_sum(field * weight, received, info)
    return weight * (sums - field * weight_sums)


def mask_of(weight):
    return jnp.where(weight > 0.0, 1.0, 0.0)


def in_order(depths, info, message_refs, out_ref):
    levels = LEVELS // depths
    for d in range(depths):
        values = by_depth(depths, info, [message_refs[own ^ d][...] for own in range(depths)])
        for tracer in range(TRACERS):
            to = tracer * LEVELS + d * levels
            out_ref[to : to + levels, :] = values[tracer * levels : (tracer + 1) * levels, :]


def own_levels(depths, info, from_ref, to_ref):
    levels = LEVELS // depths
    for tracer in range(TRACERS):
        starts = [tracer * LEVELS + d * levels for d in range(depths)]
        values = by_depth(depths, info, [from_ref[at : at + levels, :] for at in starts])
        to_ref[tracer * levels : (tracer + 1) * levels, :] = values


def prepare_kernel(*refs):
    edge_ref, land_ref, state_ref, b_in, b_mid, b_out, *weight_refs = refs[:9]
    weight_out, own_ref, in_ref, mid_ref, out_ref, *held_refs = refs[9:17]
    edge, land, bias_in, bias_mid, bias_out, sems = refs[17:]
    pairs = [
        (edge_ref, edge),
        (land_ref, land),
        (b_in, bias_in),
        (b_mid, bias_mid),
        (b_out, bias_out),
        (state_ref, own_ref),
        *zip(weight_refs, held_refs),
    ]
    copies = [pltpu.make_async_copy(source, to, sems.at[k]) for k, (source, to) in enumerate(pairs)]
    for copy in copies:
        copy.start()
    for copy in copies:
        copy.wait()
    weight = edge[...] * land[...].astype(jnp.float32)
    weight_out[...] = jnp.broadcast_to(weight, weight_out.shape)
    in_ref[...] = 0.5 * bias_in[...].reshape(in_ref.shape)
    mid_ref[...] = 0.5 * bias_mid[...].reshape(mid_ref.shape)
    for held_ref in held_refs[:2]:
        held_ref[...] = (0.5 * held_ref[...].astype(jnp.float32)).astype(jnp.bfloat16)
    rest = bias_out[...].reshape(1, FEATURES)
    terms = []
    for _ in range(3):
        term = rest.astype(jnp.bfloat16)
        terms.append(term)
        rest = rest - term.astype(jnp.float32)
    terms.append(jnp.zeros((5, FEATURES), jnp.bfloat16))
    out_ref[...] = contract(jnp.concatenate(terms, axis=0), jnp.ones((8, LANES), jnp.bfloat16), (0, 0))


def gather_kernel(depths, info, weight_ref, *refs):
    message_refs = refs[:depths]
    state_ref = refs[depths]
    edge_refs = refs[depths + 1 : depths + 4]
    in_order(depths, info, message_refs, state_ref)
    scaled = jnp.concatenate([state_ref[...] * weight_ref[0:1, :], weight_ref[...]], axis=0)
    for edge_out, edge in zip(edge_refs, edges_of(scaled, info)):
        edge_out[...] = edge


def contract(a, b, dims):
    return lax.dot_general(a, b, ((dims[:1], dims[1:]), ((), ())), preferred_element_type=jnp.float32)


def layer(y):
    a = 1.0 + jnp.tanh(y)
    hidden = y * a
    return hidden.astype(jnp.bfloat16), a * ((1.0 + (y + y)) - hidden)


def hidden_layers(state, w_in, b_in, w_mid, b_mid):
    inputs = state.astype(jnp.bfloat16)
    hidden_one, slope_one = layer(contract(inputs, w_in[...], (0, 0)) + b_in[...])
    hidden_two, slope_two = layer(contract(hidden_one, w_mid[...], (1, 0)) + b_mid[...])
    return hidden_one, slope_one, hidden_two, slope_two


def forward_kernel(state_ref, w_in, b_in, w_mid, b_mid, w_out_t, b_out, q_ref, *cache_refs):
    layers = hidden_layers(state_ref[...], w_in, b_in, w_mid, b_mid)
    bias = b_out[...]
    bias = jnp.concatenate([bias] * (q_ref.shape[1] // LANES), axis=1)
    q_ref[...] = contract(w_out_t[...], layers[2], (1, 1)) + bias
    for cache_ref, value in zip(cache_refs, layers):
        cache_ref[...] = value


def first_step_kernel(info, state_ref, weight_ref, q_ref, e0, e1, e2, next_ref, sums_ref, o0, o1, o2):
    weight = weight_ref[0:1, :]
    state = state_ref[...]
    received = (e0[...], e1[...], e2[...])
    scaled = jnp.concatenate([state * weight, weight_ref[...]], axis=0)
    sums = neighbour_sum(scaled, received, info)
    weight_sums = sums[FEATURES:, :]
    sums_ref[...] = weight_sums
    change = weight * (sums[:FEATURES, :] - state * weight_sums[0:1, :])
    state = state + diffuse_coef * change + step_size * mask_of(weight) * q_ref[...]
    next_ref[...] = state
    for edge_out, edge in zip((o0, o1, o2), edges_of(state * weight, info)):
        edge_out[...] = edge


def last_step_kernel(depths, info, state_ref, weight_ref, sums_ref, q_ref, e0, e1, e2, *refs):
    target_refs = refs[:depths]
    final_ref, adjoint_ref, upstream_ref, o0, o1, o2, ordered = refs[depths:]
    weight = weight_ref[0:1, :]
    mask = mask_of(weight)
    state = state_ref[...]
    received = (e0[...], e1[...], e2[...])
    change = diffused(state, weight, sums_ref[0:1, :], received, info)
    state = state + diffuse_coef * change + step_size * mask * q_ref[...]
    adjoint_ref[...] = state
    own_levels(depths, info, adjoint_ref, final_ref)
    in_order(depths, info, target_refs, ordered)
    adjoint = mask * (state - ordered[...])
    adjoint_ref[...] = adjoint
    upstream_ref[...] = (step_size * mask * adjoint).astype(jnp.bfloat16)
    for edge_out, edge in zip((o0, o1, o2), edges_of(adjoint * weight, info)):
        edge_out[...] = edge


def adjoint_kernel(depths, info, adjoint_ref, weight_ref, sums_ref, back_ref, e0, e1, e2, own_ref, upstream_ref, o0, o1, o2, held):
    weight = weight_ref[0:1, :]
    adjoint = adjoint_ref[...]
    received = (e0[...], e1[...], e2[...])
    adjoint = adjoint + diffuse_coef * diffused(adjoint, weight, sums_ref[0:1, :], received, info) + back_ref[...]
    upstream_ref[...] = (step_size * mask_of(weight) * adjoint).astype(jnp.bfloat16)
    held[...] = adjoint
    own_levels(depths, info, held, own_ref)
    for edge_out, edge in zip((o0, o1, o2), edges_of(own_ref[...] * weight, info)):
        edge_out[...] = edge


def end_kernel(depths, info, adjoint_ref, weight_ref, sums_ref, back_ref, e0, e1, e2, sensitivity_ref, own):
    weight = weight_ref[0:1, :]
    adjoint = adjoint_ref[...]
    received = (e0[...], e1[...], e2[...])
    own_levels(depths, info, back_ref, own)
    sensitivity_ref[...] = adjoint + diffuse_coef * diffused(adjoint, weight, sums_ref[0:1, :], received, info) + own[...]


HALVES = 2
EXPONENT_ROW = 4
TOP_EXPONENT = 14.0


def block_parts(width):
    side = FEATURES // HALVES
    second = (width // HALVES - 2 * side) // 2 // 16 * 16
    return (second, side, side), (width // HALVES - second,)


def exponent_of(part):
    largest = jnp.max(jnp.max(jnp.abs(part), axis=0, keepdims=True), axis=1, keepdims=True)
    exponent = jnp.ceil(jnp.log2(jnp.maximum(largest, 1e-37))) - TOP_EXPONENT
    return jnp.clip(exponent, -110.0, 110.0)


def gradient_parts(inputs, upstream, layers, w_in, w_mid, w_out_t):
    hidden_one, slope_one, hidden_two, slope_two = layers
    width = w_mid.shape[0]
    ones = jnp.ones((8, upstream.shape[1]), jnp.bfloat16)
    half = (0.5 * upstream.astype(jnp.float32)).astype(jnp.bfloat16)
    slope_two = (contract(half, w_out_t[...], (0, 0)) * slope_two).astype(jnp.bfloat16)
    slope_one = (contract(slope_two, w_mid[...], (1, 1)) * slope_one).astype(jnp.bfloat16)
    back = 2.0 * contract(w_in[...], slope_one, (1, 1))
    bias_out = contract(ones, upstream, (1, 1))
    return back, (
        contract(hidden_one, slope_two, (0, 0)),
        contract(inputs, slope_one, (1, 0)),
        contract(upstream, hidden_two, (1, 0)),
        contract(ones, slope_one, (1, 0)),
        contract(ones, slope_two, (1, 0)),
        jnp.concatenate([bias_out, jnp.zeros((8, width - FEATURES), jnp.float32)], axis=1),
    )


def first_backward_kernel(
    state_ref, upstream_ref, one_ref, slope_one_ref, two_ref, slope_two_ref, w_in, w_mid, w_out_t, back_ref, *part_refs
):
    layers = (one_ref[...], slope_one_ref[...], two_ref[...], slope_two_ref[...])
    inputs = state_ref[...].astype(jnp.bfloat16)
    back, parts = gradient_parts(inputs, upstream_ref[...], layers, w_in, w_mid, w_out_t)
    back_ref[...] = back
    for part_ref, part in zip(part_refs, parts):
        part_ref[...] = part


def last_backward_kernel(info, state_ref, upstream_ref, one_ref, slope_one_ref, two_ref, slope_two_ref, w_in, w_mid, w_out_t, *refs):
    earlier_refs = refs[:6]
    back_ref, *block_refs = refs[6:]
    layers = (one_ref[...], slope_one_ref[...], two_ref[...], slope_two_ref[...])
    inputs = state_ref[...].astype(jnp.bfloat16)
    back, parts = gradient_parts(inputs, upstream_ref[...], layers, w_in, w_mid, w_out_t)
    back_ref[...] = back
    mid, side_in, side_out, bias_in, bias_mid, bias_out = [part + ref[...] for part, ref in zip(parts, earlier_refs)]
    row = lax.broadcasted_iota(jnp.int32, bias_in.shape, 0)
    (top, side, _), _ = block_parts(w_mid.shape[0])
    count = mid.shape[0] // HALVES
    tails = (
        jnp.where(row == 0, bias_in, jnp.where(row == 1, bias_out, 0.0)),
        jnp.where(row == 0, bias_mid, 0.0),
    )
    for other in (False, True):

        def one(halves):
            return jnp.where(is_even_tile(info, halves[0].shape), halves[other], halves[not other])

        first = [
            one((mid[:top, :], mid[count : count + top, :])),
            one((side_in[:side, :], side_in[side:, :])),
            one((side_out[:side, :], side_out[side:, :])),
            one(tails),
        ]
        second = [one((mid[top:count, :], mid[count + top :, :])), jnp.zeros_like(tails[0])]
        for pieces, to_ref, coded_parts in zip((first, second), block_refs[2 * other :], (4, 1)):
            for k in range(coded_parts):
                pieces[-1] = jnp.where(row == EXPONENT_ROW + k, exponent_of(pieces[k]), pieces[-1])
            at = 0
            for piece in pieces:
                to_ref[at : at + piece.shape[0], :] = piece
                at += piece.shape[0]


def decoded(scale, info, half, own, other, start, rows, exponent_row):
    def rows_of(at, number):
        pair = (own[at : at + number, :], other[at : at + number, :])
        return jnp.where(is_even_tile(info, pair[0].shape), pair[half], pair[1 - half])

    return rows_of(start, rows) * (jnp.exp2(rows_of(exponent_row, 1)) * scale)


def first_finish_kernel(scale, info, own, other, mid_ref, in_ref, out_ref, b_in, b_mid, b_out, held, sems):
    width = own.shape[1]
    (top, side, _), _ = block_parts(width)
    at = top + 2 * side + EXPONENT_ROW
    copies = []
    for half in range(HALVES):
        part = functools.partial(decoded, scale, info, half, own, other)
        held[half] = part(0, top, at)
        copies.append(pltpu.make_async_copy(held.at[half], mid_ref.at[pl.ds(half * (width // HALVES), top)], sems.at[half]))
        copies[half].start()
        in_ref[half * side : (half + 1) * side, :] = part(top, side, at + 1)
        out_ref[half * side : (half + 1) * side, :] = part(top + side, side, at + 2)
        tail = part(top + 2 * side, 8, at + 3)
        if half == 0:
            b_in[...] = tail[0:1, :].reshape(b_in.shape)
            b_out[...] = tail[1:2, : b_out.shape[0]].reshape(b_out.shape)
        else:
            b_mid[...] = tail[0:1, :].reshape(b_mid.shape)
    for copy in copies:
        copy.wait()


def second_finish_kernel(scale, info, own, other, begun_ref, mid_ref, held, sems):
    width = own.shape[1]
    (top, _, _), (rest,) = block_parts(width)
    copies = []
    for half in range(HALVES):
        held[half] = decoded(scale, info, half, own, other, 0, rest, rest + EXPONENT_ROW)
        to = mid_ref.at[pl.ds(half * (width // HALVES) + top, rest)]
        copies.append(pltpu.make_async_copy(held.at[half], to, sems.at[half]))
        copies[half].start()
    for copy in copies:
        copy.wait()


def spec_of(shape, dtype=jnp.float32):
    return jax.ShapeDtypeStruct(shape, dtype)


def adjoint_backward_kernel(depths, info, *refs):
    upstream, held = refs[-2:]
    adjoint_kernel(depths, info, *refs[:7], refs[21], upstream, *refs[22:25], held)
    last_backward_kernel(info, refs[7], upstream, *refs[8:21], *refs[25:-2])


def closure_cost(passes):
    width = 640
    macs = TILE_CELLS * width * (2 * FEATURES + width) * passes
    return pl.CostEstimate(flops=2 * macs, transcendentals=2 * TILE_CELLS * width, bytes_accessed=8 * TILE_CELLS * width * passes)


def called(kernel, outs, info, args, scratch=(), name=None, fetches=False, passes=0):
    vmem = pl.BlockSpec(memory_space=pltpu.VMEM)
    in_specs = [vmem] * len(info) + [pl.BlockSpec(memory_space=pltpu.HBM) if fetches else vmem] * len(args)
    return pl.pallas_call(
        kernel,
        out_shape=tuple(outs),
        in_specs=in_specs,
        out_specs=tuple(vmem for _ in outs),
        scratch_shapes=list(scratch),
        compiler_params=pltpu.CompilerParams(vmem_limit_bytes=VMEM_LIMIT),
        cost_estimate=closure_cost(passes) if passes else None,
        name=name,
    )(*info, *[pltpu.with_memory_space_constraint(arg, pltpu.HBM) if fetches else arg for arg in args])


def swapped(x, axis, even_bit, odd_bit):
    length = lax.axis_size(axis)
    return lax.ppermute(x, axis, [(i, i ^ (odd_bit if i & 1 else even_bit)) for i in range(length)])


def by_part(parts, exponents):
    if len(parts) == 1:
        return exponents[0:1]
    rows = sum(parts) + 8
    row = lax.broadcasted_iota(jnp.int32, (rows, exponents.shape[1]), 0)
    out = exponents[3:4]
    for k in (2, 1, 0):
        out = jnp.where(row < sum(parts[: k + 1]), exponents[k : k + 1], out)
    return out


def exponents_of(half):
    return half[half.shape[0] - 8 + EXPONENT_ROW :, :].astype(jnp.float32)


def with_exponents(half, exponents):
    rows, width = half.shape
    row = lax.broadcasted_iota(jnp.int32, (rows, width), 0)
    out = half
    for k in range(4):
        out = jnp.where(row == rows - 8 + EXPONENT_ROW + k, exponents[k : k + 1], out)
    return out.astype(jnp.float16)


def exact_power(exponent):
    count = jnp.clip(-exponent, 0.0, 31.0).astype(jnp.int32)
    out = jnp.ones(exponent.shape, jnp.float32)
    for bit in range(5):
        out = out * jnp.where((count >> bit) & 1 == 1, 2.0 ** -(1 << bit), 1.0)
    return out


def coded_sum(block, other, parts):
    exponents = jnp.maximum(exponents_of(block), exponents_of(other)) + 1.0
    factors = lax.optimization_barrier(jnp.exp2(-exponents))
    return with_exponents((block + other) * by_part(parts, factors), exponents)


def sum_of_coded(block, other, parts):
    mine, others = exponents_of(block), exponents_of(other)
    exponents = jnp.maximum(mine, others) + 1.0
    factors = lax.optimization_barrier((exact_power(mine - exponents), exact_power(others - exponents)))
    total = block.astype(jnp.float32) * by_part(parts, factors[0])
    total = total + other.astype(jnp.float32) * by_part(parts, factors[1])
    return with_exponents(total, exponents)


def summed_by_tile(kept, sent, all_parts, edges, exchanged, end):
    tied = lax.optimization_barrier
    others = [swapped(block, "tile", 1, 1) for block in sent]
    first = coded_sum(kept[0], others[0], all_parts[0])
    others[1], held = tied((others[1], first))
    second = coded_sum(kept[1], others[1], all_parts[1])
    later, edges = tied((second, edges))
    arrived = exchanged(edges)
    others = [swapped(block, "tile", 2, 4) for block in (first, second)]
    others[0], second = tied((others[0], later))
    first = sum_of_coded(held, others[0], all_parts[0])
    others[1], held, arrived = tied((others[1], first, arrived))
    second = sum_of_coded(second, others[1], all_parts[1])
    others = [swapped(block, "tile", 4, 2) for block in (first, second)]
    others[0], later, ended = tied((others[0], second, end(arrived)))
    first = sum_of_coded(held, others[0], all_parts[0])
    others[1], held = tied((others[1], first))
    second = sum_of_coded(later, others[1], all_parts[1])
    blocks = [held, swapped(first, "tile", 1, 1), second, swapped(second, "tile", 1, 1)]
    return ended, [block.astype(jnp.float32) for block in blocks]


def by_half(own, other):
    first = lax.axis_index("tile") % HALVES == 0
    return jnp.where(first, jnp.stack([own, other]), jnp.stack([other, own]))


def body(initial_state, observed, edge_weight, land, w_in, b_in, w_mid, b_mid, w_out, b_out):
    tiles = lax.axis_size("tile")
    depths = lax.axis_size("depth")
    row = lax.broadcasted_iota(jnp.int32, (8, TILE_CELLS), 0)
    info = (jnp.where(row == 0, lax.axis_index("depth"), lax.axis_index("tile")).astype(jnp.int32),)
    width = w_mid.shape[0]
    levels = LEVELS // depths
    rows = TRACERS * levels
    ways = pairings(tiles)

    def exchanged(edges):
        return tuple(lax.ppermute(edge, "tile", way) for edge, way in zip(edges, ways))

    def from_depths(own):
        return (own, *(swapped(own, "depth", k, k) for k in range(1, depths)))

    w_out_t = w_out.T
    field = spec_of((FEATURES, TILE_CELLS))
    half_field = spec_of((FEATURES, TILE_CELLS), jnp.bfloat16)
    own_field = spec_of((rows, TILE_CELLS))
    weight_rows = spec_of((8, TILE_CELLS))
    edge = spec_of((FEATURES, LANES))
    first_edge = spec_of((FEATURES + 8, LANES))
    own_edge = spec_of((rows, LANES))
    whole = pltpu.VMEM((FEATURES, TILE_CELLS), jnp.float32)
    cached = (
        spec_of((TILE_CELLS, width), jnp.bfloat16),
        spec_of((TILE_CELLS, width)),
        spec_of((TILE_CELLS, width), jnp.bfloat16),
        spec_of((TILE_CELLS, width)),
    )
    own_state = initial_state.reshape(rows, TILE_CELLS)
    target = observed.reshape(rows, TILE_CELLS)
    others = from_depths(own_state)[1:]
    prepared = called(
        prepare_kernel,
        (
            weight_rows,
            own_field,
            spec_of((1, width)),
            spec_of((1, width)),
            edge,
            spec_of(w_in.shape, w_in.dtype),
            spec_of(w_mid.shape, w_mid.dtype),
            spec_of(w_out_t.shape, w_out_t.dtype),
        ),
        (),
        (edge_weight.reshape(1, TILE_CELLS), land.reshape(1, TILE_CELLS), own_state, b_in, b_mid, b_out, w_in, w_mid, w_out_t),
        scratch=[
            pltpu.VMEM((1, TILE_CELLS), jnp.float32),
            pltpu.VMEM((1, TILE_CELLS), jnp.int32),
            pltpu.VMEM((width,), jnp.float32),
            pltpu.VMEM((width,), jnp.float32),
            pltpu.VMEM((FEATURES,), jnp.float32),
            pltpu.SemaphoreType.DMA((9,)),
        ],
        name="prepare",
        fetches=True,
    )
    prepared, target = lax.optimization_barrier((prepared, target))
    targets = from_depths(target)
    others, prepared = lax.optimization_barrier((others, prepared))
    weight, own_state, bias_in, bias_mid, bias_out, w_in, w_mid, w_out_t = prepared
    weights = (w_in, bias_in, w_mid, bias_mid, w_out_t, bias_out)

    def closure(state, outs):
        return called(forward_kernel, (field, *outs), (), (state, *weights), name="closure", passes=1)

    state_0, *edges = called(
        functools.partial(gather_kernel, depths),
        (field, first_edge, first_edge, first_edge),
        info,
        (weight, own_state, *others),
        name="gather",
    )
    edges = exchanged(edges)
    q, *cache_0 = closure(state_0, cached)
    q, targets = lax.optimization_barrier((q, targets))
    state_1, weight_sums, *edges = called(
        first_step_kernel,
        (field, weight_rows, edge, edge, edge),
        info,
        (state_0, weight, q, *edges),
        name="step",
    )
    edges = exchanged(edges)
    q, *cache_1 = closure(state_1, cached)
    final_state, adjoint, upstream, *edges = called(
        functools.partial(last_step_kernel, depths),
        (own_field, field, half_field, edge, edge, edge),
        info,
        (state_1, weight, weight_sums, q, *edges, *targets),
        scratch=[whole],
        name="last_step",
    )
    edges = exchanged(edges)
    side = spec_of((FEATURES, width))
    row_sum = spec_of((8, width))
    back, *parts = called(
        first_backward_kernel,
        (field, spec_of((width, width)), side, side, row_sum, row_sum, row_sum),
        (),
        (state_1, upstream, *cache_1, w_in, w_mid, w_out_t),
        name="first_backward",
        passes=2,
    )
    all_parts = block_parts(width)
    blocks = [spec_of((sum(parts) + 8, width)) for parts in all_parts]
    adjoint, *outs = called(
        functools.partial(adjoint_backward_kernel, depths),
        (own_field, own_edge, own_edge, own_edge, field, *blocks, *blocks),
        info,
        (adjoint, weight, weight_sums, back, *edges, state_0, *cache_0, w_in, w_mid, w_out_t, *parts),
        scratch=[pltpu.VMEM((FEATURES, TILE_CELLS), jnp.bfloat16), whole],
        name="adjoint_backward",
        passes=2,
    )
    edges, back, blocks = outs[:3], outs[3], outs[4:]
    kept, sent = blocks[:2], blocks[2:]
    scale = 1.0 / (tiles * TILE_CELLS)

    def end(arrived):
        (sensitivity,) = called(
            functools.partial(end_kernel, depths),
            (own_field,),
            info,
            (adjoint, weight, weight_sums, back, *arrived),
            scratch=[pltpu.VMEM((rows, TILE_CELLS), jnp.float32)],
            name="end",
        )
        return sensitivity

    def part(block, b, k, count=None):
        start = sum(all_parts[b][:k])
        count = all_parts[b][k] if count is None else count
        return block[:, start : start + count, :] * scale

    if tiles == 8:
        sensitivity, blocks = summed_by_tile(kept, sent, all_parts, tuple(edges), exchanged, end)
        whole_mid = spec_of((width, width))
        vmem, hbm = (pl.BlockSpec(memory_space=space) for space in (pltpu.VMEM, pltpu.HBM))
        limit = pltpu.CompilerParams(vmem_limit_bytes=VMEM_LIMIT)
        begun, grad_w_in, grad_w_out, grad_b_in, grad_b_mid, grad_b_out = pl.pallas_call(
            functools.partial(first_finish_kernel, scale),
            out_shape=(whole_mid, side, side, spec_of((width,)), spec_of((width,)), spec_of((FEATURES,))),
            in_specs=[vmem, vmem, vmem],
            out_specs=(hbm, vmem, vmem, vmem, vmem, vmem),
            scratch_shapes=[pltpu.VMEM((HALVES, all_parts[0][0], width), jnp.float32), pltpu.SemaphoreType.DMA((HALVES,))],
            compiler_params=limit,
            name="first_finish",
        )(*info, *blocks[:2])
        (grad_w_mid,) = pl.pallas_call(
            functools.partial(second_finish_kernel, scale),
            out_shape=(whole_mid,),
            in_specs=[vmem, vmem, vmem, hbm],
            out_specs=(hbm,),
            scratch_shapes=[pltpu.VMEM((HALVES, all_parts[1][0], width), jnp.float32), pltpu.SemaphoreType.DMA((HALVES,))],
            input_output_aliases={3: 0},
            compiler_params=limit,
            name="second_finish",
        )(*info, *blocks[2:], begun)
        grad_w_out = grad_w_out.T
    else:
        first, second = lax.psum([by_half(*args) for args in zip(kept, sent)], "tile")
        sensitivity = end(exchanged(edges))
        grad_w_mid = jnp.concatenate([part(first, 0, 0), part(second, 1, 0)], axis=1).reshape(width, width)
        grad_w_in = part(first, 0, 1).reshape(FEATURES, width)
        grad_w_out = part(first, 0, 2).reshape(FEATURES, width).T
        biases = part(first, 0, 3, 2)
        grad_b_in, grad_b_mid, grad_b_out = biases[0, 0], biases[1, 0], biases[0, 1, :FEATURES]
    shape = (TRACERS, levels, TILE_CELLS)
    return (
        final_state.reshape(shape),
        sensitivity.reshape(shape),
        grad_w_in,
        grad_b_in,
        grad_w_mid,
        grad_b_mid,
        grad_w_out,
        grad_b_out,
    )


def solution(mesh):
    return jax.shard_map(
        body,
        mesh=mesh,
        in_specs=(
            P(None, "depth", "tile"),
            P(None, "depth", "tile"),
            P("tile"),
            P("tile"),
            P(),
            P(),
            P(),
            P(),
            P(),
            P(),
        ),
        out_specs=(
            P(None, "depth", "tile"),
            P(None, "depth", "tile"),
            P(),
            P(),
            P(),
            P(),
            P(),
            P(),
        ),
        check_vma=False,
    )
```
